32 devices in a mesh: grp: 2 (over core), cell: 16 (over z, y, x).
Axes of the slice: x: 2, y: 2, z: 4, core: 2. Of those that a mesh axis runs over, the one named last changes fastest.
Arguments:
- path_delay: float32 [133120], P('cell'), may hold values from 0 to 64
- path_angle: float32 [133120], P('cell'), may hold values from -3.140625 to 3.140625
- path_gain: float32 [2, 133120], P(None, 'cell'), may hold values from -0.9 to 0.9
- slot_counts: int32 [4096], P('cell'), may hold values from 1 to 64, as said below
- slot_offsets: int32 [4096], P('cell'), may hold values from 0 to 8319, as said below
- ray_link: int32 [4096], P('cell'), may hold values from 0 to 4095, as said below
- nearby_sectors: int32 [8, 512], P(None, 'cell'), may hold values from 0 to 511, as said below
- serving_slot: int32 [512], P('cell'), may hold values from 0 to 7
- symbols: bfloat16 [512, 2, 128], P('cell'), may hold values from -4 to 4
Outputs:
- received: float32 [512, 2, 128], P('cell')
The draws below stay inside these ranges and needn't reach their ends.
Inputs may be any that keep to these rules, and one draw needn't show every extreme that they name: `slot_counts`: the counts of one device's 256 ray slots sum to 8320, and every device has a slot of 64 paths. The ray slots of one device hold at most 1040 paths of links of one owner, and exactly 1040 for some owner. Within one device, the ranges slot_offsets to slot_offsets + slot_counts - 1 of its 256 slots cover the device's 8320 paths once each. `ray_link`: every link appears in exactly one ray slot. The owner of link g is the device g // 256, which holds its user; within the ray slots of one device the owners never fall. The ray slots of one device hold at most 32 links of one owner, and exactly 32 of some owner; every owner has 256 links in all. `nearby_sectors`: entry serving_slot[u] of user u is its serving sector, one of the sectors of the device that holds the user; every other entry lies within 16 sector indices of the serving sector, and on every device some user has entries at distance exactly 16.
All inputs are finite; a program needn't handle non-finite values.
Results may differ from the reference program's by a relative error of at most 0.0027.
Values may be sent and summed in bfloat16 or wider, within the bound.
No kernel may reach another device: no remote copies, remote signals or barrier semaphores. Data moves between devices by JAX's collectives and lax.ppermute only.
A program may use at most 64 MiB of HBM per device.

```python
import math
import jax
import jax.numpy as jnp
from jax import lax

SECTOR_ANTENNAS = 64
FRAME_TONES = 128
PMAX = 64
NEARBY_COUNT = 8
CELL_SECTORS = 32
USR_DEV = 32
LINK_DEV = 256
PATH_DEV = 8320
REACH = 16
USERS = 512
SECTOR_TOTAL = 512
LINKS = 4096
PATHS = 133120
N_CELL = 16


def layout_parts(key):
    subkeys = jax.random.split(jax.random.fold_in(key, 5), 5)
    mean_load = LINK_DEV // N_CELL
    swing = jax.random.randint(subkeys[0], (N_CELL // 2,), 0, mean_load + 1)
    swing = swing.at[0].set(mean_load)
    pair_loads = jnp.stack([mean_load + swing, mean_load - swing], axis=1).reshape(N_CELL)
    pair_loads = jax.random.permutation(subkeys[1], pair_loads)
    sender_shift = jax.random.permutation(subkeys[2], N_CELL)
    owner_shift = jax.random.permutation(subkeys[3], N_CELL)
    load_table = pair_loads[(sender_shift[:, None] + owner_shift[None, :]) % N_CELL]
    owner_start = jnp.cumsum(load_table, axis=0) - load_table
    slot_end = jnp.cumsum(load_table, axis=1)
    slot_start = slot_end - load_table
    slot_grid = jnp.arange(LINK_DEV)
    owner_pick = jax.vmap(lambda ends_row: jnp.searchsorted(ends_row, slot_grid, side='right'))(slot_end)
    owner_pick = jnp.minimum(owner_pick, N_CELL - 1)
    within = slot_grid[None, :] - jnp.take_along_axis(slot_start, owner_pick, axis=1)
    slot_load = jnp.take_along_axis(load_table, owner_pick, axis=1)
    owner_pos = jnp.take_along_axis(owner_start, owner_pick, axis=1) + within
    owner_perm = jax.vmap(lambda one_key: jax.random.permutation(one_key, LINK_DEV))(jax.random.split(subkeys[4], N_CELL))
    link_ids = owner_pick * LINK_DEV + owner_perm[owner_pick, owner_pos]
    return (link_ids.reshape(LINKS).astype(jnp.int32), within, slot_load)


def last_single(storage_row, count_row):
    single = jnp.argmax((count_row == 1).astype(jnp.int32))
    where_single = jnp.argmax((storage_row == single).astype(jnp.int32))
    tail_slot = storage_row[LINK_DEV - 1]
    return storage_row.at[where_single].set(tail_slot).at[LINK_DEV - 1].set(single)


def spread_leftover(rank_row, left_row, value_row):
    target = jnp.where(left_row, rank_row, LINK_DEV)
    return jnp.zeros((LINK_DEV + 1,), value_row.dtype).at[target].set(value_row)


def path_plan(key):
    link_ids, within, slot_load = layout_parts(key)
    subkeys = jax.random.split(jax.random.fold_in(key, 7), 3)
    value = jax.random.randint(subkeys[0], (N_CELL, LINK_DEV), 1, PMAX + 1)
    value = value.at[:, 0].set(PMAX)
    leftover = (slot_load % 2 == 1) & (within == slot_load - 1)
    left_rank = jnp.cumsum(leftover.astype(jnp.int32), axis=1) - 1
    left_value = jax.vmap(spread_leftover)(left_rank, leftover, value)
    prev_left = jnp.take_along_axis(left_value, jnp.maximum(left_rank - 1, 0), axis=1)
    prev_value = jnp.concatenate([value[:, :1], value[:, :-1]], axis=1)
    paired = jnp.where(within % 2 == 0, value, PMAX + 1 - prev_value)
    odd_pair = jnp.where(left_rank % 2 == 0, value, PMAX + 1 - prev_left)
    counts = jnp.where(leftover, odd_pair, paired)
    storage = jax.vmap(lambda one_key: jax.random.permutation(one_key, LINK_DEV))(jax.random.split(subkeys[2], N_CELL))
    storage = jax.vmap(last_single)(storage, counts)
    stored_counts = jnp.take_along_axis(counts, storage, axis=1)
    stored_start = jnp.cumsum(stored_counts, axis=1) - stored_counts
    offsets = jax.vmap(lambda order_row, start_row: jnp.zeros((LINK_DEV,), start_row.dtype).at[order_row].set(start_row))(storage, stored_start)
    return (counts.reshape(LINKS).astype(jnp.int32), offsets.reshape(LINKS).astype(jnp.int32))


def sector_plan(key):
    subkeys = jax.random.split(jax.random.fold_in(key, 23), 4)
    user_index = jnp.arange(USERS)
    home_sector = user_index // USR_DEV * CELL_SECTORS + jax.random.randint(subkeys[0], (USERS,), 0, CELL_SECTORS)
    home_sector = jnp.where(user_index == 0, 0, home_sector)
    home_sector = jnp.where(user_index == USERS - 1, SECTOR_TOTAL - 1, home_sector)
    serve_slot = jax.random.randint(subkeys[1], (USERS,), 0, NEARBY_COUNT)
    distance = jax.random.randint(subkeys[2], (NEARBY_COUNT, USERS), 1, REACH + 1)
    distance = jnp.where((user_index % USR_DEV == 0)[None, :], REACH, distance)
    sign_pick = 2 * jax.random.randint(subkeys[3], (NEARBY_COUNT, USERS), 0, 2) - 1
    forward = home_sector[None, :] + sign_pick * distance
    inside = (forward >= 0) & (forward < SECTOR_TOTAL)
    chosen = jnp.where(inside, forward, home_sector[None, :] - sign_pick * distance)
    slot_grid = jnp.arange(NEARBY_COUNT)[:, None]
    nearby = jnp.where(slot_grid == serve_slot[None, :], home_sector[None, :], chosen)
    return (nearby.astype(jnp.int32), serve_slot.astype(jnp.int32))


def draw_ray_link(key, part):
    return layout_parts(key)[0]


def draw_slot_counts(key, part):
    return path_plan(key)[0]


def draw_slot_offsets(key, part):
    return path_plan(key)[1]


def draw_nearby_sectors(key, part):
    return sector_plan(key)[0]


def draw_serving_slot(key, part):
    return sector_plan(key)[1]


def shard_levels(stream_key, extent, cuts, least, high):
    def one(axis_at, blocks):
        heights = jax.random.uniform(jax.random.fold_in(jax.random.fold_in(stream_key, 6), axis_at), (blocks,), jnp.float32, least / len(cuts), high / len(cuts))
        return jnp.repeat(jnp.exp(heights), extent[axis_at] // blocks).reshape((-1,) + (1,) * (len(extent) - axis_at - 1))

    level = one(*cuts[0])
    for cut in cuts[1:]:
        level = level * one(*cut)
    return level


def normal_values(rng, dims, deviation, reach, cuts=(), kind=jnp.bfloat16):
    level = shard_levels(rng, dims, cuts, -0.22, 0.18) if cuts else 1.0
    values = jax.random.normal(rng, dims, jnp.float32) * deviation * level
    return jnp.minimum(jnp.maximum(values, -reach), reach).astype(kind)


def setup_inputs(seed: int = 0) -> dict:
    splits = jax.random.split(jax.random.key(seed), 10)
    path_delay = jnp.clip(64.0 * jax.random.uniform(splits[0], (PATHS,), jnp.float32) ** shard_levels(splits[0], (PATHS,), ((0, 16),), -0.2, 0.2), 0.0, 64.0)
    path_angle = jnp.clip(jax.random.uniform(splits[1], (PATHS,), jnp.float32, -3.140625, 3.140625), -3.140625, 3.140625)
    path_gain = normal_values(splits[2], (2, PATHS), 0.15, 0.9, ((1, 16),), jnp.float32)
    slot_counts = draw_slot_counts(jax.random.fold_in(splits[9], 71), 0)
    slot_offsets = draw_slot_offsets(jax.random.fold_in(splits[9], 71), 0)
    ray_link = draw_ray_link(jax.random.fold_in(splits[9], 71), 0)
    nearby_sectors = draw_nearby_sectors(jax.random.fold_in(splits[9], 71), 0)
    serving_slot = draw_serving_slot(jax.random.fold_in(splits[9], 71), 0)
    symbols = normal_values(splits[8], (USERS, 2, FRAME_TONES), 1.0, 4.0, ((0, 16),))
    return {"path_delay": path_delay, "path_angle": path_angle, "path_gain": path_gain, "slot_counts": slot_counts, "slot_offsets": slot_offsets, "ray_link": ray_link, "nearby_sectors": nearby_sectors, "serving_slot": serving_slot, "symbols": symbols}


EPSILON = 1e-06

def rounded(value):
    return lax.optimization_barrier(value.astype(jnp.bfloat16)).astype(jnp.float32)

def make_response(delay_rows, angle_rows, real_rows, imag_rows, antenna_array):
    tone_freq = (jnp.arange(FRAME_TONES, dtype=jnp.float32) - FRAME_TONES // 2) / FRAME_TONES
    delay_phase = 2 * math.pi * delay_rows[:, :, None] * tone_freq[None, None, :]
    delay_real = rounded(jnp.cos(delay_phase))
    delay_imag = rounded(-jnp.sin(delay_phase))
    steer_phase = math.pi * antenna_array[None, :, None] * jnp.sin(angle_rows)[:, None, :]
    steer_cos = jnp.cos(steer_phase)
    steer_sin = jnp.sin(steer_phase)
    spread_real = rounded(real_rows[:, None, :] * steer_cos + imag_rows[:, None, :] * steer_sin)
    spread_imag = rounded(imag_rows[:, None, :] * steer_cos - real_rows[:, None, :] * steer_sin)
    resp_real = jnp.einsum('bap,bpf->baf', spread_real, delay_real) - jnp.einsum('bap,bpf->baf', spread_imag, delay_imag)
    resp_imag = jnp.einsum('bap,bpf->baf', spread_real, delay_imag) + jnp.einsum('bap,bpf->baf', spread_imag, delay_real)
    return rounded(jnp.stack([resp_real, resp_imag], axis=1))

def link_tables(path_delay, path_angle, path_gain, slot_counts, slot_offsets, ray_link):
    slot_index = jnp.arange(LINKS, dtype=jnp.int32)
    source = jnp.zeros((LINKS,), jnp.int32).at[ray_link].set(slot_index)
    counts = slot_counts[source]
    first_path = source // LINK_DEV * PATH_DEV + slot_offsets[source]
    path_steps = jnp.arange(PMAX, dtype=jnp.int32)
    live_mask = path_steps[None, :] < counts[:, None]
    where_path = jnp.clip(first_path[:, None] + path_steps[None, :], 0, PATHS - 1)
    columns = (path_delay, path_angle, path_gain[0], path_gain[1])
    return jnp.stack([jnp.where(live_mask, column[where_path], 0.0) for column in columns])

def reference(path_delay, path_angle, path_gain, slot_counts, slot_offsets, ray_link, nearby_sectors, serving_slot, symbols):
    tables = link_tables(path_delay, path_angle, path_gain, slot_counts, slot_offsets, ray_link)
    antenna_array = jnp.arange(SECTOR_ANTENNAS, dtype=jnp.float32)

    def owner_emission(owner):
        user_ids = owner * USR_DEV + jnp.arange(USR_DEV, dtype=jnp.int32)
        slot_pick = serving_slot[user_ids]
        serve_links = user_ids * NEARBY_COUNT + slot_pick
        link_rows = tables[:, serve_links, :]
        response = make_response(link_rows[0], link_rows[1], link_rows[2], link_rows[3], antenna_array)
        symbol_rows = symbols[user_ids].astype(jnp.float32)
        contribution_real = response[:, 0] * symbol_rows[:, 0, None, :] + response[:, 1] * symbol_rows[:, 1, None, :]
        contribution_imag = response[:, 0] * symbol_rows[:, 1, None, :] - response[:, 1] * symbol_rows[:, 0, None, :]
        sector_ids = nearby_sectors[slot_pick, user_ids] - owner * CELL_SECTORS
        unscaled_signal = jax.ops.segment_sum(jnp.stack([contribution_real, contribution_imag], axis=1), sector_ids, num_segments=CELL_SECTORS)
        antenna_power = lax.optimization_barrier(jnp.mean(unscaled_signal[:, 0] * unscaled_signal[:, 0] + unscaled_signal[:, 1] * unscaled_signal[:, 1], axis=2))
        return (unscaled_signal / jnp.sqrt(antenna_power + EPSILON)[:, None, :, None]).astype(jnp.bfloat16)
    transmit_weights = lax.map(owner_emission, jnp.arange(N_CELL, dtype=jnp.int32)).reshape(SECTOR_TOTAL, 2, SECTOR_ANTENNAS, FRAME_TONES)

    def owner_received(owner):
        user_ids = owner * USR_DEV + jnp.arange(USR_DEV, dtype=jnp.int32)
        link_rows = lax.dynamic_slice_in_dim(tables, owner * LINK_DEV, LINK_DEV, axis=1)
        response = make_response(link_rows[0], link_rows[1], link_rows[2], link_rows[3], antenna_array)
        sector_ids = nearby_sectors[:, user_ids].T.reshape(LINK_DEV)
        remote = transmit_weights[sector_ids].astype(jnp.float32)
        recv_real = lax.optimization_barrier(jnp.sum(response[:, 0] * remote[:, 0] - response[:, 1] * remote[:, 1], axis=1))
        recv_imag = lax.optimization_barrier(jnp.sum(response[:, 0] * remote[:, 1] + response[:, 1] * remote[:, 0], axis=1))
        link_values = jnp.stack([recv_real, recv_imag], axis=1).reshape(USR_DEV, NEARBY_COUNT, 2, FRAME_TONES)
        return lax.optimization_barrier(jnp.sum(link_values, axis=1)) / math.sqrt(SECTOR_ANTENNAS)
    return lax.map(owner_received, jnp.arange(N_CELL, dtype=jnp.int32)).reshape(USERS, 2, FRAME_TONES)
```

```python
import functools
import math

import jax
import jax.numpy as jnp
from jax import lax
from jax.experimental import pallas as pl
from jax.experimental.pallas import tpu as pltpu
from jax.sharding import PartitionSpec as P

SECTOR_ANTENNAS = 64
FRAME_TONES = 128
PMAX = 64
NEARBY_COUNT = 8
CELL_SECTORS = 32
REACH = 16
EPSILON = 1e-06

LANES = 128
GROUP = 8
HALF = FRAME_TONES // 2
COARSE = HALF // GROUP

SIN_TERMS = tuple((-1.0) ** n / math.factorial(2 * n + 1) for n in range(6))
COS_TERMS = tuple((-1.0) ** n / math.factorial(2 * n) for n in range(8))


def polynomial(terms, square):
    total = terms[-1]
    for term in terms[-2::-1]:
        total = total * square + term
    return total


def quarter_cos_sin(x):
    square = x * x
    return polynomial(COS_TERMS, square), x * polynomial(SIN_TERMS, square)


def cos_sin_turns(turns):
    turns = turns - jnp.round(turns)
    c, s = quarter_cos_sin(math.pi * turns)
    return 1.0 - 2.0 * s * s, 2.0 * s * c


def times(x, y):
    return x[0] * y[0] - x[1] * y[1], x[0] * y[1] + x[1] * y[0]


def powers(base, count):
    found = {1: base}
    for n in range(2, count + 1):
        found[n] = times(found[n // 2], found[n - n // 2])
    return found


def lane_index(rows):
    return lax.broadcasted_iota(jnp.int32, (rows, LANES), 1)


def pack_kernel(link_ref, count_ref, offset_ref, x_ref, y_ref, out_ref, *, link_total, capacity, stride):
    lane = lane_index(1)
    within = lane % PMAX
    upper = lane >= PMAX
    out_ref[...] = jnp.zeros_like(out_ref)
    empty = jnp.full((1, LANES), -1.0, jnp.float32)
    for owner in range(out_ref.shape[0] // stride):
        out_ref[owner * stride + capacity : owner * stride + capacity + 1, :] = empty

    def step(slot, carry):
        last_owner, place, tags = carry
        link = link_ref[slot]
        owner = lax.div(link, link_total)
        fresh = owner != last_owner
        place = jnp.where(fresh, 0, place + 1)
        offset = offset_ref[slot]
        row = lax.div(offset, LANES)
        shift = lax.rem(offset, LANES)
        early = lane >= shift
        x = jnp.where(early, x_ref[pl.ds(row, 1), :], x_ref[pl.ds(row + 1, 1), :])
        y = jnp.where(early, y_ref[pl.ds(row, 1), :], y_ref[pl.ds(row + 1, 1), :])
        x = pltpu.roll(x, lax.rem(LANES - shift, LANES), 1)
        y = pltpu.roll(y, lax.rem(LANES + PMAX - shift, LANES), 1)
        both = jnp.where(upper, y, x)
        both = jnp.where(within < count_ref[slot], both, 0.0)
        base = owner * stride
        out_ref[pl.ds(base + place, 1), :] = both
        local = (link - owner * link_total).astype(jnp.float32)
        tags = jnp.where(fresh, -1.0, tags)
        tags = jnp.where(lane == place, local, tags)
        out_ref[pl.ds(base + capacity, 1), :] = tags
        return owner, place, tags

    lax.fori_loop(0, link_total, step, (jnp.int32(-1), jnp.int32(0), empty), unroll=8)


def take_rows(source_ref, first, count, worker_index, own_ref, other_ref, even, odd):
    swap = worker_index == 0
    for n in range(count):
        row = source_ref[first + n]
        own = own_ref[pl.ds(row, 1), :]
        other = other_ref[pl.ds(row, 1), :]
        target = even if n % 2 == 0 else odd
        target[0, n // 2 : n // 2 + 1, :] = jnp.where(swap, own, other)
        target[1, n // 2 : n // 2 + 1, :] = jnp.where(swap, other, own)


def make_tables(even, odd, pairs, first_antenna, tables):
    fine_re, fine_im, coarse_re, coarse_im, near_re, near_im, far_re, far_im = tables
    steps = far_re.shape[0] // pairs
    left = lane_index(GROUP) < PMAX
    for group in range(pairs // GROUP):
        rows = pl.ds(group * GROUP, GROUP)
        pieces = []
        for field in range(2):
            a, b = even[field, rows, :], odd[field, rows, :]
            pieces.append(jnp.where(left, a, pltpu.roll(b, PMAX, 1)))
            pieces.append(jnp.where(left, pltpu.roll(a, PMAX, 1), b))
        delay, sine, gain_re, gain_im = pieces

        def put(ref_re, ref_im, n, count, value):
            at = pl.ds(group * GROUP * count + n, GROUP, stride=count)
            ref_re[at, :] = value[0]
            ref_im[at, :] = value[1]

        c, s = quarter_cos_sin(delay * (math.pi / FRAME_TONES))
        half = (c, -s)
        whole = times(half, half)
        fine = {0: half}
        up = powers(whole, GROUP - 1)
        put(fine_re, fine_im, 0, GROUP, half)
        for n in range(1, GROUP):
            fine[n] = times(half, up[n])
            put(fine_re, fine_im, n, GROUP, fine[n])
        stride = times(fine[GROUP - 1], half)
        for n, value in powers(stride, COARSE - 1).items():
            put(coarse_re, coarse_im, n, COARSE, value)
        c, s = cos_sin_turns(sine * 0.5)
        near = powers((c, -s), GROUP)
        put(near_re, near_im, 0, GROUP, (jnp.ones_like(c), jnp.zeros_like(c)))
        for n in range(1, GROUP):
            put(near_re, near_im, n, GROUP, near[n])
        c, s = cos_sin_turns(sine * (0.5 * first_antenna))
        value = times(times((gain_re, gain_im), (half[0], -half[1])), (c, -s))
        put(far_re, far_im, 0, steps, value)
        for n in range(1, steps):
            value = times(value, near[GROUP])
            put(far_re, far_im, n, steps, value)


def pair_response(pair, tables, steps):
    fine_re, fine_im, coarse_re, coarse_im, near_re, near_im, far_re, far_im = tables
    at = pl.ds(pl.multiple_of(pair * GROUP, GROUP), GROUP)
    fine = (fine_re[at, :], fine_im[at, :])
    delay = [fine]
    for n in range(1, COARSE):
        row = pl.ds(pair * COARSE + n, 1)
        delay.append(times((coarse_re[row, :], coarse_im[row, :]), fine))
    delay_re = jnp.concatenate([v[0] for v in delay], axis=0).astype(jnp.bfloat16)
    delay_im = jnp.concatenate([v[1] for v in delay], axis=0).astype(jnp.bfloat16)
    tones = jnp.concatenate(
        [
            jnp.concatenate([delay_re, -delay_im], axis=1),
            jnp.concatenate([delay_re, delay_im], axis=1),
        ],
        axis=0,
    )
    near = (near_re[at, :], near_im[at, :])
    spread = []
    for n in range(steps):
        row = pl.ds(pair * steps + n, 1)
        spread.append(times((far_re[row, :], far_im[row, :]), near))
    spread_re = jnp.concatenate([v[0] for v in spread], axis=0).astype(jnp.bfloat16)
    spread_im = jnp.concatenate([v[1] for v in spread], axis=0).astype(jnp.bfloat16)
    lane = lane_index(1)
    blocks = []
    for keep in (lane < PMAX, lane >= PMAX):
        keep = jnp.where(keep, 1.0, 0.0).astype(jnp.bfloat16)
        re, im = spread_re * keep, spread_im * keep
        blocks.append(jnp.concatenate([re, im], axis=1))
        blocks.append(jnp.concatenate([im, -re], axis=1))
    mixing = jnp.concatenate(blocks, axis=0)
    return lax.dot_general(
        mixing, tones, (((1,), (1,)), ((), ())), preferred_element_type=jnp.float32
    )


def reorder(values, index):
    pieces = [
        jnp.take_along_axis(values[n : n + GROUP], index, axis=1)
        for n in range(0, values.shape[0], GROUP)
    ]
    return jnp.concatenate(pieces, axis=0)


def serve_kernel(
    scalar_ref, source_ref, sector_ref, own_ref, other_ref, symbol_ref, low_ref, high_ref,
    even, odd, raw, symbols, *tables, portion,
):
    users = source_ref.shape[0]
    steps = portion // GROUP
    worker_index = scalar_ref[0]
    take_rows(source_ref, 0, users, worker_index, own_ref, other_ref, even, odd)
    make_tables(even, odd, users // 2, (worker_index * portion).astype(jnp.float32), tables)
    lane = lane_index(GROUP)
    index = jnp.where(lane < HALF, lane + HALF, FRAME_TONES - 1 - lane)
    symbols[...] = reorder(symbol_ref[...].astype(jnp.float32), index)
    raw[...] = jnp.zeros_like(raw)

    def one_pair(pair, carry):
        response = pair_response(pair, tables, steps).astype(jnp.bfloat16).astype(jnp.float32)
        for n in range(2):
            user = pair * 2 + n
            sym_re = symbols[pl.ds(user * 2, 1), :]
            sym_im = symbols[pl.ds(user * 2 + 1, 1), :]
            re = response[2 * n * portion : (2 * n + 1) * portion]
            im = response[(2 * n + 1) * portion : (2 * n + 2) * portion]
            sector = sector_ref[user]
            raw[sector, :portion, :] += re * sym_re + im * sym_im
            raw[sector, portion:, :] += re * sym_im - im * sym_re
        return carry

    lax.fori_loop(0, users // 2, one_pair, 0, unroll=2)
    half = CELL_SECTORS // 2

    def finish(sector, out_ref, row):
        value = raw[sector]
        re, im = value[:portion], value[portion:]
        power = jnp.sum(re * re + im * im, axis=1, keepdims=True) * (1.0 / FRAME_TONES)
        scale = 1.0 / jnp.sqrt(power + EPSILON)
        out_ref[row, :portion, :] = (re * scale).astype(jnp.bfloat16)
        out_ref[row, portion:, :] = (im * scale).astype(jnp.bfloat16)

    def one_sector(row, carry):
        finish(row, low_ref, row)
        finish(row + half, high_ref, row)
        return carry

    lax.fori_loop(0, half, one_sector, 0, unroll=2)


def respond_kernel(scalar_ref, source_ref, own_ref, other_ref, out_ref, even, odd, *tables, portion):
    pairs = out_ref.shape[0]
    steps = portion // GROUP
    worker_index = scalar_ref[0]
    first = pl.program_id(0) * pairs * 2
    take_rows(source_ref, first, pairs * 2, worker_index, own_ref, other_ref, even, odd)
    make_tables(even, odd, pairs, (worker_index * portion).astype(jnp.float32), tables)

    def one_pair(pair, carry):
        out_ref[pair] = pair_response(pair, tables, steps).astype(jnp.bfloat16)
        return carry

    lax.fori_loop(0, pairs, one_pair, 0, unroll=4)


def receive_kernel(
    sector_ref, response_ref, before_ref, low_ref, high_ref, after_ref, out_ref, remote, *, portion
):
    @pl.when(pl.program_id(0) == 0)
    def _():
        place = 0
        for part in (before_ref, low_ref, high_ref, after_ref):
            for n in range(part.shape[0]):
                remote[place] = part[n].astype(jnp.float32)
                place += 1

    users = out_ref.shape[0] // 2
    first = pl.program_id(0) * users

    def one_user(user, carry):
        total_re = jnp.zeros((GROUP, LANES), jnp.float32)
        total_im = jnp.zeros((GROUP, LANES), jnp.float32)
        for k in range(NEARBY_COUNT):
            sector = sector_ref[k, first + user]
            pair = user * (NEARBY_COUNT // 2) + k // 2
            base = (k % 2) * 2 * portion
            value = response_ref[pair, base : base + 2 * portion, :].astype(jnp.float32)
            other = remote[sector]
            for n in range(0, portion, GROUP):
                re, im = value[n : n + GROUP], value[portion + n : portion + n + GROUP]
                o_re, o_im = other[n : n + GROUP], other[portion + n : portion + n + GROUP]
                total_re = total_re + (re * o_re - im * o_im)
                total_im = total_im + (re * o_im + im * o_re)
        out_ref[pl.ds(user * 2, 1), :] = jnp.sum(total_re, axis=0, keepdims=True)
        out_ref[pl.ds(user * 2 + 1, 1), :] = jnp.sum(total_im, axis=0, keepdims=True)
        return carry

    lax.fori_loop(0, users, one_user, 0, unroll=2)
    lane = lane_index(GROUP)
    index = jnp.where(lane >= HALF, lane - HALF, FRAME_TONES - 1 - lane)
    out_ref[...] = reorder(out_ref[...], index)


VMEM = pl.BlockSpec(memory_space=pltpu.VMEM)
SMEM = pl.BlockSpec(memory_space=pltpu.SMEM)


def table_shapes(pairs, steps):
    return [pltpu.VMEM((pairs * n, LANES), jnp.float32) for n in (8, 8, 8, 8, 8, 8, steps, steps)]


def shards(
    path_delay,
    path_angle,
    path_gain,
    slot_counts,
    slot_offsets,
    ray_link,
    nearby_sectors,
    serving_slot,
    symbols,
):
    devices = lax.axis_size("cell")
    here = lax.axis_index("cell")
    worker_count = lax.axis_size("grp")
    worker_index = lax.axis_index("grp")
    path_total = path_delay.shape[0]
    link_total = slot_counts.shape[0]
    total_users = serving_slot.shape[0]
    capacity = 2 * link_total // devices
    stride = pl.cdiv(capacity + 1, GROUP) * GROUP
    portion = SECTOR_ANTENNAS // worker_count
    steps = portion // GROUP
    scalar = worker_index.astype(jnp.int32).reshape(1)

    path_rows = pl.cdiv(pl.cdiv(path_total, LANES) + 1, GROUP) * GROUP
    lower = worker_index == 0

    def rows_of(values):
        return jnp.pad(values, (0, path_rows * LANES - path_total)).reshape(path_rows, LANES)

    x = rows_of(jnp.where(lower, path_delay, path_gain[0]))
    y = rows_of(jnp.where(lower, jnp.sin(path_angle), path_gain[1]))
    packed = pl.pallas_call(
        functools.partial(
            pack_kernel, link_total=link_total, capacity=capacity, stride=stride
        ),
        out_shape=jax.ShapeDtypeStruct((devices * stride, LANES), jnp.float32),
        in_specs=[SMEM, SMEM, SMEM, VMEM, VMEM],
        out_specs=VMEM,
    )(ray_link, slot_counts, slot_offsets, x, y)
    arrived = lax.all_to_all(
        packed.reshape(devices, stride, LANES), "cell", split_axis=0, concat_axis=0, tiled=True
    )
    other = lax.ppermute(arrived, "grp", [(n, worker_count - 1 - n) for n in range(worker_count)])
    tags = arrived[:, capacity, :capacity].astype(jnp.int32).reshape(devices * capacity)
    slot_rows = (
        jnp.arange(devices, dtype=jnp.int32)[:, None] * stride
        + jnp.arange(capacity, dtype=jnp.int32)[None, :]
    ).reshape(devices * capacity)

    def find(links):
        return jnp.sum(jnp.where(links[:, None] == tags[None, :], slot_rows[None, :], 0), axis=1)

    source = find(jnp.arange(link_total, dtype=jnp.int32))
    serve_source = find(
        jnp.arange(total_users, dtype=jnp.int32) * NEARBY_COUNT + serving_slot
    )
    chosen = jnp.arange(NEARBY_COUNT, dtype=jnp.int32)[:, None] == serving_slot[None, :]
    serve_sector = jnp.sum(jnp.where(chosen, nearby_sectors, 0), axis=0) - here * CELL_SECTORS
    nearby_local = nearby_sectors - here * CELL_SECTORS + REACH

    own_rows = arrived.reshape(devices * stride, LANES)
    other_rows = other.reshape(devices * stride, LANES)
    half = CELL_SECTORS // 2
    part = jax.ShapeDtypeStruct((half, 2 * portion, LANES), jnp.bfloat16)
    serve_pairs = total_users // 2
    low, high = pl.pallas_call(
        functools.partial(serve_kernel, portion=portion),
        out_shape=(part, part),
        in_specs=[SMEM, SMEM, SMEM, VMEM, VMEM, VMEM],
        out_specs=(VMEM, VMEM),
        scratch_shapes=[
            pltpu.VMEM((2, serve_pairs, LANES), jnp.float32),
            pltpu.VMEM((2, serve_pairs, LANES), jnp.float32),
            pltpu.VMEM((CELL_SECTORS, 2 * portion, LANES), jnp.float32),
            pltpu.VMEM((2 * total_users, LANES), jnp.float32),
        ]
        + table_shapes(serve_pairs, steps),
    )(scalar, serve_source, serve_sector, own_rows, other_rows, symbols.reshape(2 * total_users, LANES))

    up = [(n, n + 1) for n in range(devices - 1)]
    down = [(m, n) for n, m in up]
    before = lax.ppermute(high, "cell", up)
    after = lax.ppermute(low, "cell", down)

    pair_total = link_total // 2
    block = 16
    response = pl.pallas_call(
        functools.partial(respond_kernel, portion=portion),
        out_shape=jax.ShapeDtypeStruct((pair_total, 4 * portion, LANES), jnp.bfloat16),
        grid=(pair_total // block,),
        in_specs=[SMEM, SMEM, VMEM, VMEM],
        out_specs=pl.BlockSpec((block, 4 * portion, LANES), lambda n: (n, 0, 0)),
        scratch_shapes=[
            pltpu.VMEM((2, block, LANES), jnp.float32),
            pltpu.VMEM((2, block, LANES), jnp.float32),
        ]
        + table_shapes(block, steps),
        cost_estimate=pl.CostEstimate(
            flops=pair_total * 2 * 128 * 128 * 256 * 40,
            bytes_accessed=pair_total * 4 * portion * LANES * 2,
            transcendentals=0,
        ),
    )(scalar, source, own_rows, other_rows)

    user_block = 8
    partial_value = pl.pallas_call(
        functools.partial(receive_kernel, portion=portion),
        out_shape=jax.ShapeDtypeStruct((2 * total_users, LANES), jnp.float32),
        grid=(total_users // user_block,),
        in_specs=[
            SMEM,
            pl.BlockSpec(
                (user_block * NEARBY_COUNT // 2, 4 * portion, LANES), lambda n: (n, 0, 0)
            ),
            VMEM,
            VMEM,
            VMEM,
            VMEM,
        ],
        out_specs=pl.BlockSpec((2 * user_block, LANES), lambda n: (n, 0)),
        scratch_shapes=[
            pltpu.VMEM((CELL_SECTORS + 2 * REACH, 2 * portion, LANES), jnp.float32)
        ],
    )(nearby_local, response, before, low, high, after)
    summed = partial_value + lax.ppermute(
        partial_value, "grp", [(n, worker_count - 1 - n) for n in range(worker_count)]
    )
    return (summed * (1.0 / math.sqrt(SECTOR_ANTENNAS))).reshape(total_users, 2, FRAME_TONES)


def solution(mesh):
    placed = (
        P("cell"),
        P("cell"),
        P(None, "cell"),
        P("cell"),
        P("cell"),
        P("cell"),
        P(None, "cell"),
        P("cell"),
        P("cell", None, None),
    )
    return jax.shard_map(
        shards, mesh=mesh, in_specs=placed, out_specs=P("cell", None, None), check_vma=False
    )
```

```python
import functools
import math

import jax
import jax.numpy as jnp
from jax import lax
from jax.experimental import pallas as pl
from jax.experimental.pallas import tpu as pltpu
from jax.sharding import PartitionSpec as P

SECTOR_ANTENNAS = 64
FRAME_TONES = 128
PMAX = 64
NEARBY_COUNT = 8
CELL_SECTORS = 32
REACH = 16
EPSILON = 1e-06

LANES = 128
GROUP = 8
HALF = FRAME_TONES // 2
COARSE = HALF // GROUP

SIN_TERMS = tuple((-1.0) ** n / math.factorial(2 * n + 1) for n in range(6))
COS_TERMS = tuple((-1.0) ** n / math.factorial(2 * n) for n in range(8))


def polynomial(terms, square):
    total = terms[-1]
    for term in terms[-2::-1]:
        total = total * square + term
    return total


def quarter_cos_sin(x):
    square = x * x
    return polynomial(COS_TERMS, square), x * polynomial(SIN_TERMS, square)


def cos_sin_turns(turns):
    turns = turns - jnp.round(turns)
    c, s = quarter_cos_sin(math.pi * turns)
    return 1.0 - 2.0 * s * s, 2.0 * s * c


def times(x, y):
    return x[0] * y[0] - x[1] * y[1], x[0] * y[1] + x[1] * y[0]


def powers(base, count):
    found = {1: base}
    for n in range(2, count + 1):
        found[n] = times(found[n // 2], found[n - n // 2])
    return found


def lane_index(rows):
    return lax.broadcasted_iota(jnp.int32, (rows, LANES), 1)


def pack_kernel(
    scalar_ref, link_ref, count_ref, offset_ref, delay_ref, angle_ref, gain_ref, out_ref, x_ref, y_ref,
    *, link_total, capacity, stride,
):
    rows = delay_ref.shape[0]
    lower = scalar_ref[0] == 0
    c, s = quarter_cos_sin(angle_ref[...] * 0.5)
    x_ref[:rows, :] = jnp.where(lower, delay_ref[...], gain_ref[:, 0, :])
    y = jnp.where(lower, 2.0 * s * c, gain_ref[:, 1, :])
    y = pltpu.roll(y, PMAX, 1)
    late = lane_index(1) >= PMAX
    y_ref[: rows + 1, :] = jnp.zeros((rows + 1, LANES), jnp.float32)
    pltpu.store(y_ref.at[:rows, :], y, mask=jnp.broadcast_to(late, y.shape))
    pltpu.store(y_ref.at[1 : rows + 1, :], y, mask=jnp.broadcast_to(~late, y.shape))
    lane = lane_index(1)
    within = lane & (PMAX - 1)
    out_ref[...] = jnp.zeros_like(out_ref)
    empty = jnp.full((1, LANES), -1.0, jnp.float32)
    for owner in range(out_ref.shape[0] // stride):
        out_ref[owner * stride + capacity : owner * stride + capacity + 1, :] = empty
    link_bits = link_total.bit_length() - 1

    def step(slot, carry):
        last_owner, place, tags = carry
        link = link_ref[slot]
        owner = link >> link_bits
        fresh = owner != last_owner
        place = jnp.where(fresh, 0, place + 1)
        offset = offset_ref[slot]
        row = offset >> 7
        shift = offset & (LANES - 1)
        early = lane >= shift
        first = ((lane - shift) & (LANES - 1)) < PMAX
        x = jnp.where(early, x_ref[pl.ds(row, 1), :], x_ref[pl.ds(row + 1, 1), :])
        y = jnp.where(early, y_ref[pl.ds(row, 1), :], y_ref[pl.ds(row + 1, 1), :])
        both = pltpu.roll(jnp.where(first, x, y), (LANES - shift) & (LANES - 1), 1)
        both = jnp.where(within < count_ref[slot], both, 0.0)
        base = owner * stride
        out_ref[pl.ds(base + place, 1), :] = both
        local = (link - (owner << link_bits)).astype(jnp.float32)
        tags = jnp.where(fresh, -1.0, tags)
        tags = jnp.where(lane == place, local, tags)
        out_ref[pl.ds(base + capacity, 1), :] = tags
        return owner, place, tags

    lax.fori_loop(0, link_total, step, (jnp.int32(-1), jnp.int32(0), empty), unroll=8)


def find_sources(own_ref, table_ref, source_ref, sem, capacity, stride):
    senders = own_ref.shape[0] // stride
    tags = own_ref[pl.ds(capacity, senders, stride=stride), :].T
    rows = table_ref.shape[0]
    depth = min(pl.cdiv(capacity, GROUP) * GROUP, LANES)
    tags = tags[:depth]
    place = lax.broadcasted_iota(jnp.int32, (depth, LANES), 0)
    inside = place < capacity
    place = place.astype(jnp.float32)
    lane = lane_index(depth).astype(jnp.float32)
    totals = [jnp.zeros((depth, LANES), jnp.float32) for _ in range(rows)]
    for sender in range(senders):
        column = jnp.where(inside, jnp.broadcast_to(tags[:, sender : sender + 1], (depth, LANES)), -1.0)
        value = place + float(sender * stride)
        for n in range(rows):
            totals[n] += jnp.where(column == lane + float(n * LANES), value, 0.0)
    for n in range(rows):
        table_ref[n : n + 1, :] = jnp.sum(totals[n], axis=0, keepdims=True).astype(jnp.int32)
    copy = pltpu.make_async_copy(table_ref, source_ref, sem)
    copy.start()
    copy.wait()


def take_row(row, n, lower, own_ref, other_ref, even, odd):
    own = own_ref[pl.ds(row, 1), :]
    other = other_ref[pl.ds(row, 1), :]
    target = even if n % 2 == 0 else odd
    target[0, n // 2 : n // 2 + 1, :] = jnp.where(lower, own, other)
    target[1, n // 2 : n // 2 + 1, :] = jnp.where(lower, other, own)


def make_tables(even, odd, pairs, first_antenna, tables):
    fine, centre, last, near, far = tables
    spans = centre.shape[1] // pairs
    steps = far.shape[1] // pairs
    left = lane_index(GROUP) < PMAX
    for group in range(pairs // GROUP):
        rows = pl.ds(group * GROUP, GROUP)
        pieces = []
        for field in range(2):
            a, b = even[field, rows, :], odd[field, rows, :]
            pieces.append(jnp.where(left, a, pltpu.roll(b, PMAX, 1)))
            pieces.append(jnp.where(left, pltpu.roll(a, PMAX, 1), b))
        delay, sine, gain_re, gain_im = pieces

        def put(ref, n, count, value):
            at = pl.ds(group * GROUP * count + n, GROUP, stride=count) if count > 1 else rows
            ref[0, at, :] = value[0]
            ref[1, at, :] = value[1]

        def half_steps(half):
            whole = times(half, half)
            up = powers(whole, GROUP - 1)
            found = [half] + [times(half, up[n]) for n in range(1, GROUP)]
            return whole, found

        c, s = quarter_cos_sin(delay * (math.pi / FRAME_TONES))
        whole, found = half_steps((c, -s))
        for n in range(GROUP):
            put(fine, n, GROUP, found[n])
        top = found[GROUP - 1]
        wide = times(times(top, top), whole)
        value = top
        for n in range(spans):
            if n:
                value = times(value, wide)
            put(centre, n, spans, value)
        put(last, 0, 1, times(value, times(top, whole)))

        c, s = cos_sin_turns(sine * 0.25)
        whole, found = half_steps((c, -s))
        for n in range(GROUP):
            put(near, n, GROUP, found[n])
        top = found[GROUP - 1]
        wide = times(times(top, top), whole)
        c, s = cos_sin_turns(sine * (0.5 * first_antenna))
        value = times(times((gain_re, gain_im), (c, -s)), top)
        for n in range(steps):
            if n:
                value = times(value, wide)
            put(far, n, steps, value)


def both_sides(centre, fine):
    a, b = centre[0] * fine[0], centre[1] * fine[1]
    c, d = centre[0] * fine[1], centre[1] * fine[0]
    return (a - b, c + d), (a + b, d - c)


def sides_of(centre_ref, fine_ref, pair, spans):
    at = pl.ds(pl.multiple_of(pair * GROUP, GROUP), GROUP)
    fine = (fine_ref[0, at, :], fine_ref[1, at, :])
    found = []
    for n in range(spans):
        row = pl.ds(pair * spans + n, 1)
        found.extend(both_sides((centre_ref[0, row, :], centre_ref[1, row, :]), fine))
    return found


def stack(values, part):
    return jnp.concatenate([v[part] for v in values], axis=0).astype(jnp.bfloat16)


def pair_response(pair, tables, pairs):
    fine, centre, last, near, far = tables
    delay = sides_of(centre, fine, pair, centre.shape[1] // pairs)
    delay_re, delay_im = stack(delay, 0), stack(delay, 1)
    row = pl.ds(pair, 1)
    final = lax.broadcasted_iota(jnp.int32, (GROUP, LANES), 0) == GROUP - 1
    swapped = tuple(jnp.where(final, last[n, row, :], delay[1][n]) for n in range(2))
    head = [delay[0], swapped]
    low_re = jnp.concatenate([stack(head, 0), delay_re[2 * GROUP :]], axis=0)
    low_im = jnp.concatenate([stack(head, 1), delay_im[2 * GROUP :]], axis=0)
    tones = jnp.concatenate(
        [
            jnp.concatenate([delay_re, -delay_im], axis=1),
            jnp.concatenate([low_re, low_im], axis=1),
        ],
        axis=0,
    )
    spread = sides_of(far, near, pair, far.shape[1] // pairs)
    spread_re, spread_im = stack(spread, 0), stack(spread, 1)
    lane = lane_index(1)
    blocks = []
    for keep in (lane < PMAX, lane >= PMAX):
        keep = jnp.where(keep, 1.0, 0.0).astype(jnp.bfloat16)
        re, im = spread_re * keep, spread_im * keep
        blocks.append(jnp.concatenate([re, im], axis=1))
        blocks.append(jnp.concatenate([im, -re], axis=1))
    mixing = jnp.concatenate(blocks, axis=0)
    return lax.dot_general(
        mixing, tones, (((1,), (1,)), ((), ())), preferred_element_type=jnp.float32
    )


def tone_of_place(lane):
    place = lane & (HALF - 1)
    within = place & 15
    above = (place & ~15) + jnp.where(within < GROUP, within + GROUP, 15 - within)
    below = jnp.where(above == 0, HALF, above)
    return HALF + jnp.where(lane < HALF, above, -below)


def place_of_tone(lane):
    away = jnp.where(lane >= HALF, lane - HALF, (HALF - lane) & (HALF - 1))
    within = away & 15
    place = (away & ~15) + jnp.where(within >= GROUP, within - GROUP, 15 - within)
    return jnp.where(lane >= HALF, place, HALF + place)


def reorder(values, index):
    pieces = [
        jnp.take_along_axis(values[n : n + GROUP], index, axis=1)
        for n in range(0, values.shape[0], GROUP)
    ]
    return jnp.concatenate(pieces, axis=0)


def serve_kernel(
    scalar_ref, nearby_ref, slot_ref, own_ref, other_ref, symbol_ref, low_ref, high_ref,
    table_ref, source_ref, sem, even, odd, raw, symbols, *tables, portion, capacity, stride,
):
    users = slot_ref.shape[0]
    worker_index = scalar_ref[0]
    find_sources(own_ref, table_ref, source_ref, sem, capacity, stride)
    for user in range(users):
        link = user * NEARBY_COUNT + slot_ref[user]
        row = source_ref[user * NEARBY_COUNT // LANES, link & (LANES - 1)]
        take_row(row, user, worker_index == 0, own_ref, other_ref, even, odd)
    pairs = users // 2
    make_tables(even, odd, pairs, (worker_index * portion).astype(jnp.float32), tables)
    symbols[...] = reorder(symbol_ref[...].astype(jnp.float32), tone_of_place(lane_index(GROUP)))
    raw[...] = jnp.zeros_like(raw)
    first_sector = scalar_ref[1] * CELL_SECTORS

    def one_pair(pair, carry):
        response = pair_response(pair, tables, pairs).astype(jnp.bfloat16).astype(jnp.float32)
        for n in range(2):
            user = pair * 2 + n
            sym_re = symbols[pl.ds(user * 2, 1), :]
            sym_im = symbols[pl.ds(user * 2 + 1, 1), :]
            re = response[2 * n * portion : (2 * n + 1) * portion]
            im = response[(2 * n + 1) * portion : (2 * n + 2) * portion]
            sector = nearby_ref[slot_ref[user], user] - first_sector
            raw[sector, :portion, :] += re * sym_re + im * sym_im
            raw[sector, portion:, :] += re * sym_im - im * sym_re
        return carry

    lax.fori_loop(0, pairs, one_pair, 0, unroll=4)
    half = CELL_SECTORS // 2

    def finish(sector, out_ref, row):
        value = raw[sector]
        re, im = value[:portion], value[portion:]
        power = jnp.sum(re * re + im * im, axis=1, keepdims=True) * (1.0 / FRAME_TONES)
        scale = 1.0 / jnp.sqrt(power + EPSILON)
        out_ref[row, :portion, :] = (re * scale).astype(jnp.bfloat16)
        out_ref[row, portion:, :] = (im * scale).astype(jnp.bfloat16)

    def one_sector(row, carry):
        finish(row, low_ref, row)
        finish(row + half, high_ref, row)
        return carry

    lax.fori_loop(0, half, one_sector, 0, unroll=4)


def respond_kernel(
    scalar_ref, own_ref, other_ref, out_ref, table_ref, source_ref, sem, even, odd, *tables,
    portion, capacity, stride,
):
    pairs = out_ref.shape[0]
    worker_index = scalar_ref[0]

    @pl.when(pl.program_id(0) == 0)
    def _():
        find_sources(own_ref, table_ref, source_ref, sem, capacity, stride)

    first = pl.program_id(0) * pairs * 2
    for n in range(2 * pairs):
        link = first + n
        row = source_ref[link >> 7, link & (LANES - 1)]
        take_row(row, n, worker_index == 0, own_ref, other_ref, even, odd)
    make_tables(even, odd, pairs, (worker_index * portion).astype(jnp.float32), tables)

    def one_pair(pair, carry):
        out_ref[pair] = pair_response(pair, tables, pairs).astype(jnp.bfloat16)
        return carry

    lax.fori_loop(0, pairs, one_pair, 0, unroll=UNROLL)


def receive_kernel(
    scalar_ref, nearby_ref, response_ref, before_ref, low_ref, high_ref, after_ref, out_ref, remote,
    *, portion,
):
    @pl.when(pl.program_id(0) == 0)
    def _():
        place = 0
        for part in (before_ref, low_ref, high_ref, after_ref):
            for n in range(part.shape[0]):
                remote[place] = part[n].astype(jnp.float32)
                place += 1

    users = out_ref.shape[0] // 2
    first = pl.program_id(0) * users
    first_sector = scalar_ref[1] * CELL_SECTORS - REACH

    def one_user(user, carry):
        total_re = jnp.zeros((GROUP, LANES), jnp.float32)
        total_im = jnp.zeros((GROUP, LANES), jnp.float32)
        for k in range(NEARBY_COUNT):
            sector = nearby_ref[k, first + user] - first_sector
            pair = user * (NEARBY_COUNT // 2) + k // 2
            base = (k % 2) * 2 * portion
            value = response_ref[pair, base : base + 2 * portion, :].astype(jnp.float32)
            other = remote[sector]
            for n in range(0, portion, GROUP):
                re, im = value[n : n + GROUP], value[portion + n : portion + n + GROUP]
                o_re, o_im = other[n : n + GROUP], other[portion + n : portion + n + GROUP]
                total_re = total_re + (re * o_re - im * o_im)
                total_im = total_im + (re * o_im + im * o_re)
        scale = 1.0 / math.sqrt(SECTOR_ANTENNAS)
        out_ref[pl.ds(user * 2, 1), :] = jnp.sum(total_re, axis=0, keepdims=True) * scale
        out_ref[pl.ds(user * 2 + 1, 1), :] = jnp.sum(total_im, axis=0, keepdims=True) * scale
        return carry

    lax.fori_loop(0, users, one_user, 0, unroll=2)
    out_ref[...] = reorder(out_ref[...], place_of_tone(lane_index(GROUP)))


UNROLL = 4
VMEM = pl.BlockSpec(memory_space=pltpu.VMEM)
SMEM = pl.BlockSpec(memory_space=pltpu.SMEM)


def table_shapes(pairs, steps):
    counts = (GROUP, COARSE // 2, 1, GROUP, steps // 2)
    return [pltpu.VMEM((2, pairs * n, LANES), jnp.float32) for n in counts]


def link_scratch(link_total, pairs):
    return [
        pltpu.VMEM((link_total // LANES, LANES), jnp.int32),
        pltpu.SMEM((link_total // LANES, LANES), jnp.int32),
        pltpu.SemaphoreType.DMA,
        pltpu.VMEM((2, pairs, LANES), jnp.float32),
        pltpu.VMEM((2, pairs, LANES), jnp.float32),
    ]


LIMIT = pltpu.CompilerParams(vmem_limit_bytes=16 << 20)


def shards(
    path_delay,
    path_angle,
    path_gain,
    slot_counts,
    slot_offsets,
    ray_link,
    nearby_sectors,
    serving_slot,
    symbols,
):
    devices = lax.axis_size("cell")
    worker_count = lax.axis_size("grp")
    path_total = path_delay.shape[0]
    link_total = slot_counts.shape[0]
    total_users = serving_slot.shape[0]
    capacity = 2 * link_total // devices
    stride = pl.cdiv(capacity + 1, GROUP) * GROUP
    portion = SECTOR_ANTENNAS // worker_count
    steps = portion // GROUP
    scalar = jnp.stack([lax.axis_index("grp"), lax.axis_index("cell")]).astype(jnp.int32)
    swap = [(n, worker_count - 1 - n) for n in range(worker_count)]

    path_rows = path_total // LANES
    work_rows = pl.cdiv(path_rows + 1, GROUP) * GROUP
    packed = pl.pallas_call(
        functools.partial(
            pack_kernel, link_total=link_total, capacity=capacity, stride=stride
        ),
        out_shape=jax.ShapeDtypeStruct((devices * stride, LANES), jnp.float32),
        in_specs=[SMEM, SMEM, SMEM, SMEM, VMEM, VMEM, VMEM],
        out_specs=VMEM,
        scratch_shapes=[pltpu.VMEM((work_rows, LANES), jnp.float32)] * 2,
        compiler_params=LIMIT,
    )(
        scalar,
        ray_link,
        slot_counts,
        slot_offsets,
        path_delay.reshape(path_rows, LANES),
        path_angle.reshape(path_rows, LANES),
        path_gain.reshape(2, path_rows, LANES).transpose(1, 0, 2),
    )
    arrived = lax.all_to_all(
        packed.reshape(devices, stride, LANES), "cell", split_axis=0, concat_axis=0, tiled=True
    )
    other = lax.ppermute(arrived, "grp", swap)
    own_rows = arrived.reshape(devices * stride, LANES)
    other_rows = other.reshape(devices * stride, LANES)
    sizes = dict(portion=portion, capacity=capacity, stride=stride)

    half = CELL_SECTORS // 2
    part = jax.ShapeDtypeStruct((half, 2 * portion, LANES), jnp.bfloat16)
    serve_pairs = total_users // 2
    low, high = pl.pallas_call(
        functools.partial(serve_kernel, **sizes),
        out_shape=(part, part),
        in_specs=[SMEM, SMEM, SMEM, VMEM, VMEM, VMEM],
        out_specs=(VMEM, VMEM),
        scratch_shapes=link_scratch(link_total, serve_pairs)
        + [
            pltpu.VMEM((CELL_SECTORS, 2 * portion, LANES), jnp.float32),
            pltpu.VMEM((2 * total_users, LANES), jnp.float32),
        ]
        + table_shapes(serve_pairs, steps),
        compiler_params=LIMIT,
    )(
        scalar,
        nearby_sectors,
        serving_slot,
        own_rows,
        other_rows,
        symbols.reshape(2 * total_users, LANES),
    )

    up = [(n, n + 1) for n in range(devices - 1)]
    down = [(m, n) for n, m in up]
    before = lax.ppermute(high, "cell", up)
    after = lax.ppermute(low, "cell", down)

    pair_total = link_total // 2
    block = 16
    response = pl.pallas_call(
        functools.partial(respond_kernel, **sizes),
        out_shape=jax.ShapeDtypeStruct((pair_total, 4 * portion, LANES), jnp.bfloat16),
        grid=(pair_total // block,),
        in_specs=[SMEM, VMEM, VMEM],
        out_specs=pl.BlockSpec((block, 4 * portion, LANES), lambda n: (n, 0, 0)),
        scratch_shapes=link_scratch(link_total, block) + table_shapes(block, steps),
        cost_estimate=pl.CostEstimate(
            flops=pair_total * 2 * 128 * 128 * 256 * 40,
            bytes_accessed=pair_total * 4 * portion * LANES * 2,
            transcendentals=0,
        ),
        compiler_params=LIMIT,
    )(scalar, own_rows, other_rows)

    user_block = 8
    partial_value = pl.pallas_call(
        functools.partial(receive_kernel, portion=portion),
        out_shape=jax.ShapeDtypeStruct((2 * total_users, LANES), jnp.float32),
        grid=(total_users // user_block,),
        in_specs=[
            SMEM,
            SMEM,
            pl.BlockSpec(
                (user_block * NEARBY_COUNT // 2, 4 * portion, LANES), lambda n: (n, 0, 0)
            ),
            VMEM,
            VMEM,
            VMEM,
            VMEM,
        ],
        out_specs=pl.BlockSpec((2 * user_block, LANES), lambda n: (n, 0)),
        scratch_shapes=[
            pltpu.VMEM((CELL_SECTORS + 2 * REACH, 2 * portion, LANES), jnp.float32)
        ],
        compiler_params=LIMIT,
    )(scalar, nearby_sectors, response, before, low, high, after)
    summed = partial_value + lax.ppermute(partial_value, "grp", swap)
    return summed.reshape(total_users, 2, FRAME_TONES)


def solution(mesh):
    placed = (
        P("cell"),
        P("cell"),
        P(None, "cell"),
        P("cell"),
        P("cell"),
        P("cell"),
        P(None, "cell"),
        P("cell"),
        P("cell", None, None),
    )
    return jax.shard_map(
        shards, mesh=mesh, in_specs=placed, out_specs=P("cell", None, None), check_vma=False
    )
```

```python
import functools
import math

import jax
import jax.numpy as jnp
from jax import lax
from jax.experimental import pallas as pl
from jax.experimental.pallas import tpu as pltpu
from jax.sharding import PartitionSpec as P

SECTOR_ANTENNAS = 64
FRAME_TONES = 128
PMAX = 64
NEARBY_COUNT = 8
CELL_SECTORS = 32
REACH = 16
EPSILON = 1e-06

LANES = 128
GROUP = 8
HALF = FRAME_TONES // 2
SPANS = HALF // (2 * GROUP)
LEVELS = 32767.0
DELAY_STEP = 64.0 / 65535.0
SYMBOL_TOP = 4.0

SIN_TERMS = tuple((-1.0) ** n / math.factorial(2 * n + 1) for n in range(6))
COS_TERMS = tuple((-1.0) ** n / math.factorial(2 * n) for n in range(8))


def polynomial(terms, square):
    total = terms[-1]
    for term in terms[-2::-1]:
        total = total * square + term
    return total


def quarter_cos_sin(x):
    square = x * x
    return polynomial(COS_TERMS, square), x * polynomial(SIN_TERMS, square)


def cos_sin_turns(turns):
    turns = turns - jnp.round(turns)
    c, s = quarter_cos_sin(math.pi * turns)
    return 1.0 - 2.0 * s * s, 2.0 * s * c


def times(x, y):
    return x[0] * y[0] - x[1] * y[1], x[0] * y[1] + x[1] * y[0]


def powers(base, count):
    found = {1: base}
    for n in range(2, count + 1):
        found[n] = times(found[n // 2], found[n - n // 2])
    return found


def join(high, low):
    return (high.astype(jnp.int32) << 16) | (low.astype(jnp.int32) & 0xFFFF)


def split(word):
    return (word >> 16).astype(jnp.float32), ((word << 16) >> 16).astype(jnp.float32)


def root_code(value):
    root = jnp.sqrt(jnp.sqrt(jnp.sqrt(jnp.abs(value)))) * LEVELS
    return jnp.round(jnp.where(value < 0, -root, root))


def root_value(code):
    unit = code * (1.0 / LEVELS)
    power = unit * unit
    power = power * power
    power = power * power
    return jnp.where(code < 0, -power, power)


def lane_index(rows):
    return lax.broadcasted_iota(jnp.int32, (rows, LANES), 1)


def fetch(pairs, sems):
    copies = [pltpu.make_async_copy(a, b, sems.at[n]) for n, (a, b) in enumerate(pairs)]
    for copy in copies:
        copy.start()
    return copies


def pack_kernel(
    link_hbm, count_hbm, offset_hbm, delay_hbm, angle_hbm, gain_hbm, out_ref,
    link_ref, count_ref, offset_ref, delay_ref, angle_ref, gain_ref, word_ref, sems,
    *, link_total, capacity, stride,
):
    copies = fetch(
        [
            (link_hbm, link_ref),
            (count_hbm, count_ref),
            (offset_hbm, offset_ref),
            (delay_hbm, delay_ref),
            (angle_hbm, angle_ref),
            (gain_hbm, gain_ref),
        ],
        sems,
    )
    lane = lane_index(1)
    out_ref[...] = jnp.zeros_like(out_ref)
    empty = jnp.full((1, LANES), -1, jnp.int32)
    tag_row = capacity // 2
    for owner in range(out_ref.shape[0] // stride):
        out_ref[owner * stride + tag_row : owner * stride + tag_row + 1, :] = empty
    for copy in copies:
        copy.wait()
    rows = delay_ref.shape[0]
    lower = lax.axis_index("grp") == 0
    c, s = quarter_cos_sin(angle_ref[...] * 0.5)
    gain_re, gain_im = gain_ref[:, 0, :], gain_ref[:, 1, :]
    high = jnp.where(lower, jnp.round(delay_ref[...] * (1.0 / DELAY_STEP)) - 32768.0, root_code(gain_re))
    low = jnp.where(lower, jnp.round(2.0 * LEVELS * s * c), root_code(gain_im))
    word_ref[:rows, :] = join(high, low)
    link_bits = link_total.bit_length() - 1

    def step(slot, carry):
        last_owner, place, tags = carry
        link = link_ref[slot]
        owner = link >> link_bits
        fresh = owner != last_owner
        place = jnp.where(fresh, 0, place + 1)
        offset = offset_ref[slot]
        row = offset >> 7
        shift = offset & (LANES - 1)
        word = jnp.where(lane >= shift, word_ref[pl.ds(row, 1), :], word_ref[pl.ds(row + 1, 1), :])
        start = (place & 1) * PMAX
        word = pltpu.roll(word, (start - shift) & (LANES - 1), 1)
        within = lane - start
        live = (within >= 0) & (within < count_ref[slot])
        base = owner * stride
        pltpu.store(out_ref.at[pl.ds(base + (place >> 1), 1), :], word, mask=live)
        tags = jnp.where(fresh, -1, tags)
        tags = jnp.where(lane == place, link - (owner << link_bits), tags)
        out_ref[pl.ds(base + tag_row, 1), :] = tags
        return owner, place, tags

    lax.fori_loop(0, link_total, step, (jnp.int32(-1), jnp.int32(0), empty), unroll=16)


def find_rows(own_ref, table_ref, capacity, stride):
    total_rows = own_ref.shape[0]
    senders = total_rows // stride
    tags = own_ref[pl.ds(capacity // 2, senders, stride=stride), :].astype(jnp.float32).T
    depth = min(pl.cdiv(capacity, GROUP) * GROUP, LANES)
    tags = tags[:depth]
    place = lax.broadcasted_iota(jnp.int32, (depth, LANES), 0)
    inside = place < capacity
    lane = lane_index(depth)
    value = ((place >> 1) + total_rows * ((place ^ lane) & 1)).astype(jnp.float32)
    lane = lane.astype(jnp.float32)
    rows = table_ref.shape[0]
    totals = [jnp.zeros((depth, LANES), jnp.float32) for _ in range(rows)]
    for sender in range(senders):
        column = jnp.broadcast_to(tags[:, sender : sender + 1], (depth, LANES))
        column = jnp.where(inside, column, -1.0)
        here = value + float(sender * stride)
        for n in range(rows):
            totals[n] += jnp.where(column == lane + float(n * LANES), here, 0.0)
    for n in range(rows):
        table_ref[n : n + 1, :] = jnp.sum(totals[n], axis=0, keepdims=True).astype(jnp.int32)


def sort_kernel(
    nearby_hbm, slot_hbm, symbol_hbm, own_ref, other_ref, rows_ref, table_ref, list_ref,
    nearby_ref, slot_ref, symbol_ref, place_ref, sems, *, capacity, stride,
):
    copies = fetch(
        [(nearby_hbm, nearby_ref), (slot_hbm, slot_ref), (symbol_hbm, symbol_ref)], sems
    )
    find_rows(own_ref, table_ref, capacity, stride)
    copies += fetch([(table_ref, place_ref)], sems.at[pl.ds(3, 1)])
    total_rows = own_ref.shape[0]
    lower = lax.axis_index("grp") == 0
    own, other = own_ref[...], other_ref[...]
    for n, words in enumerate((jnp.where(lower, own, other), jnp.where(lower, other, own))):
        rows_ref[n, :total_rows, :] = words
        rows_ref[n, total_rows:, :] = pltpu.roll(words, PMAX, 1)
    for copy in copies:
        copy.wait()
    users = slot_ref.shape[0]
    pairs = users // 2
    left = lane_index(1) < PMAX
    lane = lane_index(1)
    sectors = jnp.zeros((1, LANES), jnp.int32)
    first_sector = lax.axis_index("cell") * CELL_SECTORS
    for pair in range(pairs):
        found = []
        for user in (2 * pair, 2 * pair + 1):
            slot = slot_ref[user]
            link = user * NEARBY_COUNT + slot
            row = place_ref[user * NEARBY_COUNT // LANES, link & (LANES - 1)]
            turned = jnp.where(row < total_rows, row + total_rows, row - total_rows)
            found.append(jnp.where(((slot ^ user) & 1) == 0, row, turned))
            sectors = jnp.where(lane == user, nearby_ref[slot, user] - first_sector, sectors)
        for n in range(2):
            even = rows_ref[n, pl.ds(found[0], 1), :]
            odd = rows_ref[n, pl.ds(found[1], 1), :]
            list_ref[n * pairs + pair : n * pairs + pair + 1, :] = jnp.where(left, even, odd)
    symbols = symbol_ref[...].astype(jnp.float32) * (1.0 / SYMBOL_TOP)
    code_ref = list_ref.at[2 * pairs : 2 * pairs + users, :]
    codes = root_code(symbols).reshape(users, 2, LANES)
    code_ref[...] = join(codes[:, 0, :], codes[:, 1, :])
    base = 2 * pairs + users
    list_ref[base : base + GROUP, :] = jnp.broadcast_to(sectors, (GROUP, LANES))


def make_tables(words_ref, groups, first_antenna, tables):
    fine, centre, last, near, far = tables
    steps = far.shape[1] // last.shape[1]
    for group in groups:
        rows = pl.ds(group * GROUP, GROUP)
        delay, sine = split(words_ref[0, rows, :])
        delay = (delay + 32768.0) * DELAY_STEP
        sine = sine * (1.0 / LEVELS)
        gain_re, gain_im = (root_value(code) for code in split(words_ref[1, rows, :]))

        def put(ref, n, count, value):
            at = pl.ds(group * (GROUP * count) + n, GROUP, stride=count) if count > 1 else rows
            ref[0, at, :] = value[0]
            ref[1, at, :] = value[1]

        def half_steps(half):
            whole = times(half, half)
            up = powers(whole, GROUP - 1)
            return whole, [half] + [times(half, up[n]) for n in range(1, GROUP)]

        c, s = quarter_cos_sin(delay * (math.pi / FRAME_TONES))
        whole, found = half_steps((c, -s))
        for n in range(GROUP):
            put(fine, n, GROUP, found[n])
        top = found[GROUP - 1]
        wide = times(times(top, top), whole)
        value = top
        for n in range(SPANS):
            if n:
                value = times(value, wide)
            put(centre, n, SPANS, value)
        put(last, 0, 1, times(value, times(top, whole)))

        c, s = cos_sin_turns(sine * 0.25)
        whole, found = half_steps((c, -s))
        for n in range(GROUP):
            put(near, n, GROUP, found[n])
        top = found[GROUP - 1]
        wide = times(times(top, top), whole)
        c, s = cos_sin_turns(sine * (0.5 * first_antenna))
        value = times(times((gain_re, gain_im), (c, -s)), top)
        for n in range(steps):
            if n:
                value = times(value, wide)
            put(far, n, steps, value)


def both_sides(centre, fine):
    a, b = centre[0] * fine[0], centre[1] * fine[1]
    c, d = centre[0] * fine[1], centre[1] * fine[0]
    return (a - b, c + d), (a + b, d - c)


def sides_of(centre_ref, fine_ref, pair, spans):
    at = pl.ds(pl.multiple_of(pair * GROUP, GROUP), GROUP)
    fine = (fine_ref[0, at, :], fine_ref[1, at, :])
    found = []
    for n in range(spans):
        row = pl.ds(pair * spans + n, 1)
        found.extend(both_sides((centre_ref[0, row, :], centre_ref[1, row, :]), fine))
    return found


def stack(values, part):
    return jnp.concatenate([v[part] for v in values], axis=0).astype(jnp.bfloat16)


def build_operands(pair, tables, tone_ref, mix_ref):
    fine, centre, last, near, far = tables
    delay = sides_of(centre, fine, pair, SPANS)
    row = pl.ds(pair, 1)
    final = lax.broadcasted_iota(jnp.int32, (GROUP, LANES), 0) == GROUP - 1
    steps = far.shape[1] // last.shape[1]
    spread = sides_of(far, near, pair, steps)
    portion = mix_ref.shape[0] // 2
    for n in range(2):
        tone_ref[n * HALF : (n + 1) * HALF, :] = stack(delay, n)
        swapped = jnp.where(final, last[n, row, :], delay[1][n])
        head = jnp.concatenate([delay[0][n], swapped], axis=0).astype(jnp.bfloat16)
        at = 2 * HALF + 2 * GROUP * n
        tone_ref[at : at + 2 * GROUP, :] = head
        mix_ref[n * portion : (n + 1) * portion, :] = stack(spread, n)


def multiply_operands(tone_ref, mix_ref):
    re, im = tone_ref[:HALF, :], tone_ref[HALF : 2 * HALF, :]
    head = [tone_ref[2 * HALF + 2 * GROUP * n : 2 * HALF + 2 * GROUP * (n + 1), :] for n in range(2)]
    low_re = jnp.concatenate([head[0], re[2 * GROUP :]], axis=0)
    low_im = jnp.concatenate([head[1], im[2 * GROUP :]], axis=0)
    tones = jnp.concatenate(
        [jnp.concatenate([re, -im], axis=1), jnp.concatenate([low_re, low_im], axis=1)], axis=0
    )
    portion = mix_ref.shape[0] // 2
    spread_re, spread_im = mix_ref[:portion, :], mix_ref[portion:, :]
    lane = lane_index(1)
    blocks = []
    for keep in (lane < PMAX, lane >= PMAX):
        keep = jnp.where(keep, 1.0, 0.0).astype(jnp.bfloat16)
        a, b, c = spread_re * keep, spread_im * keep, spread_re * -keep
        blocks.append(jnp.concatenate([a, b], axis=1))
        blocks.append(jnp.concatenate([b, c], axis=1))
    return lax.dot_general(
        jnp.concatenate(blocks, axis=0),
        tones,
        (((1,), (1,)), ((), ())),
        preferred_element_type=jnp.float32,
    )


def all_responses(pairs, tables, buffers, emit):
    tone_a, mix_a, tone_b, mix_b = buffers
    block = tone_a.shape[0]
    blocks = pairs // block

    def build(index, tone_ref, mix_ref):
        for n in range(block):
            build_operands(index * block + n, tables, tone_ref.at[n], mix_ref.at[n])

    def multiply(index, tone_ref, mix_ref):
        for n in range(block):
            emit(index * block + n, multiply_operands(tone_ref.at[n], mix_ref.at[n]))

    build(0, tone_a, mix_a)

    def step(n, carry):
        once = jnp.minimum(n + 1, 1)

        def first(_, carry):
            multiply(2 * n, tone_a, mix_a)
            build(2 * n + 1, tone_b, mix_b)
            return carry

        def second(_, carry):
            multiply(2 * n + 1, tone_b, mix_b)
            build(jnp.minimum(2 * n + 2, blocks - 1), tone_a, mix_a)
            return carry

        lax.fori_loop(0, once, first, 0)
        lax.fori_loop(0, once, second, 0)
        return carry

    lax.fori_loop(0, blocks // 2, step, 0)


def tone_of_place(lane):
    place = lane & (HALF - 1)
    within = place & 15
    above = (place & ~15) + jnp.where(within < GROUP, within + GROUP, 15 - within)
    below = jnp.where(above == 0, HALF, above)
    return HALF + jnp.where(lane < HALF, above, -below)


def place_of_tone(lane):
    away = jnp.where(lane >= HALF, lane - HALF, (HALF - lane) & (HALF - 1))
    within = away & 15
    place = (away & ~15) + jnp.where(within >= GROUP, within - GROUP, 15 - within)
    return jnp.where(lane >= HALF, place, HALF + place)


def reorder(values, index):
    pieces = [
        jnp.take_along_axis(values[n : n + GROUP], index, axis=1)
        for n in range(0, values.shape[0], GROUP)
    ]
    return jnp.concatenate(pieces, axis=0)


def respond_kernel(rows_ref, table_ref, out_ref, place_ref, words, sem, *scratch, portion):
    tables, buffers = scratch[:5], scratch[5:]
    for copy in fetch([(table_ref, place_ref)], sem):
        copy.wait()
    pairs = out_ref.shape[0]
    left = lane_index(1) < PMAX
    chunk = 16

    def take(index, carry):
        first = index * (2 * chunk)
        row = first >> 7
        base = first & (LANES - 1)
        for n in range(chunk):
            even = place_ref[row, base + 2 * n]
            odd = place_ref[row, base + 2 * n + 1]
            for field in range(2):
                value = jnp.where(
                    left, rows_ref[field, pl.ds(even, 1), :], rows_ref[field, pl.ds(odd, 1), :]
                )
                words[field, pl.ds(index * chunk + n, 1), :] = value
        return carry

    lax.fori_loop(0, pairs // chunk, take, 0)
    first_antenna = (lax.axis_index("grp") * portion).astype(jnp.float32)
    batch = 4

    def tabulate(index, carry):
        make_tables(words, [index * batch + n for n in range(batch)], first_antenna, tables)
        return carry

    lax.fori_loop(0, pairs // (GROUP * batch), tabulate, 0)

    def emit(pair, response):
        out_ref[pair] = response

    all_responses(pairs, tables, buffers, emit)


def receive_kernel(
    nearby_hbm, slot_hbm, symbol_hbm, response_ref, first_ref, second_ref, out_ref,
    nearby_ref, slot_ref, symbol_ref, sector_ref, sems, words, symbols, remote, *scratch, portion,
):
    tables, buffers = scratch[:5], scratch[5:]
    users = nearby_hbm.shape[1]
    pairs = users // 2
    base = 2 * pairs + users
    copies = fetch(
        [
            (nearby_hbm, nearby_ref),
            (slot_hbm, slot_ref),
            (symbol_hbm, symbol_ref),
            (first_ref.at[base : base + 1, :], sector_ref.at[0:1, :]),
            (second_ref.at[base : base + 1, :], sector_ref.at[1:2, :]),
        ],
        sems,
    )
    remote[...] = jnp.zeros_like(remote)
    order = tone_of_place(lane_index(GROUP))
    for n, ref in enumerate((first_ref, second_ref)):
        for field in range(2):
            words[field, n * pairs : (n + 1) * pairs, :] = ref[field * pairs : (field + 1) * pairs, :]
        codes = split(ref[2 * pairs : 2 * pairs + users, :])
        for part in range(2):
            symbols[part, n * users : (n + 1) * users, :] = reorder(
                root_value(codes[part]) * SYMBOL_TOP, order
            )
    first_antenna = (lax.axis_index("grp") * portion).astype(jnp.float32)
    make_tables(words, list(range(2 * pairs // GROUP)), first_antenna, tables)
    for copy in copies:
        copy.wait()
    own = reorder(symbol_ref[...].astype(jnp.float32), order).reshape(users, 2, LANES)
    for part in range(2):
        symbols[part, 2 * users :, :] = own[:, part, :]

    def contribute(place, row, re, im):
        sym_re = symbols[0, pl.ds(row, 1), :]
        sym_im = symbols[1, pl.ds(row, 1), :]
        remote[place, :portion, :] += re * sym_re + im * sym_im
        remote[place, portion:, :] += re * sym_im - im * sym_re

    window = CELL_SECTORS + 2 * REACH
    here = lax.axis_index("cell")
    first_sector = here * CELL_SECTORS - REACH

    def own_user(user, carry):
        slot = slot_ref[user]
        pair = user * (NEARBY_COUNT // 2) + (slot >> 1)
        at = pl.multiple_of((slot & 1) * (2 * portion), 2 * portion)
        re = response_ref[pair, pl.ds(at, portion), :]
        im = response_ref[pair, pl.ds(at + portion, portion), :]
        contribute(nearby_ref[slot, user] - first_sector, 2 * users + user, re, im)
        return carry

    lax.fori_loop(0, users, own_user, 0, unroll=2)
    after_first = (here & 1) == 0

    def emit(pair, response):
        for n in range(2):
            row = pair * 2 + n
            second = row >= users
            user = jnp.where(second, row - users, row)
            sector = sector_ref[jnp.where(second, 1, 0), user]
            place = jnp.where(second != after_first, sector + CELL_SECTORS, sector - CELL_SECTORS) + REACH
            place = jnp.where((place >= 0) & (place < window), place, window)
            re = response[2 * n * portion : (2 * n + 1) * portion]
            im = response[(2 * n + 1) * portion : (2 * n + 2) * portion]
            contribute(place, row, re, im)

    all_responses(2 * pairs, tables, buffers, emit)

    def normalise(sector, carry):
        value = remote[sector]
        re, im = value[:portion], value[portion:]
        power = jnp.sum(re * re + im * im, axis=1, keepdims=True) * (1.0 / FRAME_TONES)
        scale = 1.0 / jnp.sqrt(power + EPSILON)
        remote[sector, :portion, :] = (re * scale).astype(jnp.bfloat16).astype(jnp.float32)
        remote[sector, portion:, :] = (im * scale).astype(jnp.bfloat16).astype(jnp.float32)
        return carry

    lax.fori_loop(0, window, normalise, 0, unroll=8)

    def one_user(user, carry):
        total_re = jnp.zeros((GROUP, LANES), jnp.float32)
        total_im = jnp.zeros((GROUP, LANES), jnp.float32)
        for k in range(NEARBY_COUNT):
            sector = nearby_ref[k, user] - first_sector
            pair = user * (NEARBY_COUNT // 2) + k // 2
            at = (k % 2) * 2 * portion
            for n in range(0, portion, GROUP):
                re = response_ref[pair, at + n : at + n + GROUP, :]
                im = response_ref[pair, at + portion + n : at + portion + n + GROUP, :]
                other_re = remote[sector, n : n + GROUP, :]
                other_im = remote[sector, portion + n : portion + n + GROUP, :]
                total_re = total_re + (re * other_re - im * other_im)
                total_im = total_im + (re * other_im + im * other_re)
        scale = 1.0 / math.sqrt(SECTOR_ANTENNAS)
        out_ref[pl.ds(user * 2, 1), :] = jnp.sum(total_re, axis=0, keepdims=True) * scale
        out_ref[pl.ds(user * 2 + 1, 1), :] = jnp.sum(total_im, axis=0, keepdims=True) * scale
        return carry

    lax.fori_loop(0, users, one_user, 0, unroll=2)
    out_ref[...] = reorder(out_ref[...], place_of_tone(lane_index(GROUP)))


VMEM = pl.BlockSpec(memory_space=pltpu.VMEM)
HBM = pl.BlockSpec(memory_space=pltpu.HBM)
LIMIT = pltpu.CompilerParams(vmem_limit_bytes=16 << 20)
BLOCK = 8


def in_hbm(values):
    return pltpu.with_memory_space_constraint(values, pltpu.HBM)


def response_scratch(pairs, portion):
    counts = (GROUP, SPANS, 1, GROUP, portion // (2 * GROUP))
    tables = [pltpu.VMEM((2, pairs * n, LANES), jnp.float32) for n in counts]
    factors = [
        pltpu.VMEM((BLOCK, 2 * HALF + 4 * GROUP, LANES), jnp.bfloat16),
        pltpu.VMEM((BLOCK, 2 * portion, LANES), jnp.bfloat16),
    ]
    return tables + factors + factors


def shards(
    path_delay,
    path_angle,
    path_gain,
    slot_counts,
    slot_offsets,
    ray_link,
    nearby_sectors,
    serving_slot,
    symbols,
):
    devices = lax.axis_size("cell")
    worker_count = lax.axis_size("grp")
    path_total = path_delay.shape[0]
    link_total = slot_counts.shape[0]
    total_users = serving_slot.shape[0]
    capacity = 2 * link_total // devices
    stride = pl.cdiv(capacity // 2 + 1, GROUP) * GROUP
    portion = SECTOR_ANTENNAS // worker_count
    swap = [(n, worker_count - 1 - n) for n in range(worker_count)]
    path_rows = path_total // LANES
    link_rows = link_total // LANES
    sizes = dict(capacity=capacity, stride=stride)

    packed = pl.pallas_call(
        functools.partial(pack_kernel, link_total=link_total, **sizes),
        out_shape=jax.ShapeDtypeStruct((devices * stride, LANES), jnp.int32),
        in_specs=[HBM] * 6,
        out_specs=VMEM,
        scratch_shapes=[pltpu.SMEM((link_total,), jnp.int32)] * 3
        + [
            pltpu.VMEM((path_rows, LANES), jnp.float32),
            pltpu.VMEM((path_rows, LANES), jnp.float32),
            pltpu.VMEM((path_rows, 2, LANES), jnp.float32),
            pltpu.VMEM((pl.cdiv(path_rows + 1, GROUP) * GROUP, LANES), jnp.int32),
            pltpu.SemaphoreType.DMA((6,)),
        ],
        compiler_params=LIMIT,
    )(
        in_hbm(ray_link),
        in_hbm(slot_counts),
        in_hbm(slot_offsets),
        in_hbm(path_delay.reshape(path_rows, LANES)),
        in_hbm(path_angle.reshape(path_rows, LANES)),
        in_hbm(path_gain.reshape(2, path_rows, LANES).transpose(1, 0, 2)),
    )
    arrived = lax.all_to_all(
        packed.reshape(devices, stride, LANES), "cell", split_axis=0, concat_axis=0, tiled=True
    )
    other = lax.ppermute(arrived, "grp", swap)

    row_total = devices * stride
    list_rows = 2 * total_users + GROUP
    symbol_rows = in_hbm(symbols.reshape(2 * total_users, LANES))
    nearby_sectors = in_hbm(nearby_sectors)
    serving_slot = in_hbm(serving_slot)
    small_scratch = [
        pltpu.SMEM(nearby_sectors.shape, jnp.int32),
        pltpu.SMEM((total_users,), jnp.int32),
        pltpu.VMEM((2 * total_users, LANES), jnp.bfloat16),
    ]
    rows, table, listed = pl.pallas_call(
        functools.partial(sort_kernel, **sizes),
        out_shape=(
            jax.ShapeDtypeStruct((2, 2 * row_total, LANES), jnp.int32),
            jax.ShapeDtypeStruct((link_rows, LANES), jnp.int32),
            jax.ShapeDtypeStruct((list_rows, LANES), jnp.int32),
        ),
        in_specs=[HBM] * 3 + [VMEM] * 2,
        out_specs=(VMEM, VMEM, VMEM),
        scratch_shapes=small_scratch
        + [pltpu.SMEM((link_rows, LANES), jnp.int32), pltpu.SemaphoreType.DMA((4,))],
        compiler_params=LIMIT,
    )(
        nearby_sectors,
        serving_slot,
        symbol_rows,
        arrived.reshape(row_total, LANES),
        other.reshape(row_total, LANES),
    )

    def exchange(first):
        pairs = [(n, n + 1) for n in range(first, devices - 1, 2)]
        return lax.ppermute(listed, "cell", pairs + [(m, n) for n, m in pairs])

    first_list, second_list = exchange(0), exchange(1)

    pair_total = link_total // 2
    response = pl.pallas_call(
        functools.partial(respond_kernel, portion=portion),
        out_shape=jax.ShapeDtypeStruct((pair_total, 4 * portion, LANES), jnp.float32),
        in_specs=[VMEM, VMEM],
        out_specs=VMEM,
        scratch_shapes=[
            pltpu.SMEM((link_rows, LANES), jnp.int32),
            pltpu.VMEM((2, pair_total, LANES), jnp.int32),
            pltpu.SemaphoreType.DMA((1,)),
        ]
        + response_scratch(pair_total, portion),
        cost_estimate=pl.CostEstimate(
            flops=pair_total * 2 * 128 * 128 * 256 * 40,
            bytes_accessed=pair_total * 4 * portion * LANES * 2,
            transcendentals=0,
        ),
        compiler_params=LIMIT,
    )(rows, table)

    partial_value = pl.pallas_call(
        functools.partial(receive_kernel, portion=portion),
        out_shape=jax.ShapeDtypeStruct((2 * total_users, LANES), jnp.float32),
        in_specs=[HBM] * 3 + [VMEM] * 3,
        out_specs=VMEM,
        scratch_shapes=small_scratch
        + [
            pltpu.SMEM((2, LANES), jnp.int32),
            pltpu.SemaphoreType.DMA((5,)),
            pltpu.VMEM((2, total_users, LANES), jnp.int32),
            pltpu.VMEM((2, 3 * total_users, LANES), jnp.float32),
            pltpu.VMEM((CELL_SECTORS + 2 * REACH + 1, 2 * portion, LANES), jnp.float32),
        ]
        + response_scratch(total_users, portion),
        compiler_params=LIMIT,
    )(nearby_sectors, serving_slot, symbol_rows, response, first_list, second_list)
    summed = partial_value + lax.ppermute(partial_value, "grp", swap)
    return summed.reshape(total_users, 2, FRAME_TONES)


def solution(mesh):
    placed = (
        P("cell"),
        P("cell"),
        P(None, "cell"),
        P("cell"),
        P("cell"),
        P("cell"),
        P(None, "cell"),
        P("cell"),
        P("cell", None, None),
    )
    return jax.shard_map(
        shards, mesh=mesh, in_specs=placed, out_specs=P("cell", None, None), check_vma=False
    )
```

```python
import functools
import math

import jax
import jax.numpy as jnp
from jax import lax
from jax.experimental import pallas as pl
from jax.experimental.pallas import tpu as pltpu
from jax.sharding import PartitionSpec as P

SECTOR_ANTENNAS = 64
FRAME_TONES = 128
PMAX = 64
NEARBY_COUNT = 8
CELL_SECTORS = 32
REACH = 16
EPSILON = 1e-06

LANES = 128
GROUP = 8
HALF = FRAME_TONES // 2
SPANS = HALF // (2 * GROUP)
LEVELS = 32767.0
PITCH = 64
UNROLL = 32
DELAY_STEP = 64.0 / 65535.0
SYMBOL_TOP = 4.0

SIN_TERMS = tuple((-1.0) ** n / math.factorial(2 * n + 1) for n in range(6))
COS_TERMS = tuple((-1.0) ** n / math.factorial(2 * n) for n in range(8))


def polynomial(terms, square):
    total = terms[-1]
    for term in terms[-2::-1]:
        total = total * square + term
    return total


def quarter_cos_sin(x):
    square = x * x
    return polynomial(COS_TERMS, square), x * polynomial(SIN_TERMS, square)


def cos_sin_turns(turns):
    turns = turns - jnp.round(turns)
    c, s = quarter_cos_sin(math.pi * turns)
    return 1.0 - 2.0 * s * s, 2.0 * s * c


def times(x, y):
    return x[0] * y[0] - x[1] * y[1], x[0] * y[1] + x[1] * y[0]


def powers(base, count):
    found = {1: base}
    for n in range(2, count + 1):
        found[n] = times(found[n // 2], found[n - n // 2])
    return found


def join(high, low):
    return (high.astype(jnp.int32) << 16) | (low.astype(jnp.int32) & 0xFFFF)


def split(word):
    return (word >> 16).astype(jnp.float32), ((word << 16) >> 16).astype(jnp.float32)


def root_code(value):
    root = jnp.sqrt(jnp.sqrt(jnp.sqrt(jnp.abs(value)))) * LEVELS
    return jnp.round(jnp.where(value < 0, -root, root))


def root_value(code):
    unit = code * (1.0 / LEVELS)
    power = unit * unit
    power = power * power
    power = power * power
    return jnp.where(code < 0, -power, power)


def lane_index(rows):
    return lax.broadcasted_iota(jnp.int32, (rows, LANES), 1)


def fetch(pairs, sems):
    copies = [pltpu.make_async_copy(a, b, sems.at[n]) for n, (a, b) in enumerate(pairs)]
    for copy in copies:
        copy.start()
    return copies


def pack_kernel(
    link_hbm, count_hbm, offset_hbm, delay_hbm, angle_hbm, gain_hbm, out_ref,
    link_ref, count_ref, offset_ref, delay_ref, angle_ref, real_ref, imag_ref, word_ref, stage_ref, sems,
    *, link_total, capacity, stride,
):
    copies = fetch(
        [
            (link_hbm, link_ref),
            (count_hbm, count_ref),
            (offset_hbm, offset_ref),
            (delay_hbm, delay_ref),
            (angle_hbm, angle_ref),
            (gain_hbm.at[:, 0, :], real_ref),
            (gain_hbm.at[:, 1, :], imag_ref),
        ],
        sems,
    )
    lane = lane_index(1)
    stage_ref[...] = jnp.zeros_like(stage_ref)
    for copy in copies:
        copy.wait()
    rows = delay_ref.shape[0]
    lower = lax.axis_index("grp") == 0
    c, s = quarter_cos_sin(angle_ref[...] * 0.5)
    gain_re, gain_im = real_ref[...], imag_ref[...]
    sine = 2.0 * s * c
    code = jnp.round(LEVELS * sine)
    turn = (sine - code * (1.0 / LEVELS)) * (0.5 * math.pi * (SECTOR_ANTENNAS - 1))
    gain_re, gain_im = gain_re + gain_im * turn, gain_im - gain_re * turn
    high = jnp.where(lower, jnp.round(delay_ref[...] * (1.0 / DELAY_STEP)) - 32768.0, root_code(gain_re))
    low = jnp.where(lower, code, root_code(gain_im))
    word_ref[:rows, :] = join(high, low)
    link_bits = link_total.bit_length() - 1
    owners = out_ref.shape[0] // stride
    tag_rows = max(owners, GROUP)
    tag_place = lax.broadcasted_iota(jnp.int32, (tag_rows, LANES), 0) * LANES + lane_index(tag_rows)

    def step(slot, carry):
        last_owner, key, tags = carry
        link = link_ref[slot]
        owner = link >> link_bits
        key = jnp.where(owner != last_owner, owner << 7, key + 1)
        offset = offset_ref[slot]
        row = offset >> 7
        shift = offset & (LANES - 1)
        word = jnp.where(lane >= shift, word_ref[pl.ds(row, 1), :], word_ref[pl.ds(row + 1, 1), :])
        start = (key & 1) << 6
        word = pltpu.roll(word, (start - shift) & (LANES - 1), 1)
        within = lane - start
        live = (within >= 0) & (within < count_ref[slot])
        pltpu.store(stage_ref.at[pl.ds(key >> 1, 1), :], word, mask=live)
        return owner, key, jnp.where(tag_place == key, link, tags)

    empty = jnp.full((tag_rows, LANES), -1, jnp.int32)
    tags = lax.fori_loop(0, link_total, step, (jnp.int32(-1), jnp.int32(0), empty), unroll=UNROLL)[2]
    for owner in range(owners):
        out_ref[owner * stride : (owner + 1) * stride, :] = stage_ref[
            owner * PITCH : owner * PITCH + stride, :
        ]
    out_ref[pl.ds(capacity // 2, owners, stride=stride), :] = tags[:owners]


def find_rows(own_ref, table_ref, capacity, stride):
    total_rows = own_ref.shape[0]
    senders = total_rows // stride
    tags = own_ref[pl.ds(capacity // 2, senders, stride=stride), :]
    tags = (tags - lax.axis_index("cell") * (table_ref.shape[0] * LANES)).astype(jnp.float32).T
    depth = min(pl.cdiv(capacity, GROUP) * GROUP, LANES)
    tags = tags[:depth]
    place = lax.broadcasted_iota(jnp.int32, (depth, LANES), 0)
    inside = place < capacity
    lane = lane_index(depth)
    value = ((place >> 1) + total_rows * ((place ^ lane) & 1)).astype(jnp.float32)
    lane = lane.astype(jnp.float32)
    rows = table_ref.shape[0]
    totals = [jnp.zeros((depth, LANES), jnp.float32) for _ in range(rows)]
    for sender in range(senders):
        column = jnp.broadcast_to(tags[:, sender : sender + 1], (depth, LANES))
        column = jnp.where(inside, column, -1.0)
        here = value + float(sender * stride)
        for n in range(rows):
            totals[n] += jnp.where(column == lane + float(n * LANES), here, 0.0)
    for n in range(rows):
        table_ref[n : n + 1, :] = jnp.sum(totals[n], axis=0, keepdims=True).astype(jnp.int32)


def sort_kernel(
    nearby_hbm, slot_hbm, symbol_hbm, own_ref, other_ref, rows_ref, table_ref, list_ref,
    nearby_ref, slot_ref, symbol_ref, place_ref, sems, *, capacity, stride,
):
    copies = fetch(
        [(nearby_hbm, nearby_ref), (slot_hbm, slot_ref), (symbol_hbm, symbol_ref)], sems
    )
    find_rows(own_ref, table_ref, capacity, stride)
    copies += fetch([(table_ref, place_ref)], sems.at[pl.ds(3, 1)])
    total_rows = own_ref.shape[0]
    lower = lax.axis_index("grp") == 0
    own, other = own_ref[...], other_ref[...]
    for n, words in enumerate((jnp.where(lower, own, other), jnp.where(lower, other, own))):
        rows_ref[n, :total_rows, :] = words
        rows_ref[n, total_rows:, :] = pltpu.roll(words, PMAX, 1)
    for copy in copies:
        copy.wait()
    users = slot_ref.shape[0]
    pairs = users // 2
    left = lane_index(1) < PMAX
    lane = lane_index(1)
    sectors = jnp.zeros((1, LANES), jnp.int32)
    first_sector = lax.axis_index("cell") * CELL_SECTORS
    for pair in range(pairs):
        found = []
        for user in (2 * pair, 2 * pair + 1):
            slot = slot_ref[user]
            link = user * NEARBY_COUNT + slot
            row = place_ref[user * NEARBY_COUNT // LANES, link & (LANES - 1)]
            turned = jnp.where(row < total_rows, row + total_rows, row - total_rows)
            found.append(jnp.where(((slot ^ user) & 1) == 0, row, turned))
            sectors = jnp.where(lane == user, nearby_ref[slot, user] - first_sector, sectors)
        for n in range(2):
            even = rows_ref[n, pl.ds(found[0], 1), :]
            odd = rows_ref[n, pl.ds(found[1], 1), :]
            list_ref[n * pairs + pair : n * pairs + pair + 1, :] = jnp.where(left, even, odd)
    symbols = symbol_ref[...].astype(jnp.float32) * (1.0 / SYMBOL_TOP)
    code_ref = list_ref.at[2 * pairs : 2 * pairs + users, :]
    codes = root_code(symbols).reshape(users, 2, LANES)
    code_ref[...] = join(codes[:, 0, :], codes[:, 1, :])
    base = 2 * pairs + users
    list_ref[base : base + GROUP, :] = jnp.broadcast_to(sectors, (GROUP, LANES))


def make_tables(words_ref, groups, first_antenna, tables):
    fine, centre, last, near, far = tables
    steps = far.shape[1] // last.shape[1]
    for group in groups:
        rows = pl.ds(group * GROUP, GROUP)
        delay, sine = split(words_ref[0, rows, :])
        delay = (delay + 32768.0) * DELAY_STEP
        sine = sine * (1.0 / LEVELS)
        gain_re, gain_im = (root_value(code) for code in split(words_ref[1, rows, :]))

        def put(ref, n, count, value):
            at = pl.ds(group * (GROUP * count) + n, GROUP, stride=count) if count > 1 else rows
            ref[0, at, :] = value[0]
            ref[1, at, :] = value[1]

        def half_steps(half):
            whole = times(half, half)
            up = powers(whole, GROUP - 1)
            return whole, [half] + [times(half, up[n]) for n in range(1, GROUP)]

        c, s = quarter_cos_sin(delay * (math.pi / FRAME_TONES))
        whole, found = half_steps((c, -s))
        for n in range(GROUP):
            put(fine, n, GROUP, found[n])
        top = found[GROUP - 1]
        wide = times(times(top, top), whole)
        value = top
        for n in range(SPANS):
            if n:
                value = times(value, wide)
            put(centre, n, SPANS, value)
        put(last, 0, 1, times(value, times(top, whole)))

        c, s = cos_sin_turns(sine * 0.25)
        whole, found = half_steps((c, -s))
        for n in range(GROUP):
            put(near, n, GROUP, found[n])
        top = found[GROUP - 1]
        wide = times(times(top, top), whole)
        c, s = cos_sin_turns(sine * (0.5 * first_antenna))
        value = times(times((gain_re, gain_im), (c, -s)), top)
        for n in range(steps):
            if n:
                value = times(value, wide)
            put(far, n, steps, value)


def both_sides(centre, fine):
    a, b = centre[0] * fine[0], centre[1] * fine[1]
    c, d = centre[0] * fine[1], centre[1] * fine[0]
    return (a - b, c + d), (a + b, d - c)


def sides_of(centre_ref, fine_ref, pair, spans):
    at = pl.ds(pl.multiple_of(pair * GROUP, GROUP), GROUP)
    fine = (fine_ref[0, at, :], fine_ref[1, at, :])
    found = []
    for n in range(spans):
        row = pl.ds(pair * spans + n, 1)
        found.extend(both_sides((centre_ref[0, row, :], centre_ref[1, row, :]), fine))
    return found


def stack(values, part):
    return jnp.concatenate([v[part] for v in values], axis=0).astype(jnp.bfloat16)


def build_operands(pair, tables, tone_ref, mix_ref):
    fine, centre, last, near, far = tables
    delay = sides_of(centre, fine, pair, SPANS)
    row = pl.ds(pair, 1)
    final = lax.broadcasted_iota(jnp.int32, (GROUP, LANES), 0) == GROUP - 1
    steps = far.shape[1] // last.shape[1]
    spread = sides_of(far, near, pair, steps)
    portion = mix_ref.shape[0] // 2
    for n in range(2):
        tone_ref[n * HALF : (n + 1) * HALF, :] = stack(delay, n)
        swapped = jnp.where(final, last[n, row, :], delay[1][n])
        head = jnp.concatenate([delay[0][n], swapped], axis=0).astype(jnp.bfloat16)
        at = 2 * HALF + 2 * GROUP * n
        tone_ref[at : at + 2 * GROUP, :] = head
        mix_ref[n * portion : (n + 1) * portion, :] = stack(spread, n)


def multiply_operands(tone_ref, mix_ref):
    re, im = tone_ref[:HALF, :], tone_ref[HALF : 2 * HALF, :]
    head = [tone_ref[2 * HALF + 2 * GROUP * n : 2 * HALF + 2 * GROUP * (n + 1), :] for n in range(2)]
    low_re = jnp.concatenate([head[0], re[2 * GROUP :]], axis=0)
    low_im = jnp.concatenate([head[1], im[2 * GROUP :]], axis=0)
    tones = jnp.concatenate(
        [jnp.concatenate([re, -im], axis=1), jnp.concatenate([low_re, low_im], axis=1)], axis=0
    )
    portion = mix_ref.shape[0] // 2
    spread_re, spread_im = mix_ref[:portion, :], mix_ref[portion:, :]
    lane = lane_index(1)
    blocks = []
    for keep in (lane < PMAX, lane >= PMAX):
        keep = jnp.where(keep, 1.0, 0.0).astype(jnp.bfloat16)
        a, b, c = spread_re * keep, spread_im * keep, spread_re * -keep
        blocks.append(jnp.concatenate([a, b], axis=1))
        blocks.append(jnp.concatenate([b, c], axis=1))
    return lax.dot_general(
        jnp.concatenate(blocks, axis=0),
        tones,
        (((1,), (1,)), ((), ())),
        preferred_element_type=jnp.float32,
    )


def all_responses(pairs, tables, buffers, emit):
    tone_a, mix_a, tone_b, mix_b = buffers
    block = tone_a.shape[0]
    blocks = pairs // block
    once = jnp.minimum(lax.axis_index("cell") + 1, 1)

    def build(index, tone_ref, mix_ref):
        for n in range(block):
            build_operands(index * block + n, tables, tone_ref.at[n], mix_ref.at[n])

    def multiply(index, tone_ref, mix_ref):
        for n in range(block):
            emit(index * block + n, multiply_operands(tone_ref.at[n], mix_ref.at[n]))

    def stage(index, now, later):
        def body(_, carry):
            if now is not None:
                multiply(index, *now)
            if later is not None:
                build(index + 1, *later)
            return carry

        lax.fori_loop(0, once, body, 0)

    first, second = (tone_a, mix_a), (tone_b, mix_b)
    stage(-1, None, first)

    def step(n, carry):
        stage(2 * n, first, second)
        stage(2 * n + 1, second, first)
        return carry

    lax.fori_loop(0, blocks // 2 - 1, step, 0)
    stage(blocks - 2, first, second)
    stage(blocks - 1, second, None)


def tone_of_place(lane):
    place = lane & (HALF - 1)
    within = place & 15
    above = (place & ~15) + jnp.where(within < GROUP, within + GROUP, 15 - within)
    below = jnp.where(above == 0, HALF, above)
    return HALF + jnp.where(lane < HALF, above, -below)


def place_of_tone(lane):
    away = jnp.where(lane >= HALF, lane - HALF, (HALF - lane) & (HALF - 1))
    within = away & 15
    place = (away & ~15) + jnp.where(within >= GROUP, within - GROUP, 15 - within)
    return jnp.where(lane >= HALF, place, HALF + place)


def reorder(values, index):
    pieces = [
        jnp.take_along_axis(values[n : n + GROUP], index, axis=1)
        for n in range(0, values.shape[0], GROUP)
    ]
    return jnp.concatenate(pieces, axis=0)


def respond_kernel(rows_ref, table_ref, out_ref, place_ref, words, sem, *scratch, portion):
    tables, buffers = scratch[:5], scratch[5:]
    for copy in fetch([(table_ref, place_ref)], sem):
        copy.wait()
    pairs = out_ref.shape[0]
    left = lane_index(1) < PMAX
    chunk = 16

    def take(index, carry):
        first = index * (2 * chunk)
        row = first >> 7
        base = first & (LANES - 1)
        for n in range(chunk):
            even = place_ref[row, base + 2 * n]
            odd = place_ref[row, base + 2 * n + 1]
            for field in range(2):
                value = jnp.where(
                    left, rows_ref[field, pl.ds(even, 1), :], rows_ref[field, pl.ds(odd, 1), :]
                )
                words[field, pl.ds(index * chunk + n, 1), :] = value
        return carry

    lax.fori_loop(0, pairs // chunk, take, 0)
    first_antenna = (lax.axis_index("grp") * portion).astype(jnp.float32)
    batch = 4

    def tabulate(index, carry):
        make_tables(words, [index * batch + n for n in range(batch)], first_antenna, tables)
        return carry

    lax.fori_loop(0, pairs // (GROUP * batch), tabulate, 0)

    def emit(pair, response):
        out_ref[pair] = response

    all_responses(pairs, tables, buffers, emit)


def receive_kernel(
    nearby_hbm, slot_hbm, symbol_hbm, response_ref, first_ref, second_ref, out_ref,
    nearby_ref, slot_ref, symbol_ref, sector_ref, sems, words, symbols, remote, *scratch, portion,
):
    tables, buffers = scratch[:5], scratch[5:]
    users = nearby_hbm.shape[1]
    pairs = users // 2
    base = 2 * pairs + users
    copies = fetch(
        [
            (nearby_hbm, nearby_ref),
            (slot_hbm, slot_ref),
            (symbol_hbm, symbol_ref),
            (first_ref.at[base : base + 1, :], sector_ref.at[0:1, :]),
            (second_ref.at[base : base + 1, :], sector_ref.at[1:2, :]),
        ],
        sems,
    )
    remote[...] = jnp.zeros_like(remote)
    order = tone_of_place(lane_index(GROUP))
    for n, ref in enumerate((first_ref, second_ref)):
        for field in range(2):
            words[field, n * pairs : (n + 1) * pairs, :] = ref[field * pairs : (field + 1) * pairs, :]
        codes = split(ref[2 * pairs : 2 * pairs + users, :])
        for part in range(2):
            symbols[part, n * users : (n + 1) * users, :] = reorder(
                root_value(codes[part]) * SYMBOL_TOP, order
            )
    first_antenna = (lax.axis_index("grp") * portion).astype(jnp.float32)
    make_tables(words, list(range(2 * pairs // GROUP)), first_antenna, tables)
    for copy in copies:
        copy.wait()
    own = reorder(symbol_ref[...].astype(jnp.float32), order).reshape(users, 2, LANES)
    for part in range(2):
        symbols[part, 2 * users :, :] = own[:, part, :]

    def contribute(place, row, re, im):
        sym_re = symbols[0, pl.ds(row, 1), :]
        sym_im = symbols[1, pl.ds(row, 1), :]
        remote[place, :portion, :] += re * sym_re + im * sym_im
        remote[place, portion:, :] += re * sym_im - im * sym_re

    window = CELL_SECTORS + 2 * REACH
    here = lax.axis_index("cell")
    first_sector = here * CELL_SECTORS - REACH

    def own_user(user, carry):
        slot = slot_ref[user]
        pair = user * (NEARBY_COUNT // 2) + (slot >> 1)
        at = pl.multiple_of((slot & 1) * (2 * portion), 2 * portion)
        re = response_ref[pair, pl.ds(at, portion), :]
        im = response_ref[pair, pl.ds(at + portion, portion), :]
        contribute(nearby_ref[slot, user] - first_sector, 2 * users + user, re, im)
        return carry

    lax.fori_loop(0, users, own_user, 0, unroll=8)
    after_first = (here & 1) == 0

    def emit(pair, response):
        for n in range(2):
            row = pair * 2 + n
            second = row >= users
            user = jnp.where(second, row - users, row)
            sector = sector_ref[jnp.where(second, 1, 0), user]
            place = jnp.where(second != after_first, sector + CELL_SECTORS, sector - CELL_SECTORS) + REACH
            place = jnp.where((place >= 0) & (place < window), place, window)
            re = response[2 * n * portion : (2 * n + 1) * portion]
            im = response[(2 * n + 1) * portion : (2 * n + 2) * portion]
            contribute(place, row, re, im)

    all_responses(2 * pairs, tables, buffers, emit)

    def normalise(sector, carry):
        value = remote[sector]
        re, im = value[:portion], value[portion:]
        power = jnp.sum(re * re + im * im, axis=1, keepdims=True) * (1.0 / FRAME_TONES)
        scale = 1.0 / jnp.sqrt(power + EPSILON)
        remote[sector, :portion, :] = (re * scale).astype(jnp.bfloat16).astype(jnp.float32)
        remote[sector, portion:, :] = (im * scale).astype(jnp.bfloat16).astype(jnp.float32)
        return carry

    lax.fori_loop(0, window, normalise, 0, unroll=8)

    def one_user(user, carry):
        total_re = jnp.zeros((GROUP, LANES), jnp.float32)
        total_im = jnp.zeros((GROUP, LANES), jnp.float32)
        for k in range(NEARBY_COUNT):
            sector = nearby_ref[k, user] - first_sector
            pair = user * (NEARBY_COUNT // 2) + k // 2
            at = (k % 2) * 2 * portion
            for n in range(0, portion, GROUP):
                re = response_ref[pair, at + n : at + n + GROUP, :]
                im = response_ref[pair, at + portion + n : at + portion + n + GROUP, :]
                other_re = remote[sector, n : n + GROUP, :]
                other_im = remote[sector, portion + n : portion + n + GROUP, :]
                total_re = total_re + (re * other_re - im * other_im)
                total_im = total_im + (re * other_im + im * other_re)
        scale = 1.0 / math.sqrt(SECTOR_ANTENNAS)
        out_ref[pl.ds(user * 2, 1), :] = jnp.sum(total_re, axis=0, keepdims=True) * scale
        out_ref[pl.ds(user * 2 + 1, 1), :] = jnp.sum(total_im, axis=0, keepdims=True) * scale
        return carry

    lax.fori_loop(0, users, one_user, 0, unroll=4)
    out_ref[...] = reorder(out_ref[...], place_of_tone(lane_index(GROUP)))


VMEM = pl.BlockSpec(memory_space=pltpu.VMEM)
HBM = pl.BlockSpec(memory_space=pltpu.HBM)
ANY = pl.BlockSpec(memory_space=pl.ANY)
LIMIT = pltpu.CompilerParams(vmem_limit_bytes=16 << 20)
BLOCK = 8


def in_hbm(values):
    return pltpu.with_memory_space_constraint(values, pltpu.HBM)


def response_scratch(pairs, portion):
    counts = (GROUP, SPANS, 1, GROUP, portion // (2 * GROUP))
    tables = [pltpu.VMEM((2, pairs * n, LANES), jnp.float32) for n in counts]
    factors = [
        pltpu.VMEM((BLOCK, 2 * HALF + 4 * GROUP, LANES), jnp.bfloat16),
        pltpu.VMEM((BLOCK, 2 * portion, LANES), jnp.bfloat16),
    ]
    return tables + factors + factors


def shards(
    path_delay,
    path_angle,
    path_gain,
    slot_counts,
    slot_offsets,
    ray_link,
    nearby_sectors,
    serving_slot,
    symbols,
):
    devices = lax.axis_size("cell")
    worker_count = lax.axis_size("grp")
    path_total = path_delay.shape[0]
    link_total = slot_counts.shape[0]
    total_users = serving_slot.shape[0]
    capacity = 2 * link_total // devices
    stride = pl.cdiv(capacity // 2 + 1, GROUP) * GROUP
    portion = SECTOR_ANTENNAS // worker_count
    swap = [(n, worker_count - 1 - n) for n in range(worker_count)]
    path_rows = path_total // LANES
    link_rows = link_total // LANES
    sizes = dict(capacity=capacity, stride=stride)

    packed = pl.pallas_call(
        functools.partial(pack_kernel, link_total=link_total, **sizes),
        out_shape=jax.ShapeDtypeStruct((devices * stride, LANES), jnp.int32),
        in_specs=[HBM] * 6,
        out_specs=VMEM,
        scratch_shapes=[pltpu.SMEM((link_total,), jnp.int32)] * 3
        + [
            pltpu.VMEM((path_rows, LANES), jnp.float32),
            pltpu.VMEM((path_rows, LANES), jnp.float32),
            pltpu.VMEM((path_rows, LANES), jnp.float32),
            pltpu.VMEM((path_rows, LANES), jnp.float32),
            pltpu.VMEM((pl.cdiv(path_rows + 1, GROUP) * GROUP, LANES), jnp.int32),
            pltpu.VMEM((devices * PITCH, LANES), jnp.int32),
            pltpu.SemaphoreType.DMA((7,)),
        ],
        compiler_params=LIMIT,
    )(
        in_hbm(ray_link),
        in_hbm(slot_counts),
        in_hbm(slot_offsets),
        in_hbm(path_delay.reshape(path_rows, LANES)),
        in_hbm(path_angle.reshape(path_rows, LANES)),
        in_hbm(path_gain.reshape(2, path_rows, LANES).transpose(1, 0, 2)),
    )
    arrived = lax.all_to_all(
        packed.reshape(devices, stride, LANES), "cell", split_axis=0, concat_axis=0, tiled=True
    )
    other = lax.ppermute(arrived, "grp", swap)

    row_total = devices * stride
    list_rows = 2 * total_users + GROUP
    symbol_rows = symbols.reshape(2 * total_users, LANES)
    small_scratch = [
        pltpu.SMEM(nearby_sectors.shape, jnp.int32),
        pltpu.SMEM((total_users,), jnp.int32),
        pltpu.VMEM((2 * total_users, LANES), jnp.bfloat16),
    ]
    rows, table, listed = pl.pallas_call(
        functools.partial(sort_kernel, **sizes),
        out_shape=(
            jax.ShapeDtypeStruct((2, 2 * row_total, LANES), jnp.int32),
            jax.ShapeDtypeStruct((link_rows, LANES), jnp.int32),
            jax.ShapeDtypeStruct((list_rows, LANES), jnp.int32),
        ),
        in_specs=[HBM] * 3 + [VMEM] * 2,
        out_specs=(VMEM, VMEM, VMEM),
        scratch_shapes=small_scratch
        + [pltpu.SMEM((link_rows, LANES), jnp.int32), pltpu.SemaphoreType.DMA((4,))],
        compiler_params=LIMIT,
    )(
        in_hbm(nearby_sectors),
        in_hbm(serving_slot),
        in_hbm(symbol_rows),
        arrived.reshape(row_total, LANES),
        other.reshape(row_total, LANES),
    )

    def exchange(first):
        pairs = [(n, n + 1) for n in range(first, devices - 1, 2)]
        return lax.ppermute(listed, "cell", pairs + [(m, n) for n, m in pairs])

    first_list, second_list = exchange(0), exchange(1)

    pair_total = link_total // 2
    response = pl.pallas_call(
        functools.partial(respond_kernel, portion=portion),
        out_shape=jax.ShapeDtypeStruct((pair_total, 4 * portion, LANES), jnp.float32),
        in_specs=[VMEM, VMEM],
        out_specs=VMEM,
        scratch_shapes=[
            pltpu.SMEM((link_rows, LANES), jnp.int32),
            pltpu.VMEM((2, pair_total, LANES), jnp.int32),
            pltpu.SemaphoreType.DMA((1,)),
        ]
        + response_scratch(pair_total, portion),
        cost_estimate=pl.CostEstimate(
            flops=pair_total * 2 * 128 * 128 * 256 * 40,
            bytes_accessed=pair_total * 4 * portion * LANES * 2,
            transcendentals=0,
        ),
        compiler_params=LIMIT,
    )(rows, table)

    partial_value = pl.pallas_call(
        functools.partial(receive_kernel, portion=portion),
        out_shape=jax.ShapeDtypeStruct((2 * total_users, LANES), jnp.float32),
        in_specs=[ANY] * 3 + [VMEM] * 3,
        out_specs=VMEM,
        scratch_shapes=small_scratch
        + [
            pltpu.SMEM((2, LANES), jnp.int32),
            pltpu.SemaphoreType.DMA((5,)),
            pltpu.VMEM((2, total_users, LANES), jnp.int32),
            pltpu.VMEM((2, 3 * total_users, LANES), jnp.float32),
            pltpu.VMEM((CELL_SECTORS + 2 * REACH + 1, 2 * portion, LANES), jnp.float32),
        ]
        + response_scratch(total_users, portion),
        compiler_params=LIMIT,
    )(nearby_sectors, serving_slot, symbol_rows, response, first_list, second_list)
    summed = partial_value + lax.ppermute(partial_value, "grp", swap)
    return summed.reshape(total_users, 2, FRAME_TONES)


def solution(mesh):
    placed = (
        P("cell"),
        P("cell"),
        P(None, "cell"),
        P("cell"),
        P("cell"),
        P("cell"),
        P(None, "cell"),
        P("cell"),
        P("cell", None, None),
    )
    return jax.shard_map(
        shards, mesh=mesh, in_specs=placed, out_specs=P("cell", None, None), check_vma=False
    )
```

```python
import functools
import math

import jax
import jax.numpy as jnp
from jax import lax
from jax.experimental import pallas as pl
from jax.experimental.pallas import tpu as pltpu
from jax.sharding import PartitionSpec as P

SECTOR_ANTENNAS = 64
FRAME_TONES = 128
PMAX = 64
NEARBY_COUNT = 8
CELL_SECTORS = 32
REACH = 16
EPSILON = 1e-06

LANES = 128
GROUP = 8
HALF = FRAME_TONES // 2
SPANS = HALF // (2 * GROUP)
LEVELS = 32767.0
TAG_LANE = LANES - PMAX // 2
UNROLL = 32
DELAY_STEP = 64.0 / 65535.0
SYMBOL_TOP = 4.0

SIN_TERMS = tuple((-1.0) ** n / math.factorial(2 * n + 1) for n in range(6))
COS_TERMS = tuple((-1.0) ** n / math.factorial(2 * n) for n in range(8))


def polynomial(terms, square):
    total = terms[-1]
    for term in terms[-2::-1]:
        total = total * square + term
    return total


def quarter_cos_sin(x):
    square = x * x
    return polynomial(COS_TERMS, square), x * polynomial(SIN_TERMS, square)


def cos_sin_turns(turns):
    turns = turns - jnp.round(turns)
    c, s = quarter_cos_sin(math.pi * turns)
    return 1.0 - 2.0 * s * s, 2.0 * s * c


def times(x, y):
    return x[0] * y[0] - x[1] * y[1], x[0] * y[1] + x[1] * y[0]


def powers(base, count):
    found = {1: base}
    for n in range(2, count + 1):
        found[n] = times(found[n // 2], found[n - n // 2])
    return found


def join(high, low):
    return (high.astype(jnp.int32) << 16) | (low.astype(jnp.int32) & 0xFFFF)


def split(word):
    return (word >> 16).astype(jnp.float32), ((word << 16) >> 16).astype(jnp.float32)


def root_code(value):
    root = jnp.sqrt(jnp.sqrt(jnp.sqrt(jnp.abs(value)))) * LEVELS
    return jnp.round(jnp.where(value < 0, -root, root))


def root_value(code):
    unit = code * (1.0 / LEVELS)
    power = unit * unit
    power = power * power
    power = power * power
    return jnp.where(code < 0, -power, power)


def lane_index(rows):
    return lax.broadcasted_iota(jnp.int32, (rows, LANES), 1)


def fetch(pairs, sems):
    copies = [pltpu.make_async_copy(a, b, sems.at[n]) for n, (a, b) in enumerate(pairs)]
    for copy in copies:
        copy.start()
    return copies


def pack_kernel(
    link_hbm, count_hbm, offset_hbm, delay_hbm, angle_hbm, gain_hbm, out_ref,
    link_ref, count_ref, offset_ref, delay_ref, angle_ref, real_ref, imag_ref, word_ref, sems,
    *, link_total, capacity, stride,
):
    copies = fetch(
        [
            (link_hbm, link_ref),
            (count_hbm, count_ref),
            (offset_hbm, offset_ref),
            (delay_hbm, delay_ref),
            (angle_hbm, angle_ref),
            (gain_hbm.at[:, 0, :], real_ref),
            (gain_hbm.at[:, 1, :], imag_ref),
        ],
        sems,
    )
    lane = lane_index(1)
    out_ref[...] = jnp.zeros_like(out_ref)
    for copy in copies:
        copy.wait()
    rows = delay_ref.shape[0]
    lower = lax.axis_index("grp") == 0
    c, s = quarter_cos_sin(angle_ref[...] * 0.5)
    gain_re, gain_im = real_ref[...], imag_ref[...]
    sine = 2.0 * s * c
    code = jnp.round(LEVELS * sine)
    turn = (sine - code * (1.0 / LEVELS)) * (0.5 * math.pi * (SECTOR_ANTENNAS - 1))
    gain_re, gain_im = gain_re + gain_im * turn, gain_im - gain_re * turn
    high = jnp.where(lower, jnp.round(delay_ref[...] * (1.0 / DELAY_STEP)) - 32768.0, root_code(gain_re))
    low = jnp.where(lower, code, root_code(gain_im))
    word_ref[:rows, :] = join(high, low)
    link_bits = link_total.bit_length() - 1
    owners = out_ref.shape[0] // stride
    tag_rows = max(owners, GROUP)
    column = lane_index(tag_rows)
    tag_place = lax.broadcasted_iota(jnp.int32, (tag_rows, LANES), 0) * (2 * stride) + column - TAG_LANE
    tag_place = jnp.where(column >= TAG_LANE, tag_place, -1)

    def step(slot, carry):
        last_owner, free, taken, tags = carry
        link = link_ref[slot]
        count = count_ref[slot]
        owner = link >> link_bits
        fresh = owner != last_owner
        first = owner * (2 * stride)
        free = jnp.where(fresh, first, free)
        taken = jnp.where(fresh, 0, taken)
        short = jnp.where(count <= PMAX // 2, 1 - taken, 0)
        place = jnp.where(short == 1, first + (capacity - 1), free)
        offset = offset_ref[slot]
        row = offset >> 7
        shift = offset & (LANES - 1)
        word = jnp.where(lane >= shift, word_ref[pl.ds(row, 1), :], word_ref[pl.ds(row + 1, 1), :])
        start = (place & 1) << 6
        word = pltpu.roll(word, (start - shift) & (LANES - 1), 1)
        within = lane - start
        live = (within >= 0) & (within < count)
        pltpu.store(out_ref.at[pl.ds(place >> 1, 1), :], word, mask=live)
        tags = jnp.where(tag_place == place, link, tags)
        return owner, free + 1 - short, taken + short, tags

    empty = jnp.full((tag_rows, LANES), -1, jnp.int32)
    zero = jnp.int32(0)
    tags = lax.fori_loop(0, link_total, step, (jnp.int32(-1), zero, zero, empty), unroll=UNROLL)[3]
    last = pl.ds(capacity // 2 - 1, owners, stride=stride)
    out_ref[last, :] = jnp.where(lane >= TAG_LANE, tags[:owners], out_ref[last, :])


def find_rows(own_ref, table_ref, capacity, stride):
    total_rows = own_ref.shape[0]
    senders = total_rows // stride
    tags = own_ref[pl.ds(capacity // 2 - 1, senders, stride=stride), :]
    tags = (tags - lax.axis_index("cell") * (table_ref.shape[0] * LANES)).astype(jnp.float32).T
    depth = pl.cdiv(capacity, GROUP) * GROUP
    tags = tags[TAG_LANE : TAG_LANE + depth]
    place = lax.broadcasted_iota(jnp.int32, (depth, LANES), 0)
    inside = place < capacity
    lane = lane_index(depth)
    value = ((place >> 1) + total_rows * ((place ^ lane) & 1)).astype(jnp.float32)
    lane = lane.astype(jnp.float32)
    rows = table_ref.shape[0]
    totals = [jnp.zeros((depth, LANES), jnp.float32) for _ in range(rows)]
    for sender in range(senders):
        column = jnp.broadcast_to(tags[:, sender : sender + 1], (depth, LANES))
        column = jnp.where(inside, column, -1.0)
        here = value + float(sender * stride)
        for n in range(rows):
            totals[n] += jnp.where(column == lane + float(n * LANES), here, 0.0)
    for n in range(rows):
        table_ref[n : n + 1, :] = jnp.sum(totals[n], axis=0, keepdims=True).astype(jnp.int32)


def sort_kernel(
    nearby_hbm, slot_hbm, symbol_hbm, own_ref, other_ref, rows_ref, table_ref, list_ref,
    nearby_ref, slot_ref, symbol_ref, place_ref, sems, *, capacity, stride,
):
    copies = fetch(
        [(nearby_hbm, nearby_ref), (slot_hbm, slot_ref), (symbol_hbm, symbol_ref)], sems
    )
    find_rows(own_ref, table_ref, capacity, stride)
    copies += fetch([(table_ref, place_ref)], sems.at[pl.ds(3, 1)])
    total_rows = own_ref.shape[0]
    lower = lax.axis_index("grp") == 0
    own, other = own_ref[...], other_ref[...]
    for n, words in enumerate((jnp.where(lower, own, other), jnp.where(lower, other, own))):
        rows_ref[n, :total_rows, :] = words
        rows_ref[n, total_rows:, :] = pltpu.roll(words, PMAX, 1)
        senders = total_rows // stride
        for m, at in enumerate((TAG_LANE, TAG_LANE - PMAX)):
            last = pl.ds(m * total_rows + capacity // 2 - 1, senders, stride=stride)
            kept = (lane_index(senders) < at) | (lane_index(senders) >= at + PMAX // 2)
            rows_ref[n, last, :] = jnp.where(kept, rows_ref[n, last, :], 0)
    for copy in copies:
        copy.wait()
    users = slot_ref.shape[0]
    pairs = users // 2
    left = lane_index(1) < PMAX
    lane = lane_index(1)
    sectors = jnp.zeros((1, LANES), jnp.int32)
    first_sector = lax.axis_index("cell") * CELL_SECTORS
    for pair in range(pairs):
        found = []
        for user in (2 * pair, 2 * pair + 1):
            slot = slot_ref[user]
            link = user * NEARBY_COUNT + slot
            row = place_ref[user * NEARBY_COUNT // LANES, link & (LANES - 1)]
            turned = jnp.where(row < total_rows, row + total_rows, row - total_rows)
            found.append(jnp.where(((slot ^ user) & 1) == 0, row, turned))
            sectors = jnp.where(lane == user, nearby_ref[slot, user] - first_sector, sectors)
        for n in range(2):
            even = rows_ref[n, pl.ds(found[0], 1), :]
            odd = rows_ref[n, pl.ds(found[1], 1), :]
            list_ref[n * pairs + pair : n * pairs + pair + 1, :] = jnp.where(left, even, odd)
    symbols = symbol_ref[...].astype(jnp.float32) * (1.0 / SYMBOL_TOP)
    code_ref = list_ref.at[2 * pairs : 2 * pairs + users, :]
    codes = root_code(symbols).reshape(users, 2, LANES)
    code_ref[...] = join(codes[:, 0, :], codes[:, 1, :])
    base = 2 * pairs + users
    list_ref[base : base + GROUP, :] = jnp.broadcast_to(sectors, (GROUP, LANES))


def make_tables(words_ref, groups, first_antenna, tables):
    fine, centre, last, near, far = tables
    steps = far.shape[1] // last.shape[1]
    for group in groups:
        rows = pl.ds(group * GROUP, GROUP)
        delay, sine = split(words_ref[0, rows, :])
        delay = (delay + 32768.0) * DELAY_STEP
        sine = sine * (1.0 / LEVELS)
        gain_re, gain_im = (root_value(code) for code in split(words_ref[1, rows, :]))

        def put(ref, n, count, value):
            at = pl.ds(group * (GROUP * count) + n, GROUP, stride=count) if count > 1 else rows
            ref[0, at, :] = value[0]
            ref[1, at, :] = value[1]

        def half_steps(half):
            whole = times(half, half)
            up = powers(whole, GROUP - 1)
            return whole, [half] + [times(half, up[n]) for n in range(1, GROUP)]

        c, s = quarter_cos_sin(delay * (math.pi / FRAME_TONES))
        whole, found = half_steps((c, -s))
        for n in range(GROUP):
            put(fine, n, GROUP, found[n])
        top = found[GROUP - 1]
        wide = times(times(top, top), whole)
        value = top
        for n in range(SPANS):
            if n:
                value = times(value, wide)
            put(centre, n, SPANS, value)
        put(last, 0, 1, times(value, times(top, whole)))

        c, s = cos_sin_turns(sine * 0.25)
        whole, found = half_steps((c, -s))
        for n in range(GROUP):
            put(near, n, GROUP, found[n])
        top = found[GROUP - 1]
        wide = times(times(top, top), whole)
        c, s = cos_sin_turns(sine * (0.5 * first_antenna))
        value = times(times((gain_re, gain_im), (c, -s)), top)
        for n in range(steps):
            if n:
                value = times(value, wide)
            put(far, n, steps, value)


def both_sides(centre, fine):
    a, b = centre[0] * fine[0], centre[1] * fine[1]
    c, d = centre[0] * fine[1], centre[1] * fine[0]
    return (a - b, c + d), (a + b, d - c)


def sides_of(centre_ref, fine_ref, pair, spans):
    at = pl.ds(pl.multiple_of(pair * GROUP, GROUP), GROUP)
    fine = (fine_ref[0, at, :], fine_ref[1, at, :])
    found = []
    for n in range(spans):
        row = pl.ds(pair * spans + n, 1)
        found.extend(both_sides((centre_ref[0, row, :], centre_ref[1, row, :]), fine))
    return found


def stack(values, part):
    return jnp.concatenate([v[part] for v in values], axis=0).astype(jnp.bfloat16)


def build_operands(pair, tables, tone_ref, mix_ref):
    fine, centre, last, near, far = tables
    delay = sides_of(centre, fine, pair, SPANS)
    row = pl.ds(pair, 1)
    final = lax.broadcasted_iota(jnp.int32, (GROUP, LANES), 0) == GROUP - 1
    steps = far.shape[1] // last.shape[1]
    spread = sides_of(far, near, pair, steps)
    portion = mix_ref.shape[0] // 2
    for n in range(2):
        tone_ref[n * HALF : (n + 1) * HALF, :] = stack(delay, n)
        swapped = jnp.where(final, last[n, row, :], delay[1][n])
        head = jnp.concatenate([delay[0][n], swapped], axis=0).astype(jnp.bfloat16)
        at = 2 * HALF + 2 * GROUP * n
        tone_ref[at : at + 2 * GROUP, :] = head
        mix_ref[n * portion : (n + 1) * portion, :] = stack(spread, n)


def multiply_operands(tone_ref, mix_ref):
    re, im = tone_ref[:HALF, :], tone_ref[HALF : 2 * HALF, :]
    head = [tone_ref[2 * HALF + 2 * GROUP * n : 2 * HALF + 2 * GROUP * (n + 1), :] for n in range(2)]
    low_re = jnp.concatenate([head[0], re[2 * GROUP :]], axis=0)
    low_im = jnp.concatenate([head[1], im[2 * GROUP :]], axis=0)
    tones = jnp.concatenate(
        [jnp.concatenate([re, -im], axis=1), jnp.concatenate([low_re, low_im], axis=1)], axis=0
    )
    portion = mix_ref.shape[0] // 2
    spread_re, spread_im = mix_ref[:portion, :], mix_ref[portion:, :]
    lane = lane_index(1)
    blocks = []
    for keep in (lane < PMAX, lane >= PMAX):
        keep = jnp.where(keep, 1.0, 0.0).astype(jnp.bfloat16)
        a, b, c = spread_re * keep, spread_im * keep, spread_re * -keep
        blocks.append(jnp.concatenate([a, b], axis=1))
        blocks.append(jnp.concatenate([b, c], axis=1))
    return lax.dot_general(
        jnp.concatenate(blocks, axis=0),
        tones,
        (((1,), (1,)), ((), ())),
        preferred_element_type=jnp.float32,
    )


def all_responses(pairs, tables, buffers, emit):
    tone_a, mix_a, tone_b, mix_b = buffers
    block = tone_a.shape[0]
    blocks = pairs // block
    once = jnp.minimum(lax.axis_index("cell") + 1, 1)

    def build(index, tone_ref, mix_ref):
        for n in range(block):
            build_operands(index * block + n, tables, tone_ref.at[n], mix_ref.at[n])

    def multiply(index, tone_ref, mix_ref):
        for n in range(block):
            emit(index * block + n, multiply_operands(tone_ref.at[n], mix_ref.at[n]))

    def stage(index, now, later):
        def body(_, carry):
            if now is not None:
                multiply(index, *now)
            if later is not None:
                build(index + 1, *later)
            return carry

        lax.fori_loop(0, once, body, 0)

    first, second = (tone_a, mix_a), (tone_b, mix_b)
    stage(-1, None, first)

    def step(n, carry):
        stage(2 * n, first, second)
        stage(2 * n + 1, second, first)
        return carry

    lax.fori_loop(0, blocks // 2 - 1, step, 0)
    stage(blocks - 2, first, second)
    stage(blocks - 1, second, None)


def tone_of_place(lane):
    place = lane & (HALF - 1)
    within = place & 15
    above = (place & ~15) + jnp.where(within < GROUP, within + GROUP, 15 - within)
    below = jnp.where(above == 0, HALF, above)
    return HALF + jnp.where(lane < HALF, above, -below)


def place_of_tone(lane):
    away = jnp.where(lane >= HALF, lane - HALF, (HALF - lane) & (HALF - 1))
    within = away & 15
    place = (away & ~15) + jnp.where(within >= GROUP, within - GROUP, 15 - within)
    return jnp.where(lane >= HALF, place, HALF + place)


def reorder(values, index):
    pieces = [
        jnp.take_along_axis(values[n : n + GROUP], index, axis=1)
        for n in range(0, values.shape[0], GROUP)
    ]
    return jnp.concatenate(pieces, axis=0)


def respond_kernel(rows_ref, table_ref, out_ref, place_ref, words, sem, *scratch, portion):
    tables, buffers = scratch[:5], scratch[5:]
    for copy in fetch([(table_ref, place_ref)], sem):
        copy.wait()
    pairs = out_ref.shape[0]
    left = lane_index(1) < PMAX
    chunk = 16

    def take(index, carry):
        first = index * (2 * chunk)
        row = first >> 7
        base = first & (LANES - 1)
        for n in range(chunk):
            even = place_ref[row, base + 2 * n]
            odd = place_ref[row, base + 2 * n + 1]
            for field in range(2):
                value = jnp.where(
                    left, rows_ref[field, pl.ds(even, 1), :], rows_ref[field, pl.ds(odd, 1), :]
                )
                words[field, pl.ds(index * chunk + n, 1), :] = value
        return carry

    lax.fori_loop(0, pairs // chunk, take, 0)
    first_antenna = (lax.axis_index("grp") * portion).astype(jnp.float32)
    batch = 4

    def tabulate(index, carry):
        make_tables(words, [index * batch + n for n in range(batch)], first_antenna, tables)
        return carry

    lax.fori_loop(0, pairs // (GROUP * batch), tabulate, 0)

    def emit(pair, response):
        out_ref[pair] = response

    all_responses(pairs, tables, buffers, emit)


def receive_kernel(
    nearby_hbm, slot_hbm, symbol_hbm, response_ref, first_ref, second_ref, out_ref,
    nearby_ref, slot_ref, symbol_ref, sector_ref, sems, words, symbols, remote, *scratch, portion,
):
    tables, buffers = scratch[:5], scratch[5:]
    users = nearby_hbm.shape[1]
    pairs = users // 2
    base = 2 * pairs + users
    copies = fetch(
        [
            (nearby_hbm, nearby_ref),
            (slot_hbm, slot_ref),
            (symbol_hbm, symbol_ref),
            (first_ref.at[base : base + 1, :], sector_ref.at[0:1, :]),
            (second_ref.at[base : base + 1, :], sector_ref.at[1:2, :]),
        ],
        sems,
    )
    remote[...] = jnp.zeros_like(remote)
    order = tone_of_place(lane_index(GROUP))
    for n, ref in enumerate((first_ref, second_ref)):
        for field in range(2):
            words[field, n * pairs : (n + 1) * pairs, :] = ref[field * pairs : (field + 1) * pairs, :]
        codes = split(ref[2 * pairs : 2 * pairs + users, :])
        for part in range(2):
            symbols[part, n * users : (n + 1) * users, :] = reorder(
                root_value(codes[part]) * SYMBOL_TOP, order
            )
    first_antenna = (lax.axis_index("grp") * portion).astype(jnp.float32)
    make_tables(words, list(range(2 * pairs // GROUP)), first_antenna, tables)
    for copy in copies:
        copy.wait()
    own = reorder(symbol_ref[...].astype(jnp.float32), order).reshape(users, 2, LANES)
    for part in range(2):
        symbols[part, 2 * users :, :] = own[:, part, :]

    def contribute(place, row, re, im):
        sym_re = symbols[0, pl.ds(row, 1), :]
        sym_im = symbols[1, pl.ds(row, 1), :]
        remote[place, :portion, :] += re * sym_re + im * sym_im
        remote[place, portion:, :] += re * sym_im - im * sym_re

    window = CELL_SECTORS + 2 * REACH
    here = lax.axis_index("cell")
    first_sector = here * CELL_SECTORS - REACH

    def own_user(user, carry):
        slot = slot_ref[user]
        pair = user * (NEARBY_COUNT // 2) + (slot >> 1)
        at = pl.multiple_of((slot & 1) * (2 * portion), 2 * portion)
        re = response_ref[pair, pl.ds(at, portion), :]
        im = response_ref[pair, pl.ds(at + portion, portion), :]
        contribute(nearby_ref[slot, user] - first_sector, 2 * users + user, re, im)
        return carry

    lax.fori_loop(0, users, own_user, 0, unroll=8)
    after_first = (here & 1) == 0

    def emit(pair, response):
        for n in range(2):
            row = pair * 2 + n
            second = row >= users
            user = jnp.where(second, row - users, row)
            sector = sector_ref[jnp.where(second, 1, 0), user]
            place = jnp.where(second != after_first, sector + CELL_SECTORS, sector - CELL_SECTORS) + REACH
            place = jnp.where((place >= 0) & (place < window), place, window)
            re = response[2 * n * portion : (2 * n + 1) * portion]
            im = response[(2 * n + 1) * portion : (2 * n + 2) * portion]
            contribute(place, row, re, im)

    all_responses(2 * pairs, tables, buffers, emit)

    def normalise(sector, carry):
        value = remote[sector]
        re, im = value[:portion], value[portion:]
        power = jnp.sum(re * re + im * im, axis=1, keepdims=True) * (1.0 / FRAME_TONES)
        scale = lax.rsqrt(power + EPSILON)
        remote[sector, :portion, :] = (re * scale).astype(jnp.bfloat16).astype(jnp.float32)
        remote[sector, portion:, :] = (im * scale).astype(jnp.bfloat16).astype(jnp.float32)
        return carry

    lax.fori_loop(0, window, normalise, 0, unroll=8)

    def one_user(user, carry):
        total_re = jnp.zeros((GROUP, LANES), jnp.float32)
        total_im = jnp.zeros((GROUP, LANES), jnp.float32)
        for k in range(NEARBY_COUNT):
            sector = nearby_ref[k, user] - first_sector
            pair = user * (NEARBY_COUNT // 2) + k // 2
            at = (k % 2) * 2 * portion
            for n in range(0, portion, GROUP):
                re = response_ref[pair, at + n : at + n + GROUP, :]
                im = response_ref[pair, at + portion + n : at + portion + n + GROUP, :]
                other_re = remote[sector, n : n + GROUP, :]
                other_im = remote[sector, portion + n : portion + n + GROUP, :]
                total_re = total_re + (re * other_re - im * other_im)
                total_im = total_im + (re * other_im + im * other_re)
        scale = 1.0 / math.sqrt(SECTOR_ANTENNAS)
        out_ref[pl.ds(user * 2, 1), :] = jnp.sum(total_re, axis=0, keepdims=True) * scale
        out_ref[pl.ds(user * 2 + 1, 1), :] = jnp.sum(total_im, axis=0, keepdims=True) * scale
        return carry

    lax.fori_loop(0, users, one_user, 0, unroll=4)
    out_ref[...] = reorder(out_ref[...], place_of_tone(lane_index(GROUP)))


VMEM = pl.BlockSpec(memory_space=pltpu.VMEM)
HBM = pl.BlockSpec(memory_space=pltpu.HBM)
ANY = pl.BlockSpec(memory_space=pl.ANY)
LIMIT = pltpu.CompilerParams(vmem_limit_bytes=16 << 20)
BLOCK = 8


def in_hbm(values):
    return pltpu.with_memory_space_constraint(values, pltpu.HBM)


def response_scratch(pairs, portion):
    counts = (GROUP, SPANS, 1, GROUP, portion // (2 * GROUP))
    tables = [pltpu.VMEM((2, pairs * n, LANES), jnp.float32) for n in counts]
    factors = [
        pltpu.VMEM((BLOCK, 2 * HALF + 4 * GROUP, LANES), jnp.bfloat16),
        pltpu.VMEM((BLOCK, 2 * portion, LANES), jnp.bfloat16),
    ]
    return tables + factors + factors


def shards(
    path_delay,
    path_angle,
    path_gain,
    slot_counts,
    slot_offsets,
    ray_link,
    nearby_sectors,
    serving_slot,
    symbols,
):
    devices = lax.axis_size("cell")
    worker_count = lax.axis_size("grp")
    path_total = path_delay.shape[0]
    link_total = slot_counts.shape[0]
    total_users = serving_slot.shape[0]
    capacity = 2 * link_total // devices
    stride = pl.cdiv(capacity // 2, GROUP) * GROUP
    portion = SECTOR_ANTENNAS // worker_count
    swap = [(n, worker_count - 1 - n) for n in range(worker_count)]
    path_rows = path_total // LANES
    link_rows = link_total // LANES
    sizes = dict(capacity=capacity, stride=stride)

    packed = pl.pallas_call(
        functools.partial(pack_kernel, link_total=link_total, **sizes),
        out_shape=jax.ShapeDtypeStruct((devices * stride, LANES), jnp.int32),
        in_specs=[HBM] * 6,
        out_specs=VMEM,
        scratch_shapes=[pltpu.SMEM((link_total,), jnp.int32)] * 3
        + [
            pltpu.VMEM((path_rows, LANES), jnp.float32),
            pltpu.VMEM((path_rows, LANES), jnp.float32),
            pltpu.VMEM((path_rows, LANES), jnp.float32),
            pltpu.VMEM((path_rows, LANES), jnp.float32),
            pltpu.VMEM((pl.cdiv(path_rows + 1, GROUP) * GROUP, LANES), jnp.int32),
            pltpu.SemaphoreType.DMA((7,)),
        ],
        compiler_params=LIMIT,
    )(
        in_hbm(ray_link),
        in_hbm(slot_counts),
        in_hbm(slot_offsets),
        in_hbm(path_delay.reshape(path_rows, LANES)),
        in_hbm(path_angle.reshape(path_rows, LANES)),
        in_hbm(path_gain.reshape(2, path_rows, LANES).transpose(1, 0, 2)),
    )
    arrived = lax.all_to_all(
        packed.reshape(devices, stride, LANES), "cell", split_axis=0, concat_axis=0, tiled=True
    )
    other = lax.ppermute(arrived, "grp", swap)

    row_total = devices * stride
    list_rows = 2 * total_users + GROUP
    symbol_rows = symbols.reshape(2 * total_users, LANES)
    small_scratch = [
        pltpu.SMEM(nearby_sectors.shape, jnp.int32),
        pltpu.SMEM((total_users,), jnp.int32),
        pltpu.VMEM((2 * total_users, LANES), jnp.bfloat16),
    ]
    rows, table, listed = pl.pallas_call(
        functools.partial(sort_kernel, **sizes),
        out_shape=(
            jax.ShapeDtypeStruct((2, 2 * row_total, LANES), jnp.int32),
            jax.ShapeDtypeStruct((link_rows, LANES), jnp.int32),
            jax.ShapeDtypeStruct((list_rows, LANES), jnp.int32),
        ),
        in_specs=[HBM] * 3 + [VMEM] * 2,
        out_specs=(VMEM, VMEM, VMEM),
        scratch_shapes=small_scratch
        + [pltpu.SMEM((link_rows, LANES), jnp.int32), pltpu.SemaphoreType.DMA((4,))],
        compiler_params=LIMIT,
    )(
        in_hbm(nearby_sectors),
        in_hbm(serving_slot),
        in_hbm(symbol_rows),
        arrived.reshape(row_total, LANES),
        other.reshape(row_total, LANES),
    )

    def exchange(first):
        pairs = [(n, n + 1) for n in range(first, devices - 1, 2)]
        return lax.ppermute(listed, "cell", pairs + [(m, n) for n, m in pairs])

    first_list, second_list = exchange(0), exchange(1)

    pair_total = link_total // 2
    response = pl.pallas_call(
        functools.partial(respond_kernel, portion=portion),
        out_shape=jax.ShapeDtypeStruct((pair_total, 4 * portion, LANES), jnp.float32),
        in_specs=[VMEM, VMEM],
        out_specs=VMEM,
        scratch_shapes=[
            pltpu.SMEM((link_rows, LANES), jnp.int32),
            pltpu.VMEM((2, pair_total, LANES), jnp.int32),
            pltpu.SemaphoreType.DMA((1,)),
        ]
        + response_scratch(pair_total, portion),
        cost_estimate=pl.CostEstimate(
            flops=pair_total * 2 * 128 * 128 * 256 * 40,
            bytes_accessed=pair_total * 4 * portion * LANES * 2,
            transcendentals=0,
        ),
        compiler_params=LIMIT,
    )(rows, table)

    partial_value = pl.pallas_call(
        functools.partial(receive_kernel, portion=portion),
        out_shape=jax.ShapeDtypeStruct((2 * total_users, LANES), jnp.float32),
        in_specs=[ANY] * 3 + [VMEM] * 3,
        out_specs=VMEM,
        scratch_shapes=small_scratch
        + [
            pltpu.SMEM((2, LANES), jnp.int32),
            pltpu.SemaphoreType.DMA((5,)),
            pltpu.VMEM((2, total_users, LANES), jnp.int32),
            pltpu.VMEM((2, 3 * total_users, LANES), jnp.float32),
            pltpu.VMEM((CELL_SECTORS + 2 * REACH + 1, 2 * portion, LANES), jnp.float32),
        ]
        + response_scratch(total_users, portion),
        compiler_params=LIMIT,
    )(nearby_sectors, serving_slot, symbol_rows, response, first_list, second_list)
    summed = partial_value + lax.ppermute(partial_value, "grp", swap)
    return summed.reshape(total_users, 2, FRAME_TONES)


def solution(mesh):
    placed = (
        P("cell"),
        P("cell"),
        P(None, "cell"),
        P("cell"),
        P("cell"),
        P("cell"),
        P(None, "cell"),
        P("cell"),
        P("cell", None, None),
    )
    return jax.shard_map(
        shards, mesh=mesh, in_specs=placed, out_specs=P("cell", None, None), check_vma=False
    )
```

```python
import functools
import math

import jax
import jax.numpy as jnp
from jax import lax
from jax.experimental import pallas as pl
from jax.experimental.pallas import tpu as pltpu
from jax.sharding import PartitionSpec as P

SECTOR_ANTENNAS = 64
FRAME_TONES = 128
PMAX = 64
NEARBY_COUNT = 8
CELL_SECTORS = 32
REACH = 16
EPSILON = 1e-06

LANES = 128
GROUP = 8
HALF = FRAME_TONES // 2
SPANS = HALF // (2 * GROUP)
LEVELS = 32767.0
TAG_LANE = LANES - PMAX // 2
UNROLL = 32
DELAY_STEP = 64.0 / 65535.0
SYMBOL_TOP = 4.0

SIN_TERMS = tuple((-1.0) ** n / math.factorial(2 * n + 1) for n in range(6))
COS_TERMS = tuple((-1.0) ** n / math.factorial(2 * n) for n in range(8))


def polynomial(terms, square):
    total = terms[-1]
    for term in terms[-2::-1]:
        total = total * square + term
    return total


def quarter_cos_sin(x):
    square = x * x
    return polynomial(COS_TERMS, square), x * polynomial(SIN_TERMS, square)


def cos_sin_turns(turns):
    turns = turns - jnp.round(turns)
    c, s = quarter_cos_sin(math.pi * turns)
    return 1.0 - 2.0 * s * s, 2.0 * s * c


def times(x, y):
    return x[0] * y[0] - x[1] * y[1], x[0] * y[1] + x[1] * y[0]


def powers(base, count):
    found = {1: base}
    for n in range(2, count + 1):
        found[n] = times(found[n // 2], found[n - n // 2])
    return found


def join(high, low):
    return (high.astype(jnp.int32) << 16) | (low.astype(jnp.int32) & 0xFFFF)


def split(word):
    return (word >> 16).astype(jnp.float32), ((word << 16) >> 16).astype(jnp.float32)


def root_code(value):
    root = jnp.sqrt(jnp.sqrt(jnp.sqrt(jnp.abs(value)))) * LEVELS
    return jnp.round(jnp.where(value < 0, -root, root))


def root_value(code):
    unit = code * (1.0 / LEVELS)
    power = unit * unit
    power = power * power
    power = power * power
    return jnp.where(code < 0, -power, power)


def lane_index(rows):
    return lax.broadcasted_iota(jnp.int32, (rows, LANES), 1)


def fetch(pairs, sems):
    copies = [pltpu.make_async_copy(a, b, sems.at[n]) for n, (a, b) in enumerate(pairs)]
    for copy in copies:
        copy.start()
    return copies


def pack_kernel(
    link_hbm, count_hbm, offset_hbm, delay_hbm, angle_hbm, gain_hbm, out_ref,
    link_ref, count_ref, offset_ref, delay_ref, angle_ref, real_ref, imag_ref, word_ref, sems,
    *, link_total, capacity, stride,
):
    copies = fetch(
        [
            (link_hbm, link_ref),
            (count_hbm, count_ref),
            (offset_hbm, offset_ref),
            (delay_hbm, delay_ref),
            (angle_hbm, angle_ref),
            (gain_hbm.at[:, 0, :], real_ref),
            (gain_hbm.at[:, 1, :], imag_ref),
        ],
        sems,
    )
    lane = lane_index(1)
    out_ref[...] = jnp.zeros_like(out_ref)
    for copy in copies:
        copy.wait()
    rows = delay_ref.shape[0]
    lower = lax.axis_index("grp") == 0
    c, s = quarter_cos_sin(angle_ref[...] * 0.5)
    gain_re, gain_im = real_ref[...], imag_ref[...]
    sine = 2.0 * s * c
    code = jnp.round(LEVELS * sine)
    turn = (sine - code * (1.0 / LEVELS)) * (0.5 * math.pi * (SECTOR_ANTENNAS - 1))
    gain_re, gain_im = gain_re + gain_im * turn, gain_im - gain_re * turn
    high = jnp.where(lower, jnp.round(delay_ref[...] * (1.0 / DELAY_STEP)) - 32768.0, root_code(gain_re))
    low = jnp.where(lower, code, root_code(gain_im))
    word_ref[:rows, :] = join(high, low)
    link_bits = link_total.bit_length() - 1
    owners = out_ref.shape[0] // stride
    tag_rows = max(owners, GROUP)
    column = lane_index(tag_rows)
    tag_place = lax.broadcasted_iota(jnp.int32, (tag_rows, LANES), 0) * (2 * stride) + column - TAG_LANE
    tag_place = jnp.where(column >= TAG_LANE, tag_place, -1)

    def step(slot, carry):
        last_owner, free, taken, tags = carry
        link = link_ref[slot]
        count = count_ref[slot]
        owner = link >> link_bits
        fresh = owner != last_owner
        first = owner * (2 * stride)
        free = jnp.where(fresh, first, free)
        taken = jnp.where(fresh, 0, taken)
        short = jnp.where(count <= PMAX // 2, 1 - taken, 0)
        place = jnp.where(short == 1, first + (capacity - 1), free)
        offset = offset_ref[slot]
        row = offset >> 7
        shift = offset & (LANES - 1)
        word = jnp.where(lane >= shift, word_ref[pl.ds(row, 1), :], word_ref[pl.ds(row + 1, 1), :])
        start = (place & 1) << 6
        word = pltpu.roll(word, (start - shift) & (LANES - 1), 1)
        within = lane - start
        live = (within >= 0) & (within < count)
        pltpu.store(out_ref.at[pl.ds(place >> 1, 1), :], word, mask=live)
        tags = jnp.where(tag_place == place, link, tags)
        return owner, free + 1 - short, taken + short, tags

    empty = jnp.full((tag_rows, LANES), -1, jnp.int32)
    zero = jnp.int32(0)
    tags = lax.fori_loop(0, link_total, step, (jnp.int32(-1), zero, zero, empty), unroll=UNROLL)[3]
    last = pl.ds(capacity // 2 - 1, owners, stride=stride)
    out_ref[last, :] = jnp.where(lane >= TAG_LANE, tags[:owners], out_ref[last, :])


def find_rows(own_ref, table_ref, capacity, stride):
    total_rows = own_ref.shape[0]
    senders = total_rows // stride
    tags = own_ref[pl.ds(capacity // 2 - 1, senders, stride=stride), :]
    tags = (tags - lax.axis_index("cell") * (table_ref.shape[0] * LANES)).astype(jnp.float32).T
    depth = pl.cdiv(capacity, GROUP) * GROUP
    tags = tags[TAG_LANE : TAG_LANE + depth]
    place = lax.broadcasted_iota(jnp.int32, (depth, LANES), 0)
    inside = place < capacity
    lane = lane_index(depth)
    value = ((place >> 1) + total_rows * ((place ^ lane) & 1)).astype(jnp.float32)
    lane = lane.astype(jnp.float32)
    rows = table_ref.shape[0]
    totals = [jnp.zeros((depth, LANES), jnp.float32) for _ in range(rows)]
    for sender in range(senders):
        column = jnp.broadcast_to(tags[:, sender : sender + 1], (depth, LANES))
        column = jnp.where(inside, column, -1.0)
        here = value + float(sender * stride)
        for n in range(rows):
            totals[n] += jnp.where(column == lane + float(n * LANES), here, 0.0)
    for n in range(rows):
        table_ref[n : n + 1, :] = jnp.sum(totals[n], axis=0, keepdims=True).astype(jnp.int32)


def sort_kernel(
    nearby_hbm, slot_hbm, symbol_hbm, own_ref, other_ref, rows_ref, table_ref, list_ref,
    nearby_ref, slot_ref, symbol_ref, place_ref, sems, *, capacity, stride,
):
    copies = fetch(
        [(nearby_hbm, nearby_ref), (slot_hbm, slot_ref), (symbol_hbm, symbol_ref)], sems
    )
    find_rows(own_ref, table_ref, capacity, stride)
    copies += fetch([(table_ref, place_ref)], sems.at[pl.ds(3, 1)])
    total_rows = own_ref.shape[0]
    lower = lax.axis_index("grp") == 0
    own, other = own_ref[...], other_ref[...]
    for n, words in enumerate((jnp.where(lower, own, other), jnp.where(lower, other, own))):
        rows_ref[n, :total_rows, :] = words
        rows_ref[n, total_rows:, :] = pltpu.roll(words, PMAX, 1)
        senders = total_rows // stride
        for m, at in enumerate((TAG_LANE, TAG_LANE - PMAX)):
            last = pl.ds(m * total_rows + capacity // 2 - 1, senders, stride=stride)
            kept = (lane_index(senders) < at) | (lane_index(senders) >= at + PMAX // 2)
            rows_ref[n, last, :] = jnp.where(kept, rows_ref[n, last, :], 0)
    for copy in copies:
        copy.wait()
    users = slot_ref.shape[0]
    pairs = users // 2
    left = lane_index(1) < PMAX
    lane = lane_index(1)
    sectors = jnp.zeros((1, LANES), jnp.int32)
    first_sector = lax.axis_index("cell") * CELL_SECTORS
    for pair in range(pairs):
        found = []
        for user in (2 * pair, 2 * pair + 1):
            slot = slot_ref[user]
            link = user * NEARBY_COUNT + slot
            row = place_ref[user * NEARBY_COUNT // LANES, link & (LANES - 1)]
            turned = jnp.where(row < total_rows, row + total_rows, row - total_rows)
            found.append(jnp.where(((slot ^ user) & 1) == 0, row, turned))
            sectors = jnp.where(lane == user, nearby_ref[slot, user] - first_sector, sectors)
        for n in range(2):
            even = rows_ref[n, pl.ds(found[0], 1), :]
            odd = rows_ref[n, pl.ds(found[1], 1), :]
            list_ref[n * pairs + pair : n * pairs + pair + 1, :] = jnp.where(left, even, odd)
    symbols = symbol_ref[...].astype(jnp.float32) * (1.0 / SYMBOL_TOP)
    code_ref = list_ref.at[2 * pairs : 2 * pairs + users, :]
    codes = root_code(symbols).reshape(users, 2, LANES)
    code_ref[...] = join(codes[:, 0, :], codes[:, 1, :])
    base = 2 * pairs + users
    list_ref[base : base + GROUP, :] = jnp.broadcast_to(sectors, (GROUP, LANES))


def make_tables(words_ref, groups, first_antenna, tables):
    fine, centre, last, near, far = tables
    steps = far.shape[1] // last.shape[1]
    for group in groups:
        rows = pl.ds(group * GROUP, GROUP)
        delay, sine = split(words_ref[0, rows, :])
        delay = (delay + 32768.0) * DELAY_STEP
        sine = sine * (1.0 / LEVELS)
        gain_re, gain_im = (root_value(code) for code in split(words_ref[1, rows, :]))

        def put(ref, n, count, value):
            at = pl.ds(group * (GROUP * count) + n, GROUP, stride=count) if count > 1 else rows
            ref[0, at, :] = value[0]
            ref[1, at, :] = value[1]

        def half_steps(half):
            whole = times(half, half)
            up = powers(whole, GROUP - 1)
            return whole, [half] + [times(half, up[n]) for n in range(1, GROUP)]

        c, s = quarter_cos_sin(delay * (math.pi / FRAME_TONES))
        whole, found = half_steps((c, -s))
        for n in range(GROUP):
            put(fine, n, GROUP, found[n])
        top = found[GROUP - 1]
        wide = times(times(top, top), whole)
        value = top
        for n in range(SPANS):
            if n:
                value = times(value, wide)
            put(centre, n, SPANS, value)
        put(last, 0, 1, times(value, times(top, whole)))

        c, s = cos_sin_turns(sine * 0.25)
        whole, found = half_steps((c, -s))
        for n in range(GROUP):
            put(near, n, GROUP, found[n])
        top = found[GROUP - 1]
        wide = times(times(top, top), whole)
        c, s = cos_sin_turns(sine * (0.5 * first_antenna))
        value = times(times((gain_re, gain_im), (c, -s)), top)
        for n in range(steps):
            if n:
                value = times(value, wide)
            put(far, n, steps, value)


def both_sides(centre, fine):
    a, b = centre[0] * fine[0], centre[1] * fine[1]
    c, d = centre[0] * fine[1], centre[1] * fine[0]
    return (a - b, c + d), (a + b, d - c)


def sides_of(centre_ref, fine_ref, pair, spans):
    at = pl.ds(pl.multiple_of(pair * GROUP, GROUP), GROUP)
    fine = (fine_ref[0, at, :], fine_ref[1, at, :])
    found = []
    for n in range(spans):
        row = pl.ds(pair * spans + n, 1)
        found.extend(both_sides((centre_ref[0, row, :], centre_ref[1, row, :]), fine))
    return found


def stack(values, part):
    return jnp.concatenate([v[part] for v in values], axis=0).astype(jnp.bfloat16)


def build_operands(pair, tables, tone_ref, mix_ref):
    fine, centre, last, near, far = tables
    delay = sides_of(centre, fine, pair, SPANS)
    row = pl.ds(pair, 1)
    final = lax.broadcasted_iota(jnp.int32, (GROUP, LANES), 0) == GROUP - 1
    steps = far.shape[1] // last.shape[1]
    spread = sides_of(far, near, pair, steps)
    portion = mix_ref.shape[0] // 2
    for n in range(2):
        tone_ref[n * HALF : (n + 1) * HALF, :] = stack(delay, n)
        swapped = jnp.where(final, last[n, row, :], delay[1][n])
        head = jnp.concatenate([delay[0][n], swapped], axis=0).astype(jnp.bfloat16)
        at = 2 * HALF + 2 * GROUP * n
        tone_ref[at : at + 2 * GROUP, :] = head
        mix_ref[n * portion : (n + 1) * portion, :] = stack(spread, n)


def multiply_operands(tone_ref, mix_ref):
    re, im = tone_ref[:HALF, :], tone_ref[HALF : 2 * HALF, :]
    head = [tone_ref[2 * HALF + 2 * GROUP * n : 2 * HALF + 2 * GROUP * (n + 1), :] for n in range(2)]
    low_re = jnp.concatenate([head[0], re[2 * GROUP :]], axis=0)
    low_im = jnp.concatenate([head[1], im[2 * GROUP :]], axis=0)
    tones = jnp.concatenate(
        [jnp.concatenate([re, -im], axis=1), jnp.concatenate([low_re, low_im], axis=1)], axis=0
    )
    portion = mix_ref.shape[0] // 2
    spread_re, spread_im = mix_ref[:portion, :], mix_ref[portion:, :]
    lane = lane_index(1)
    blocks = []
    for keep in (lane < PMAX, lane >= PMAX):
        keep = jnp.where(keep, 1.0, 0.0).astype(jnp.bfloat16)
        a, b, c = spread_re * keep, spread_im * keep, spread_re * -keep
        blocks.append(jnp.concatenate([a, b], axis=1))
        blocks.append(jnp.concatenate([b, c], axis=1))
    return lax.dot_general(
        jnp.concatenate(blocks, axis=0),
        tones,
        (((1,), (1,)), ((), ())),
        preferred_element_type=jnp.float32,
    )


def all_responses(pairs, tables, buffers, emit):
    tone_a, mix_a, tone_b, mix_b = buffers
    block = tone_a.shape[0]
    blocks = pairs // block
    once = jnp.minimum(lax.axis_index("cell") + 1, 1)

    def build(index, tone_ref, mix_ref):
        for n in range(block):
            build_operands(index * block + n, tables, tone_ref.at[n], mix_ref.at[n])

    def multiply(index, tone_ref, mix_ref):
        for n in range(block):
            emit(index * block + n, multiply_operands(tone_ref.at[n], mix_ref.at[n]))

    def stage(index, now, later):
        def body(_, carry):
            if now is not None:
                multiply(index, *now)
            if later is not None:
                build(index + 1, *later)
            return carry

        lax.fori_loop(0, once, body, 0)

    first, second = (tone_a, mix_a), (tone_b, mix_b)
    stage(-1, None, first)

    def step(n, carry):
        stage(2 * n, first, second)
        stage(2 * n + 1, second, first)
        return carry

    lax.fori_loop(0, blocks // 2 - 1, step, 0)
    stage(blocks - 2, first, second)
    stage(blocks - 1, second, None)


def tone_of_place(lane):
    place = lane & (HALF - 1)
    within = place & 15
    above = (place & ~15) + jnp.where(within < GROUP, within + GROUP, 15 - within)
    below = jnp.where(above == 0, HALF, above)
    return HALF + jnp.where(lane < HALF, above, -below)


def place_of_tone(lane):
    away = jnp.where(lane >= HALF, lane - HALF, (HALF - lane) & (HALF - 1))
    within = away & 15
    place = (away & ~15) + jnp.where(within >= GROUP, within - GROUP, 15 - within)
    return jnp.where(lane >= HALF, place, HALF + place)


def reorder(values, index):
    pieces = [
        jnp.take_along_axis(values[n : n + GROUP], index, axis=1)
        for n in range(0, values.shape[0], GROUP)
    ]
    return jnp.concatenate(pieces, axis=0)


def respond_kernel(rows_ref, table_ref, out_ref, place_ref, words, sem, *scratch, portion):
    tables, buffers = scratch[:5], scratch[5:]
    for copy in fetch([(table_ref, place_ref)], sem):
        copy.wait()
    pairs = out_ref.shape[0]
    left = lane_index(1) < PMAX
    for pair in range(pairs):
        even, odd = (place_ref[link // LANES, link % LANES] for link in (2 * pair, 2 * pair + 1))
        for field in range(2):
            words[field, pair : pair + 1, :] = jnp.where(
                left, rows_ref[field, pl.ds(even, 1), :], rows_ref[field, pl.ds(odd, 1), :]
            )
    first_antenna = (lax.axis_index("grp") * portion).astype(jnp.float32)
    batch = 4

    def tabulate(index, carry):
        make_tables(words, [index * batch + n for n in range(batch)], first_antenna, tables)
        return carry

    lax.fori_loop(0, pairs // (GROUP * batch), tabulate, 0)

    def emit(pair, response):
        out_ref[pair] = response

    all_responses(pairs, tables, buffers, emit)


def receive_kernel(
    nearby_hbm, slot_hbm, symbol_hbm, response_ref, first_ref, second_ref, out_ref,
    nearby_ref, slot_ref, symbol_ref, sector_ref, sems, words, symbols, remote, *scratch, portion,
):
    tables, buffers = scratch[:5], scratch[5:]
    users = nearby_hbm.shape[1]
    pairs = users // 2
    base = 2 * pairs + users
    copies = fetch(
        [
            (nearby_hbm, nearby_ref),
            (slot_hbm, slot_ref),
            (symbol_hbm, symbol_ref),
            (first_ref.at[base : base + 1, :], sector_ref.at[0:1, :]),
            (second_ref.at[base : base + 1, :], sector_ref.at[1:2, :]),
        ],
        sems,
    )
    remote[...] = jnp.zeros_like(remote)
    order = tone_of_place(lane_index(GROUP))
    for n, ref in enumerate((first_ref, second_ref)):
        for field in range(2):
            words[field, n * pairs : (n + 1) * pairs, :] = ref[field * pairs : (field + 1) * pairs, :]
        codes = split(ref[2 * pairs : 2 * pairs + users, :])
        for part in range(2):
            symbols[part, n * users : (n + 1) * users, :] = reorder(
                root_value(codes[part]) * SYMBOL_TOP, order
            )
    first_antenna = (lax.axis_index("grp") * portion).astype(jnp.float32)
    make_tables(words, list(range(2 * pairs // GROUP)), first_antenna, tables)
    for copy in copies:
        copy.wait()
    own = reorder(symbol_ref[...].astype(jnp.float32), order).reshape(users, 2, LANES)
    for part in range(2):
        symbols[part, 2 * users :, :] = own[:, part, :]

    def contribute(place, row, re, im):
        sym_re = symbols[0, pl.ds(row, 1), :]
        sym_im = symbols[1, pl.ds(row, 1), :]
        remote[place, :portion, :] += re * sym_re + im * sym_im
        remote[place, portion:, :] += re * sym_im - im * sym_re

    window = CELL_SECTORS + 2 * REACH
    here = lax.axis_index("cell")
    first_sector = here * CELL_SECTORS - REACH

    def own_user(user, carry):
        slot = slot_ref[user]
        pair = user * (NEARBY_COUNT // 2) + (slot >> 1)
        at = pl.multiple_of((slot & 1) * (2 * portion), 2 * portion)
        re = response_ref[pair, pl.ds(at, portion), :]
        im = response_ref[pair, pl.ds(at + portion, portion), :]
        contribute(nearby_ref[slot, user] - first_sector, 2 * users + user, re, im)
        return carry

    lax.fori_loop(0, users, own_user, 0, unroll=8)
    after_first = (here & 1) == 0

    def emit(pair, response):
        for n in range(2):
            row = pair * 2 + n
            second = row >= users
            user = jnp.where(second, row - users, row)
            sector = sector_ref[jnp.where(second, 1, 0), user]
            place = jnp.where(second != after_first, sector + CELL_SECTORS, sector - CELL_SECTORS) + REACH
            place = jnp.where((place >= 0) & (place < window), place, window)
            re = response[2 * n * portion : (2 * n + 1) * portion]
            im = response[(2 * n + 1) * portion : (2 * n + 2) * portion]
            contribute(place, row, re, im)

    all_responses(2 * pairs, tables, buffers, emit)

    def normalise(sector, carry):
        value = remote[sector]
        re, im = value[:portion], value[portion:]
        power = jnp.sum(re * re + im * im, axis=1, keepdims=True) * (1.0 / FRAME_TONES)
        scale = lax.rsqrt(power + EPSILON)
        remote[sector, :portion, :] = (re * scale).astype(jnp.bfloat16).astype(jnp.float32)
        remote[sector, portion:, :] = (im * scale).astype(jnp.bfloat16).astype(jnp.float32)
        return carry

    lax.fori_loop(0, window, normalise, 0, unroll=8)

    def one_user(user, carry):
        total_re = jnp.zeros((GROUP, LANES), jnp.float32)
        total_im = jnp.zeros((GROUP, LANES), jnp.float32)
        for k in range(NEARBY_COUNT):
            sector = nearby_ref[k, user] - first_sector
            pair = user * (NEARBY_COUNT // 2) + k // 2
            at = (k % 2) * 2 * portion
            for n in range(0, portion, GROUP):
                re = response_ref[pair, at + n : at + n + GROUP, :]
                im = response_ref[pair, at + portion + n : at + portion + n + GROUP, :]
                other_re = remote[sector, n : n + GROUP, :]
                other_im = remote[sector, portion + n : portion + n + GROUP, :]
                total_re = total_re + (re * other_re - im * other_im)
                total_im = total_im + (re * other_im + im * other_re)
        scale = 1.0 / math.sqrt(SECTOR_ANTENNAS)
        out_ref[pl.ds(user * 2, 1), :] = jnp.sum(total_re, axis=0, keepdims=True) * scale
        out_ref[pl.ds(user * 2 + 1, 1), :] = jnp.sum(total_im, axis=0, keepdims=True) * scale
        return carry

    lax.fori_loop(0, users, one_user, 0, unroll=4)
    out_ref[...] = reorder(out_ref[...], place_of_tone(lane_index(GROUP)))


VMEM = pl.BlockSpec(memory_space=pltpu.VMEM)
HBM = pl.BlockSpec(memory_space=pltpu.HBM)
ANY = pl.BlockSpec(memory_space=pl.ANY)
LIMIT = pltpu.CompilerParams(vmem_limit_bytes=16 << 20)
BLOCK = 8


def in_hbm(values):
    return pltpu.with_memory_space_constraint(values, pltpu.HBM)


def response_scratch(pairs, portion):
    counts = (GROUP, SPANS, 1, GROUP, portion // (2 * GROUP))
    tables = [pltpu.VMEM((2, pairs * n, LANES), jnp.float32) for n in counts]
    factors = [
        pltpu.VMEM((BLOCK, 2 * HALF + 4 * GROUP, LANES), jnp.bfloat16),
        pltpu.VMEM((BLOCK, 2 * portion, LANES), jnp.bfloat16),
    ]
    return tables + factors + factors


def shards(
    path_delay,
    path_angle,
    path_gain,
    slot_counts,
    slot_offsets,
    ray_link,
    nearby_sectors,
    serving_slot,
    symbols,
):
    devices = lax.axis_size("cell")
    worker_count = lax.axis_size("grp")
    path_total = path_delay.shape[0]
    link_total = slot_counts.shape[0]
    total_users = serving_slot.shape[0]
    capacity = 2 * link_total // devices
    stride = pl.cdiv(capacity // 2, GROUP) * GROUP
    portion = SECTOR_ANTENNAS // worker_count
    swap = [(n, worker_count - 1 - n) for n in range(worker_count)]
    path_rows = path_total // LANES
    link_rows = link_total // LANES
    sizes = dict(capacity=capacity, stride=stride)

    packed = pl.pallas_call(
        functools.partial(pack_kernel, link_total=link_total, **sizes),
        out_shape=jax.ShapeDtypeStruct((devices * stride, LANES), jnp.int32),
        in_specs=[HBM] * 6,
        out_specs=VMEM,
        scratch_shapes=[pltpu.SMEM((link_total,), jnp.int32)] * 3
        + [
            pltpu.VMEM((path_rows, LANES), jnp.float32),
            pltpu.VMEM((path_rows, LANES), jnp.float32),
            pltpu.VMEM((path_rows, LANES), jnp.float32),
            pltpu.VMEM((path_rows, LANES), jnp.float32),
            pltpu.VMEM((pl.cdiv(path_rows + 1, GROUP) * GROUP, LANES), jnp.int32),
            pltpu.SemaphoreType.DMA((7,)),
        ],
        compiler_params=LIMIT,
    )(
        in_hbm(ray_link),
        in_hbm(slot_counts),
        in_hbm(slot_offsets),
        in_hbm(path_delay.reshape(path_rows, LANES)),
        in_hbm(path_angle.reshape(path_rows, LANES)),
        in_hbm(path_gain.reshape(2, path_rows, LANES).transpose(1, 0, 2)),
    )
    arrived = lax.all_to_all(
        packed.reshape(devices, stride, LANES), "cell", split_axis=0, concat_axis=0, tiled=True
    )
    other = lax.ppermute(arrived, "grp", swap)

    row_total = devices * stride
    list_rows = 2 * total_users + GROUP
    symbol_rows = symbols.reshape(2 * total_users, LANES)
    small_scratch = [
        pltpu.SMEM(nearby_sectors.shape, jnp.int32),
        pltpu.SMEM((total_users,), jnp.int32),
        pltpu.VMEM((2 * total_users, LANES), jnp.bfloat16),
    ]
    rows, table, listed = pl.pallas_call(
        functools.partial(sort_kernel, **sizes),
        out_shape=(
            jax.ShapeDtypeStruct((2, 2 * row_total, LANES), jnp.int32),
            jax.ShapeDtypeStruct((link_rows, LANES), jnp.int32),
            jax.ShapeDtypeStruct((list_rows, LANES), jnp.int32),
        ),
        in_specs=[HBM] * 3 + [VMEM] * 2,
        out_specs=(VMEM, VMEM, VMEM),
        scratch_shapes=small_scratch
        + [pltpu.SMEM((link_rows, LANES), jnp.int32), pltpu.SemaphoreType.DMA((4,))],
        compiler_params=LIMIT,
    )(
        in_hbm(nearby_sectors),
        in_hbm(serving_slot),
        in_hbm(symbol_rows),
        arrived.reshape(row_total, LANES),
        other.reshape(row_total, LANES),
    )

    def exchange(first):
        pairs = [(n, n + 1) for n in range(first, devices - 1, 2)]
        return lax.ppermute(listed, "cell", pairs + [(m, n) for n, m in pairs])

    first_list, second_list = exchange(0), exchange(1)

    pair_total = link_total // 2
    response = pl.pallas_call(
        functools.partial(respond_kernel, portion=portion),
        out_shape=jax.ShapeDtypeStruct((pair_total, 4 * portion, LANES), jnp.float32),
        in_specs=[VMEM, VMEM],
        out_specs=VMEM,
        scratch_shapes=[
            pltpu.SMEM((link_rows, LANES), jnp.int32),
            pltpu.VMEM((2, pair_total, LANES), jnp.int32),
            pltpu.SemaphoreType.DMA((1,)),
        ]
        + response_scratch(pair_total, portion),
        cost_estimate=pl.CostEstimate(
            flops=pair_total * 2 * 128 * 128 * 256 * 40,
            bytes_accessed=pair_total * 4 * portion * LANES * 2,
            transcendentals=0,
        ),
        compiler_params=LIMIT,
    )(rows, table)

    partial_value = pl.pallas_call(
        functools.partial(receive_kernel, portion=portion),
        out_shape=jax.ShapeDtypeStruct((2 * total_users, LANES), jnp.float32),
        in_specs=[ANY] * 3 + [VMEM] * 3,
        out_specs=VMEM,
        scratch_shapes=small_scratch
        + [
            pltpu.SMEM((2, LANES), jnp.int32),
            pltpu.SemaphoreType.DMA((5,)),
            pltpu.VMEM((2, total_users, LANES), jnp.int32),
            pltpu.VMEM((2, 3 * total_users, LANES), jnp.float32),
            pltpu.VMEM((CELL_SECTORS + 2 * REACH + 1, 2 * portion, LANES), jnp.float32),
        ]
        + response_scratch(total_users, portion),
        compiler_params=LIMIT,
    )(nearby_sectors, serving_slot, symbol_rows, response, first_list, second_list)
    summed = partial_value + lax.ppermute(partial_value, "grp", swap)
    return summed.reshape(total_users, 2, FRAME_TONES)


def solution(mesh):
    placed = (
        P("cell"),
        P("cell"),
        P(None, "cell"),
        P("cell"),
        P("cell"),
        P("cell"),
        P(None, "cell"),
        P("cell"),
        P("cell", None, None),
    )
    return jax.shard_map(
        shards, mesh=mesh, in_specs=placed, out_specs=P("cell", None, None), check_vma=False
    )
```

```python
import functools
import math

import jax
import jax.numpy as jnp
from jax import lax
from jax.experimental import pallas as pl
from jax.experimental.pallas import tpu as pltpu
from jax.sharding import PartitionSpec as P

SECTOR_ANTENNAS = 64
FRAME_TONES = 128
PMAX = 64
NEARBY_COUNT = 8
CELL_SECTORS = 32
REACH = 16
EPSILON = 1e-06

LANES = 128
GROUP = 8
HALF = FRAME_TONES // 2
SPANS = HALF // (2 * GROUP)
LEVELS = 32767.0
TAG_LANE = LANES - PMAX // 2
UNROLL = 32
DELAY_STEP = 64.0 / 65535.0
SYMBOL_TOP = 4.0

SIN_TERMS = tuple((-1.0) ** n / math.factorial(2 * n + 1) for n in range(6))
COS_TERMS = tuple((-1.0) ** n / math.factorial(2 * n) for n in range(8))


def polynomial(terms, square):
    total = terms[-1]
    for term in terms[-2::-1]:
        total = total * square + term
    return total


def quarter_cos_sin(x):
    square = x * x
    return polynomial(COS_TERMS, square), x * polynomial(SIN_TERMS, square)


def cos_sin_turns(turns):
    turns = turns - jnp.round(turns)
    c, s = quarter_cos_sin(math.pi * turns)
    return 1.0 - 2.0 * s * s, 2.0 * s * c


def times(x, y):
    return x[0] * y[0] - x[1] * y[1], x[0] * y[1] + x[1] * y[0]


def powers(base, count):
    found = {1: base}
    for n in range(2, count + 1):
        found[n] = times(found[n // 2], found[n - n // 2])
    return found


def join(high, low):
    return (high.astype(jnp.int32) << 16) | (low.astype(jnp.int32) & 0xFFFF)


def split(word):
    return (word >> 16).astype(jnp.float32), ((word << 16) >> 16).astype(jnp.float32)


def root_code(value):
    root = jnp.sqrt(jnp.sqrt(jnp.sqrt(jnp.abs(value)))) * LEVELS
    return jnp.round(jnp.where(value < 0, -root, root))


def root_value(code):
    unit = code * (1.0 / LEVELS)
    power = unit * unit
    power = power * power
    power = power * power
    return jnp.where(code < 0, -power, power)


def lane_index(rows):
    return lax.broadcasted_iota(jnp.int32, (rows, LANES), 1)


def fetch(pairs, sems):
    copies = [pltpu.make_async_copy(a, b, sems.at[n]) for n, (a, b) in enumerate(pairs)]
    for copy in copies:
        copy.start()
    return copies


def pack_kernel(
    link_hbm, count_hbm, offset_hbm, delay_hbm, angle_hbm, gain_hbm, out_ref,
    link_ref, count_ref, offset_ref, delay_ref, angle_ref, real_ref, imag_ref, word_ref, sems,
    *, link_total, capacity, stride,
):
    copies = fetch(
        [
            (link_hbm, link_ref),
            (count_hbm, count_ref),
            (offset_hbm, offset_ref),
            (delay_hbm, delay_ref),
            (angle_hbm, angle_ref),
            (gain_hbm.at[:, 0, :], real_ref),
            (gain_hbm.at[:, 1, :], imag_ref),
        ],
        sems,
    )
    lane = lane_index(1)
    out_ref[...] = jnp.zeros_like(out_ref)
    for copy in copies:
        copy.wait()
    rows = delay_ref.shape[0]
    lower = lax.axis_index("grp") == 0
    c, s = quarter_cos_sin(angle_ref[...] * 0.5)
    gain_re, gain_im = real_ref[...], imag_ref[...]
    sine = 2.0 * s * c
    code = jnp.round(LEVELS * sine)
    turn = (sine - code * (1.0 / LEVELS)) * (0.5 * math.pi * (SECTOR_ANTENNAS - 1))
    gain_re, gain_im = gain_re + gain_im * turn, gain_im - gain_re * turn
    high = jnp.where(lower, jnp.round(delay_ref[...] * (1.0 / DELAY_STEP)) - 32768.0, root_code(gain_re))
    low = jnp.where(lower, code, root_code(gain_im))
    word_ref[:rows, :] = join(high, low)
    link_bits = link_total.bit_length() - 1
    owners = out_ref.shape[0] // stride
    tag_rows = max(owners, GROUP)
    column = lane_index(tag_rows)
    tag_place = lax.broadcasted_iota(jnp.int32, (tag_rows, LANES), 0) * (2 * stride) + column - TAG_LANE
    tag_place = jnp.where(column >= TAG_LANE, tag_place, -1)

    def step(slot, carry):
        last_owner, free, taken, tags = carry
        link = link_ref[slot]
        count = count_ref[slot]
        owner = link >> link_bits
        fresh = owner != last_owner
        first = owner * (2 * stride)
        free = jnp.where(fresh, first, free)
        taken = jnp.where(fresh, 0, taken)
        short = jnp.where(count <= PMAX // 2, 1 - taken, 0)
        place = jnp.where(short == 1, first + (capacity - 1), free)
        offset = offset_ref[slot]
        row = offset >> 7
        shift = offset & (LANES - 1)
        word = jnp.where(lane >= shift, word_ref[pl.ds(row, 1), :], word_ref[pl.ds(row + 1, 1), :])
        start = (place & 1) << 6
        word = pltpu.roll(word, (start - shift) & (LANES - 1), 1)
        within = lane - start
        live = (within >= 0) & (within < count)
        pltpu.store(out_ref.at[pl.ds(place >> 1, 1), :], word, mask=live)
        tags = jnp.where(tag_place == place, link, tags)
        return owner, free + 1 - short, taken + short, tags

    empty = jnp.full((tag_rows, LANES), -1, jnp.int32)
    zero = jnp.int32(0)
    tags = lax.fori_loop(0, link_total, step, (jnp.int32(-1), zero, zero, empty), unroll=UNROLL)[3]
    last = pl.ds(capacity // 2 - 1, owners, stride=stride)
    out_ref[last, :] = jnp.where(lane >= TAG_LANE, tags[:owners], out_ref[last, :])


def find_rows(own_ref, table_ref, capacity, stride):
    total_rows = own_ref.shape[0]
    senders = total_rows // stride
    tags = own_ref[pl.ds(capacity // 2 - 1, senders, stride=stride), :]
    tags = (tags - lax.axis_index("cell") * (table_ref.shape[0] * LANES)).astype(jnp.float32).T
    depth = pl.cdiv(capacity, GROUP) * GROUP
    tags = tags[TAG_LANE : TAG_LANE + depth]
    place = lax.broadcasted_iota(jnp.int32, (depth, LANES), 0)
    inside = place < capacity
    lane = lane_index(depth)
    value = ((place >> 1) + total_rows * ((place ^ lane) & 1)).astype(jnp.float32)
    lane = lane.astype(jnp.float32)
    rows = table_ref.shape[0]
    totals = [jnp.zeros((depth, LANES), jnp.float32) for _ in range(rows)]
    for sender in range(senders):
        column = jnp.broadcast_to(tags[:, sender : sender + 1], (depth, LANES))
        column = jnp.where(inside, column, -1.0)
        here = value + float(sender * stride)
        for n in range(rows):
            totals[n] += jnp.where(column == lane + float(n * LANES), here, 0.0)
    for n in range(rows):
        table_ref[n : n + 1, :] = jnp.sum(totals[n], axis=0, keepdims=True).astype(jnp.int32)


def sort_kernel(
    nearby_hbm, slot_hbm, symbol_hbm, own_ref, other_ref, rows_ref, table_ref, list_ref,
    nearby_ref, slot_ref, symbol_ref, place_ref, sems, *, capacity, stride,
):
    copies = fetch(
        [(nearby_hbm, nearby_ref), (slot_hbm, slot_ref), (symbol_hbm, symbol_ref)], sems
    )
    find_rows(own_ref, table_ref, capacity, stride)
    copies += fetch([(table_ref, place_ref)], sems.at[pl.ds(3, 1)])
    total_rows = own_ref.shape[0]
    lower = lax.axis_index("grp") == 0
    own, other = own_ref[...], other_ref[...]
    for n, words in enumerate((jnp.where(lower, own, other), jnp.where(lower, other, own))):
        rows_ref[n, :total_rows, :] = words
        rows_ref[n, total_rows:, :] = pltpu.roll(words, PMAX, 1)
        senders = total_rows // stride
        for m, at in enumerate((TAG_LANE, TAG_LANE - PMAX)):
            last = pl.ds(m * total_rows + capacity // 2 - 1, senders, stride=stride)
            kept = (lane_index(senders) < at) | (lane_index(senders) >= at + PMAX // 2)
            rows_ref[n, last, :] = jnp.where(kept, rows_ref[n, last, :], 0)
    for copy in copies:
        copy.wait()
    users = slot_ref.shape[0]
    pairs = users // 2
    left = lane_index(1) < PMAX
    lane = lane_index(1)
    sectors = jnp.zeros((1, LANES), jnp.int32)
    first_sector = lax.axis_index("cell") * CELL_SECTORS
    for pair in range(pairs):
        found = []
        for user in (2 * pair, 2 * pair + 1):
            slot = slot_ref[user]
            link = user * NEARBY_COUNT + slot
            row = place_ref[user * NEARBY_COUNT // LANES, link & (LANES - 1)]
            turned = jnp.where(row < total_rows, row + total_rows, row - total_rows)
            found.append(jnp.where(((slot ^ user) & 1) == 0, row, turned))
            sectors = jnp.where(lane == user, nearby_ref[slot, user] - first_sector, sectors)
        for n in range(2):
            even = rows_ref[n, pl.ds(found[0], 1), :]
            odd = rows_ref[n, pl.ds(found[1], 1), :]
            list_ref[n * pairs + pair : n * pairs + pair + 1, :] = jnp.where(left, even, odd)
    symbols = symbol_ref[...].astype(jnp.float32) * (1.0 / SYMBOL_TOP)
    code_ref = list_ref.at[2 * pairs : 2 * pairs + users, :]
    codes = root_code(symbols).reshape(users, 2, LANES)
    code_ref[...] = join(codes[:, 0, :], codes[:, 1, :])
    base = 2 * pairs + users
    list_ref[base : base + GROUP, :] = jnp.broadcast_to(sectors, (GROUP, LANES))


def make_tables(words_ref, groups, first_antenna, tables):
    fine, centre, last, near, far = tables
    steps = far.shape[1] // last.shape[1]
    for group in groups:
        rows = pl.ds(group * GROUP, GROUP)
        delay, sine = split(words_ref[0, rows, :])
        delay = (delay + 32768.0) * DELAY_STEP
        sine = sine * (1.0 / LEVELS)
        gain_re, gain_im = (root_value(code) for code in split(words_ref[1, rows, :]))

        def put(ref, n, count, value):
            at = pl.ds(group * (GROUP * count) + n, GROUP, stride=count) if count > 1 else rows
            ref[0, at, :] = value[0]
            ref[1, at, :] = value[1]

        def half_steps(half):
            whole = times(half, half)
            up = powers(whole, GROUP - 1)
            return whole, [half] + [times(half, up[n]) for n in range(1, GROUP)]

        c, s = quarter_cos_sin(delay * (math.pi / FRAME_TONES))
        whole, found = half_steps((c, -s))
        for n in range(GROUP):
            put(fine, n, GROUP, found[n])
        top = found[GROUP - 1]
        wide = times(times(top, top), whole)
        value = top
        for n in range(SPANS):
            if n:
                value = times(value, wide)
            put(centre, n, SPANS, value)
        put(last, 0, 1, times(value, times(top, whole)))

        c, s = cos_sin_turns(sine * 0.25)
        whole, found = half_steps((c, -s))
        for n in range(GROUP):
            put(near, n, GROUP, found[n])
        top = found[GROUP - 1]
        wide = times(times(top, top), whole)
        c, s = cos_sin_turns(sine * (0.5 * first_antenna))
        value = times(times((gain_re, gain_im), (c, -s)), top)
        for n in range(steps):
            if n:
                value = times(value, wide)
            put(far, n, steps, value)


def both_sides(centre, fine):
    a, b = centre[0] * fine[0], centre[1] * fine[1]
    c, d = centre[0] * fine[1], centre[1] * fine[0]
    return (a - b, c + d), (a + b, d - c)


def sides_of(centre_ref, fine_ref, pair, spans):
    at = pl.ds(pl.multiple_of(pair * GROUP, GROUP), GROUP)
    fine = (fine_ref[0, at, :], fine_ref[1, at, :])
    found = []
    for n in range(spans):
        row = pl.ds(pair * spans + n, 1)
        found.extend(both_sides((centre_ref[0, row, :], centre_ref[1, row, :]), fine))
    return found


def stack(values, part):
    return jnp.concatenate([v[part] for v in values], axis=0).astype(jnp.bfloat16)


def build_operands(pair, tables, tone_ref, mix_ref):
    fine, centre, last, near, far = tables
    delay = sides_of(centre, fine, pair, SPANS)
    row = pl.ds(pair, 1)
    final = lax.broadcasted_iota(jnp.int32, (GROUP, LANES), 0) == GROUP - 1
    steps = far.shape[1] // last.shape[1]
    spread = sides_of(far, near, pair, steps)
    portion = mix_ref.shape[0] // 2
    for n in range(2):
        tone_ref[n * HALF : (n + 1) * HALF, :] = stack(delay, n)
        swapped = jnp.where(final, last[n, row, :], delay[1][n])
        head = jnp.concatenate([delay[0][n], swapped], axis=0).astype(jnp.bfloat16)
        at = 2 * HALF + 2 * GROUP * n
        tone_ref[at : at + 2 * GROUP, :] = head
        mix_ref[n * portion : (n + 1) * portion, :] = stack(spread, n)


def multiply_operands(tone_ref, mix_ref):
    re, im = tone_ref[:HALF, :], tone_ref[HALF : 2 * HALF, :]
    head = [tone_ref[2 * HALF + 2 * GROUP * n : 2 * HALF + 2 * GROUP * (n + 1), :] for n in range(2)]
    low_re = jnp.concatenate([head[0], re[2 * GROUP :]], axis=0)
    low_im = jnp.concatenate([head[1], im[2 * GROUP :]], axis=0)
    tones = jnp.concatenate(
        [jnp.concatenate([re, -im], axis=1), jnp.concatenate([low_re, low_im], axis=1)], axis=0
    )
    portion = mix_ref.shape[0] // 2
    spread_re, spread_im = mix_ref[:portion, :], mix_ref[portion:, :]
    lane = lane_index(1)
    blocks = []
    for keep in (lane < PMAX, lane >= PMAX):
        keep = jnp.where(keep, 1.0, 0.0).astype(jnp.bfloat16)
        a, b, c = spread_re * keep, spread_im * keep, spread_re * -keep
        blocks.append(jnp.concatenate([a, b], axis=1))
        blocks.append(jnp.concatenate([b, c], axis=1))
    return lax.dot_general(
        jnp.concatenate(blocks, axis=0),
        tones,
        (((1,), (1,)), ((), ())),
        preferred_element_type=jnp.float32,
    )


def all_responses(pairs, tables, buffers, emit):
    tone_a, mix_a, tone_b, mix_b = buffers
    block = tone_a.shape[0]
    blocks = pairs // block
    once = jnp.minimum(lax.axis_index("cell") + 1, 1)

    def build(index, tone_ref, mix_ref):
        for n in range(block):
            build_operands(index * block + n, tables, tone_ref.at[n], mix_ref.at[n])

    def multiply(index, tone_ref, mix_ref):
        for n in range(block):
            emit(index * block + n, multiply_operands(tone_ref.at[n], mix_ref.at[n]))

    def stage(index, now, later):
        def body(_, carry):
            if now is not None:
                multiply(index, *now)
            if later is not None:
                build(index + 1, *later)
            return carry

        lax.fori_loop(0, once, body, 0)

    first, second = (tone_a, mix_a), (tone_b, mix_b)
    stage(-1, None, first)

    def step(n, carry):
        stage(2 * n, first, second)
        stage(2 * n + 1, second, first)
        return carry

    lax.fori_loop(0, blocks // 2 - 1, step, 0)
    stage(blocks - 2, first, second)
    stage(blocks - 1, second, None)


def tone_of_place(lane):
    place = lane & (HALF - 1)
    within = place & 15
    above = (place & ~15) + jnp.where(within < GROUP, within + GROUP, 15 - within)
    below = jnp.where(above == 0, HALF, above)
    return HALF + jnp.where(lane < HALF, above, -below)


def place_of_tone(lane):
    away = jnp.where(lane >= HALF, lane - HALF, (HALF - lane) & (HALF - 1))
    within = away & 15
    place = (away & ~15) + jnp.where(within >= GROUP, within - GROUP, 15 - within)
    return jnp.where(lane >= HALF, place, HALF + place)


def reorder(values, index):
    pieces = [
        jnp.take_along_axis(values[n : n + GROUP], index, axis=1)
        for n in range(0, values.shape[0], GROUP)
    ]
    return jnp.concatenate(pieces, axis=0)


def respond_kernel(rows_ref, table_ref, out_ref, place_ref, words, sem, *scratch, portion):
    tables, buffers = scratch[:5], scratch[5:]
    for copy in fetch([(table_ref, place_ref)], sem):
        copy.wait()
    pairs = out_ref.shape[0]
    left = lane_index(1) < PMAX
    for pair in range(pairs):
        even, odd = (place_ref[link // LANES, link % LANES] for link in (2 * pair, 2 * pair + 1))
        for field in range(2):
            words[field, pair : pair + 1, :] = jnp.where(
                left, rows_ref[field, pl.ds(even, 1), :], rows_ref[field, pl.ds(odd, 1), :]
            )
    first_antenna = (lax.axis_index("grp") * portion).astype(jnp.float32)
    batch = 4

    def tabulate(index, carry):
        make_tables(words, [index * batch + n for n in range(batch)], first_antenna, tables)
        return carry

    lax.fori_loop(0, pairs // (GROUP * batch), tabulate, 0)

    def emit(pair, response):
        out_ref[pair] = response

    all_responses(pairs, tables, buffers, emit)


def receive_kernel(
    nearby_hbm, slot_hbm, symbol_hbm, response_ref, first_ref, second_ref, out_ref,
    nearby_ref, slot_ref, symbol_ref, sector_ref, sems, words, symbols, remote, *scratch, portion,
):
    tables, buffers = scratch[:5], scratch[5:]
    users = nearby_hbm.shape[1]
    pairs = users // 2
    base = 2 * pairs + users
    copies = fetch(
        [
            (nearby_hbm, nearby_ref),
            (slot_hbm, slot_ref),
            (symbol_hbm, symbol_ref),
            (first_ref.at[base : base + 1, :], sector_ref.at[0:1, :]),
            (second_ref.at[base : base + 1, :], sector_ref.at[1:2, :]),
        ],
        sems,
    )
    remote[...] = jnp.zeros_like(remote)
    order = tone_of_place(lane_index(GROUP))
    for n, ref in enumerate((first_ref, second_ref)):
        for field in range(2):
            words[field, n * pairs : (n + 1) * pairs, :] = ref[field * pairs : (field + 1) * pairs, :]
        codes = split(ref[2 * pairs : 2 * pairs + users, :])
        for part in range(2):
            symbols[part, n * users : (n + 1) * users, :] = reorder(
                root_value(codes[part]) * SYMBOL_TOP, order
            )
    first_antenna = (lax.axis_index("grp") * portion).astype(jnp.float32)
    make_tables(words, list(range(2 * pairs // GROUP)), first_antenna, tables)
    for copy in copies:
        copy.wait()
    own = reorder(symbol_ref[...].astype(jnp.float32), order).reshape(users, 2, LANES)
    for part in range(2):
        symbols[part, 2 * users :, :] = own[:, part, :]

    def contribute(place, row, re, im):
        sym_re = symbols[0, pl.ds(row, 1), :]
        sym_im = symbols[1, pl.ds(row, 1), :]
        remote[place, :portion, :] += re * sym_re + im * sym_im
        remote[place, portion:, :] += re * sym_im - im * sym_re

    window = CELL_SECTORS + 2 * REACH
    here = lax.axis_index("cell")
    first_sector = here * CELL_SECTORS - REACH

    def own_user(user, carry):
        slot = slot_ref[user]
        pair = user * (NEARBY_COUNT // 2) + (slot >> 1)
        at = pl.multiple_of((slot & 1) * (2 * portion), 2 * portion)
        re = response_ref[pair, pl.ds(at, portion), :]
        im = response_ref[pair, pl.ds(at + portion, portion), :]
        contribute(nearby_ref[slot, user] - first_sector, 2 * users + user, re, im)
        return carry

    lax.fori_loop(0, users, own_user, 0, unroll=8)
    after_first = (here & 1) == 0

    def emit(pair, response):
        for n in range(2):
            row = pair * 2 + n
            second = row >= users
            user = jnp.where(second, row - users, row)
            sector = sector_ref[jnp.where(second, 1, 0), user]
            place = jnp.where(second != after_first, sector + CELL_SECTORS, sector - CELL_SECTORS) + REACH
            place = jnp.where((place >= 0) & (place < window), place, window)
            re = response[2 * n * portion : (2 * n + 1) * portion]
            im = response[(2 * n + 1) * portion : (2 * n + 2) * portion]
            contribute(place, row, re, im)

    all_responses(2 * pairs, tables, buffers, emit)

    def normalise(sector, carry):
        value = remote[sector]
        re, im = value[:portion], value[portion:]
        power = jnp.sum(re * re + im * im, axis=1, keepdims=True) * (1.0 / FRAME_TONES)
        scale = lax.rsqrt(power + EPSILON)
        remote[sector, :portion, :] = (re * scale).astype(jnp.bfloat16).astype(jnp.float32)
        remote[sector, portion:, :] = (im * scale).astype(jnp.bfloat16).astype(jnp.float32)
        return carry

    lax.fori_loop(0, window, normalise, 0, unroll=8)

    def one_user(user, carry):
        total_re = jnp.zeros((GROUP, LANES), jnp.float32)
        total_im = jnp.zeros((GROUP, LANES), jnp.float32)
        for k in range(NEARBY_COUNT):
            sector = nearby_ref[k, user] - first_sector
            pair = user * (NEARBY_COUNT // 2) + k // 2
            at = (k % 2) * 2 * portion
            for n in range(0, portion, GROUP):
                re = response_ref[pair, at + n : at + n + GROUP, :]
                im = response_ref[pair, at + portion + n : at + portion + n + GROUP, :]
                other_re = remote[sector, n : n + GROUP, :]
                other_im = remote[sector, portion + n : portion + n + GROUP, :]
                total_re = total_re + (re * other_re - im * other_im)
                total_im = total_im + (re * other_im + im * other_re)
        scale = 1.0 / math.sqrt(SECTOR_ANTENNAS)
        out_ref[pl.ds(user * 2, 1), :] = jnp.sum(total_re, axis=0, keepdims=True) * scale
        out_ref[pl.ds(user * 2 + 1, 1), :] = jnp.sum(total_im, axis=0, keepdims=True) * scale
        return carry

    lax.fori_loop(0, users, one_user, 0, unroll=8)
    out_ref[...] = reorder(out_ref[...], place_of_tone(lane_index(GROUP)))


VMEM = pl.BlockSpec(memory_space=pltpu.VMEM)
HBM = pl.BlockSpec(memory_space=pltpu.HBM)
ANY = pl.BlockSpec(memory_space=pl.ANY)
LIMIT = pltpu.CompilerParams(vmem_limit_bytes=16 << 20)
BLOCK = 8


def in_hbm(values):
    return pltpu.with_memory_space_constraint(values, pltpu.HBM)


def response_scratch(pairs, portion):
    counts = (GROUP, SPANS, 1, GROUP, portion // (2 * GROUP))
    tables = [pltpu.VMEM((2, pairs * n, LANES), jnp.float32) for n in counts]
    factors = [
        pltpu.VMEM((BLOCK, 2 * HALF + 4 * GROUP, LANES), jnp.bfloat16),
        pltpu.VMEM((BLOCK, 2 * portion, LANES), jnp.bfloat16),
    ]
    return tables + factors + factors


def shards(
    path_delay,
    path_angle,
    path_gain,
    slot_counts,
    slot_offsets,
    ray_link,
    nearby_sectors,
    serving_slot,
    symbols,
):
    devices = lax.axis_size("cell")
    worker_count = lax.axis_size("grp")
    path_total = path_delay.shape[0]
    link_total = slot_counts.shape[0]
    total_users = serving_slot.shape[0]
    capacity = 2 * link_total // devices
    stride = pl.cdiv(capacity // 2, GROUP) * GROUP
    portion = SECTOR_ANTENNAS // worker_count
    swap = [(n, worker_count - 1 - n) for n in range(worker_count)]
    path_rows = path_total // LANES
    link_rows = link_total // LANES
    sizes = dict(capacity=capacity, stride=stride)

    packed = pl.pallas_call(
        functools.partial(pack_kernel, link_total=link_total, **sizes),
        out_shape=jax.ShapeDtypeStruct((devices * stride, LANES), jnp.int32),
        in_specs=[HBM] * 6,
        out_specs=VMEM,
        scratch_shapes=[pltpu.SMEM((link_total,), jnp.int32)] * 3
        + [
            pltpu.VMEM((path_rows, LANES), jnp.float32),
            pltpu.VMEM((path_rows, LANES), jnp.float32),
            pltpu.VMEM((path_rows, LANES), jnp.float32),
            pltpu.VMEM((path_rows, LANES), jnp.float32),
            pltpu.VMEM((pl.cdiv(path_rows + 1, GROUP) * GROUP, LANES), jnp.int32),
            pltpu.SemaphoreType.DMA((7,)),
        ],
        compiler_params=LIMIT,
    )(
        in_hbm(ray_link),
        in_hbm(slot_counts),
        in_hbm(slot_offsets),
        in_hbm(path_delay.reshape(path_rows, LANES)),
        in_hbm(path_angle.reshape(path_rows, LANES)),
        in_hbm(path_gain.reshape(2, path_rows, LANES).transpose(1, 0, 2)),
    )
    arrived = lax.all_to_all(
        packed.reshape(devices, stride, LANES), "cell", split_axis=0, concat_axis=0, tiled=True
    )
    other = lax.ppermute(arrived, "grp", swap)

    row_total = devices * stride
    list_rows = 2 * total_users + GROUP
    symbol_rows = symbols.reshape(2 * total_users, LANES)
    small_scratch = [
        pltpu.SMEM(nearby_sectors.shape, jnp.int32),
        pltpu.SMEM((total_users,), jnp.int32),
        pltpu.VMEM((2 * total_users, LANES), jnp.bfloat16),
    ]
    rows, table, listed = pl.pallas_call(
        functools.partial(sort_kernel, **sizes),
        out_shape=(
            jax.ShapeDtypeStruct((2, 2 * row_total, LANES), jnp.int32),
            jax.ShapeDtypeStruct((link_rows, LANES), jnp.int32),
            jax.ShapeDtypeStruct((list_rows, LANES), jnp.int32),
        ),
        in_specs=[HBM] * 3 + [VMEM] * 2,
        out_specs=(VMEM, VMEM, VMEM),
        scratch_shapes=small_scratch
        + [pltpu.SMEM((link_rows, LANES), jnp.int32), pltpu.SemaphoreType.DMA((4,))],
        compiler_params=LIMIT,
    )(
        in_hbm(nearby_sectors),
        in_hbm(serving_slot),
        in_hbm(symbol_rows),
        arrived.reshape(row_total, LANES),
        other.reshape(row_total, LANES),
    )

    def exchange(first):
        pairs = [(n, n + 1) for n in range(first, devices - 1, 2)]
        return lax.ppermute(listed, "cell", pairs + [(m, n) for n, m in pairs])

    first_list, second_list = exchange(0), exchange(1)

    pair_total = link_total // 2
    response = pl.pallas_call(
        functools.partial(respond_kernel, portion=portion),
        out_shape=jax.ShapeDtypeStruct((pair_total, 4 * portion, LANES), jnp.float32),
        in_specs=[VMEM, VMEM],
        out_specs=VMEM,
        scratch_shapes=[
            pltpu.SMEM((link_rows, LANES), jnp.int32),
            pltpu.VMEM((2, pair_total, LANES), jnp.int32),
            pltpu.SemaphoreType.DMA((1,)),
        ]
        + response_scratch(pair_total, portion),
        cost_estimate=pl.CostEstimate(
            flops=pair_total * 2 * 128 * 128 * 256 * 40,
            bytes_accessed=pair_total * 4 * portion * LANES * 2,
            transcendentals=0,
        ),
        compiler_params=LIMIT,
    )(rows, table)

    partial_value = pl.pallas_call(
        functools.partial(receive_kernel, portion=portion),
        out_shape=jax.ShapeDtypeStruct((2 * total_users, LANES), jnp.float32),
        in_specs=[ANY] * 3 + [VMEM] * 3,
        out_specs=VMEM,
        scratch_shapes=small_scratch
        + [
            pltpu.SMEM((2, LANES), jnp.int32),
            pltpu.SemaphoreType.DMA((5,)),
            pltpu.VMEM((2, total_users, LANES), jnp.int32),
            pltpu.VMEM((2, 3 * total_users, LANES), jnp.float32),
            pltpu.VMEM((CELL_SECTORS + 2 * REACH + 1, 2 * portion, LANES), jnp.float32),
        ]
        + response_scratch(total_users, portion),
        compiler_params=LIMIT,
    )(nearby_sectors, serving_slot, symbol_rows, response, first_list, second_list)
    summed = partial_value + lax.ppermute(partial_value, "grp", swap)
    return summed.reshape(total_users, 2, FRAME_TONES)


def solution(mesh):
    placed = (
        P("cell"),
        P("cell"),
        P(None, "cell"),
        P("cell"),
        P("cell"),
        P("cell"),
        P(None, "cell"),
        P("cell"),
        P("cell", None, None),
    )
    return jax.shard_map(
        shards, mesh=mesh, in_specs=placed, out_specs=P("cell", None, None), check_vma=False
    )
```
